32 devices in a mesh: shard: 4 (over y, x), dp: 8 (over z, core).
Axes of the slice: x: 2, y: 2, z: 4, core: 2. Of those that a mesh axis runs over, the one named last changes fastest.
Arguments:
- inputs: bfloat16 [8, 512, 1088], P('dp', 'shard')
- segment: int32 [8, 512], P('dp'), may hold values from 0 to 3, never falling along the last dimension, each value on 1 to 256 neighbouring positions
- cotangent: bfloat16 [8, 512, 1088], P('dp', 'shard'), may hold values from -6 to 6
- query_weight: bfloat16 [1088, 1088], P('shard')
- key_weight: bfloat16 [1088, 1088], P('shard')
- value_weight: bfloat16 [1088, 1088], P('shard'), may hold values from -0.1875 to 0.1875
- out_weight: bfloat16 [1088, 1088], P('shard'), may hold values from -3 to 3
- up_weight: bfloat16 [1088, 4352], P('shard'), may hold values from -0.1875 to 0.1875
- down_weight: bfloat16 [4352, 1088], P('shard'), may hold values from -0.09375 to 0.09375
- query_bias: bfloat16 [1088], P('shard'), may hold values from -3 to 3
- value_bias: bfloat16 [1088], P('shard'), may hold values from -3 to 3
- out_bias: bfloat16 [1088], P('shard'), may hold values from -3 to 3
- up_bias: bfloat16 [4352], P('shard'), may hold values from -3 to 3
- down_bias: bfloat16 [1088], P('shard'), may hold values from -3 to 3
- first_gain: bfloat16 [1088], P('shard'), may hold values from 0.5 to 1.5
- first_shift: bfloat16 [1088], P('shard'), may hold values from -3 to 3
- second_gain: bfloat16 [1088], P('shard'), may hold values from 0.5 to 1.5
- second_shift: bfloat16 [1088], P('shard'), may hold values from -3 to 3
Outputs:
- outputs: bfloat16 [8, 512, 1088], P('dp', 'shard')
- input_grad: float32 [8, 512, 1088], P('dp', 'shard')
- query_weight_grad: float32 [1088, 1088], P('shard')
- key_weight_grad: float32 [1088, 1088], P('shard')
- value_weight_grad: float32 [1088, 1088], P('shard')
- out_weight_grad: float32 [1088, 1088], P('shard')
- up_weight_grad: float32 [1088, 4352], P('shard')
- down_weight_grad: float32 [4352, 1088], P('shard')
- query_bias_grad: float32 [1088], P('shard')
- value_bias_grad: float32 [1088], P('shard')
- out_bias_grad: float32 [1088], P('shard')
- up_bias_grad: float32 [4352], P('shard')
- down_bias_grad: float32 [1088], P('shard')
- first_gain_grad: float32 [1088], P('shard')
- first_shift_grad: float32 [1088], P('shard')
- second_gain_grad: float32 [1088], P('shard')
- second_shift_grad: float32 [1088], P('shard')
The draws below stay inside these ranges and needn't reach their ends.
Inputs may be any that keep to these rules, and one draw needn't show every extreme that they name: `segment`: along each sequence the document numbers never fall; each of the 4 documents holds 1 to 256 tokens and one holds exactly 256.
All inputs are finite; a program needn't handle non-finite values.
Results may differ from the reference program's by a relative error of at most 0.018.
The reference program's roundings to bfloat16 on the way (of `first_in`, `attn_probs`, `attended`, `second_in`, `activated`, `grad_pre_low`, `grad_attended` and `grad_scores`) count: a program that leaves them out, or rounds other values in their place, can miss the bound.
Values may be sent and summed in bfloat16 or wider, within the bound.
No kernel may reach another device: no remote copies, remote signals or barrier semaphores. Data moves between devices by JAX's collectives and lax.ppermute only.
A program may use at most 192 MiB of HBM per device.

```python
import math
from functools import partial
import jax
import jax.numpy as jnp
import numpy as np
from jax import lax

D = 1088
HEADS = 17
HD = 64
FF = 4352
SEGS = 4
SEQS = 8
LEN = 512
MOST = 256


def draw_inputs(key, part):
    key_base, key_rows, key_cols = jax.random.split(key, 3)
    row_scale = jnp.exp(jax.random.uniform(key_rows, (SEQS, LEN, 1), minval=math.log(0.3), maxval=math.log(3.0)))
    col_scale = jnp.exp(jax.random.uniform(key_cols, (1, 1, D), minval=-0.7, maxval=0.7))
    mixed = jax.random.normal(key_base, (SEQS, LEN, D)) * col_scale
    return (mixed * row_scale).astype(jnp.bfloat16)


def projection_with_direction(key, salt):
    noise = jnp.clip(jax.random.normal(jax.random.fold_in(key, salt), (D, D)), -6.0, 6.0) / math.sqrt(D)
    return noise.astype(jnp.bfloat16)


def draw_query_weight(key, part):
    return projection_with_direction(key, 21)


def draw_key_weight(key, part):
    return projection_with_direction(key, 22)


def shard_levels(own_key, dims, pieces, least, high):
    loudness, own = 1.0, jax.random.fold_in(own_key, 6)
    for dim, shards_of in pieces:
        heights = jnp.exp(jax.random.uniform(jax.random.fold_in(own, dim), (shards_of,), jnp.float32, least / len(pieces), high / len(pieces)))
        loudness = loudness * jnp.repeat(heights, dims[dim] // shards_of).reshape([-1 if axis == dim else 1 for axis in range(len(dims))])
    return loudness


def profile(count, total, bound, skew):
    portions = [(1 << 20) // math.isqrt(standing ** skew) + 1 for standing in range(2, count + 1)]
    spare, given = total - bound - (count - 1), [1] * (count - 1)
    while spare > 0:
        candidates = [i for i in range(count - 1) if given[i] < bound]
        pool, budget = sum([portions[i] for i in candidates]), spare
        for i in candidates:
            extra = min(bound - given[i], max(1, budget * portions[i] // pool), spare)
            given[i] = given[i] + extra
            spare = spare - extra
    return np.array([bound] + given)


def ragged_sizes(own_key, amount, total, bound, lean):
    if amount == 2:
        one = jax.random.randint(own_key, (), max(1, total - bound), min(bound, total - 1) + 1)
        return jnp.stack([one, total - one])
    lengths = jnp.asarray(profile(amount, total, bound, lean), jnp.int32)
    twos = (amount - 1) // 2
    source_of, taker = lengths[1:1 + 2 * twos:2], lengths[2:2 + 2 * twos:2]
    margin = jnp.minimum(source_of - 1, bound - taker)
    shifted = jax.random.randint(jax.random.fold_in(own_key, 1), (twos,), 0, 1 << 20) % (margin + 1)
    lengths = lengths.at[1:1 + 2 * twos:2].set(source_of - shifted).at[2:2 + 2 * twos:2].set(taker + shifted)
    return lengths[jax.random.permutation(jax.random.fold_in(own_key, 2), amount)]


def normal_values(stream_key, shape, scale, most, cuts=(), kind=jnp.bfloat16):
    array = jax.random.normal(stream_key, shape, jnp.float32) * scale
    if len(cuts) > 0:
        array = shard_levels(stream_key, shape, cuts, -0.22, 0.18) * array
    return jnp.clip(array, min=-most, max=most).astype(kind)


def setup_inputs(seed: int = 0) -> dict:
    streams_of = jax.random.split(jax.random.key(seed), 19)
    inputs = draw_inputs(jax.random.fold_in(streams_of[18], 71), 0)
    segment = jax.vmap(lambda own: jnp.searchsorted(jnp.cumsum(ragged_sizes(own, SEGS, LEN, MOST, 0)), jnp.arange(LEN), side="right"))(jax.random.split(streams_of[1], SEQS)).reshape((SEQS, LEN)).astype(jnp.int32)
    cotangent = normal_values(streams_of[2], (SEQS, LEN, D), 1.0, 6.0, ((0, 8), (1, 4)))
    query_weight = draw_query_weight(jax.random.fold_in(streams_of[18], 71), 0)
    key_weight = draw_key_weight(jax.random.fold_in(streams_of[18], 71), 0)
    value_weight = normal_values(streams_of[5], (D, D), D ** -0.5, 0.1875, ((0, 4),))
    out_weight = normal_values(streams_of[6], (D, D), (max(1, D // 256)) ** -0.5, 3.0, ((0, 4),))
    up_weight = normal_values(streams_of[7], (D, FF), D ** -0.5, 0.1875, ((0, 4),))
    down_weight = normal_values(streams_of[8], (FF, D), FF ** -0.5, 0.09375, ((0, 4),))
    query_bias = normal_values(streams_of[9], (D,), 0.5, 3.0, ((0, 4),))
    value_bias = normal_values(streams_of[10], (D,), 0.5, 3.0, ((0, 4),))
    out_bias = normal_values(streams_of[11], (D,), 0.5, 3.0, ((0, 4),))
    up_bias = normal_values(streams_of[12], (FF,), 0.5, 3.0, ((0, 4),))
    down_bias = normal_values(streams_of[13], (D,), 0.5, 3.0, ((0, 4),))
    first_gain = jnp.clip(1.0 + 0.1 * jax.random.normal(streams_of[14], (D,), jnp.float32), 0.5, 1.5).astype(jnp.bfloat16)
    first_shift = normal_values(streams_of[15], (D,), 0.5, 3.0, ((0, 4),))
    second_gain = jnp.clip(1.0 + 0.1 * jax.random.normal(streams_of[16], (D,), jnp.float32), 0.5, 1.5).astype(jnp.bfloat16)
    second_shift = normal_values(streams_of[17], (D,), 0.5, 3.0, ((0, 4),))
    return dict(inputs=inputs, segment=segment, cotangent=cotangent, query_weight=query_weight, key_weight=key_weight, value_weight=value_weight, out_weight=out_weight, up_weight=up_weight, down_weight=down_weight, query_bias=query_bias, value_bias=value_bias, out_bias=out_bias, up_bias=up_bias, down_bias=down_bias, first_gain=first_gain, first_shift=first_shift, second_gain=second_gain, second_shift=second_shift)


EPSILON = 1e-05
SCORE_SCALE = 0.125
MASKED_SCORE = -1e+30

def norm_forward(values, gain_vec, shift_vec):
    average = lax.optimization_barrier(jnp.mean(values, axis=-1, keepdims=True))
    centred = values - average
    variance = lax.optimization_barrier(jnp.mean(centred * centred, axis=-1, keepdims=True))
    inv_std = lax.rsqrt(variance + EPSILON)
    normed = centred * inv_std
    return (normed, inv_std, normed * gain_vec.astype(jnp.float32) + shift_vec.astype(jnp.float32))

def norm_backward(grad_normed, normed, inv_std, gain_vec):
    scaled = grad_normed * gain_vec.astype(jnp.float32)
    first_mean = lax.optimization_barrier(jnp.mean(scaled, axis=-1, keepdims=True))
    second_mean = lax.optimization_barrier(jnp.mean(scaled * normed, axis=-1, keepdims=True))
    return inv_std * (scaled - first_mean - normed * second_mean)

def matmul(left_side, right_side):
    return jnp.dot(left_side, right_side, preferred_element_type=jnp.float32)

def contract_rows(left_side, right_side):
    return lax.dot_general(left_side, right_side, (((0,), (0,)), ((), ())), preferred_element_type=jnp.float32)

def contract_last(left_side, right_side):
    return lax.dot_general(left_side, right_side, (((1,), (1,)), ((), ())), preferred_element_type=jnp.float32)

def split_heads(matrix):
    return matrix.reshape(matrix.shape[0], HEADS, HD).transpose(1, 0, 2)

def join_heads(stacked):
    return stacked.transpose(1, 0, 2).reshape(stacked.shape[1], HEADS * HD)

def masked_scores(query_head, key_head, allowed):
    scores = contract_last(query_head, key_head) * SCORE_SCALE
    return jnp.where(allowed, scores, MASKED_SCORE)

def head_forward(query_head, key_head, value_head, allowed):
    scores = masked_scores(query_head, key_head, allowed)
    largest = lax.optimization_barrier(jnp.max(scores, axis=1, keepdims=True))
    log_total = largest + jnp.log(lax.optimization_barrier(jnp.sum(jnp.exp(scores - largest), axis=1, keepdims=True)))
    attn_probs = jnp.exp(scores - log_total).astype(jnp.bfloat16)
    return (matmul(attn_probs, value_head).astype(jnp.bfloat16), log_total[:, 0])

def head_backward(query_head, key_head, value_head, attended_head, grad_head, log_total, allowed):
    scores = masked_scores(query_head, key_head, allowed)
    exact = jnp.exp(scores - log_total[:, None])
    grad_probs = contract_last(grad_head, value_head)
    row_delta = lax.optimization_barrier(jnp.sum(grad_head.astype(jnp.float32) * attended_head.astype(jnp.float32), axis=1, keepdims=True))
    grad_scores = (exact * (grad_probs - row_delta) * SCORE_SCALE).astype(jnp.bfloat16)
    grad_query = matmul(grad_scores, key_head)
    grad_key = contract_rows(grad_scores, query_head)
    grad_value = contract_rows(exact.astype(jnp.bfloat16), grad_head)
    return (grad_query, grad_key, grad_value)

def layer_sequence(inputs, segment, cotangent, params):
    query_weight, key_weight, value_weight, out_weight, up_weight, down_weight, query_bias, value_bias, out_bias, up_bias, down_bias, first_gain, first_shift, second_gain, second_shift = params
    residual_in = inputs.astype(jnp.float32)
    first_hat, first_inv, first_in = norm_forward(residual_in, first_gain, first_shift)
    first_in = first_in.astype(jnp.bfloat16)
    queries = (matmul(first_in, query_weight) + query_bias.astype(jnp.float32)).astype(jnp.bfloat16)
    key_rows = matmul(first_in, key_weight).astype(jnp.bfloat16)
    value_rows = (matmul(first_in, value_weight) + value_bias.astype(jnp.float32)).astype(jnp.bfloat16)
    position = jnp.arange(segment.shape[0], dtype=jnp.int32)
    allowed = (position[None, :] <= position[:, None]) & (segment[None, :] == segment[:, None])
    head_queries = split_heads(queries)
    head_keys = split_heads(key_rows)
    head_values = split_heads(value_rows)
    attended_heads, log_totals = lax.map(lambda triple: head_forward(triple[0], triple[1], triple[2], allowed), (head_queries, head_keys, head_values))
    attended = join_heads(attended_heads)
    middle = residual_in + matmul(attended, out_weight) + out_bias.astype(jnp.float32)
    second_hat, second_inv, second_in = norm_forward(middle, second_gain, second_shift)
    second_in = second_in.astype(jnp.bfloat16)
    pre_act = matmul(second_in, up_weight) + up_bias.astype(jnp.float32)
    gelu_exact = partial(jax.nn.gelu, approximate=False)
    activated = gelu_exact(pre_act).astype(jnp.bfloat16)
    outputs = (middle + matmul(activated, down_weight) + down_bias.astype(jnp.float32)).astype(jnp.bfloat16)
    cot_float = cotangent.astype(jnp.float32)
    down_bias_grad = lax.optimization_barrier(jnp.sum(cot_float, axis=0))
    down_weight_grad = contract_rows(activated, cotangent)
    grad_activated = contract_last(cotangent, down_weight)
    grad_pre = jax.vjp(gelu_exact, pre_act)[1](grad_activated)[0]
    up_bias_grad = lax.optimization_barrier(jnp.sum(grad_pre, axis=0))
    grad_pre_low = grad_pre.astype(jnp.bfloat16)
    up_weight_grad = contract_rows(second_in, grad_pre_low)
    grad_second = contract_last(grad_pre_low, up_weight)
    second_gain_grad = lax.optimization_barrier(jnp.sum(grad_second * second_hat, axis=0))
    second_shift_grad = lax.optimization_barrier(jnp.sum(grad_second, axis=0))
    grad_middle = cot_float + norm_backward(grad_second, second_hat, second_inv, second_gain)
    out_bias_grad = lax.optimization_barrier(jnp.sum(grad_middle, axis=0))
    grad_middle_low = grad_middle.astype(jnp.bfloat16)
    out_weight_grad = contract_rows(attended, grad_middle_low)
    grad_attended = contract_last(grad_middle_low, out_weight).astype(jnp.bfloat16)
    grad_heads = lax.map(lambda sextet: head_backward(sextet[0], sextet[1], sextet[2], sextet[3], sextet[4], sextet[5], allowed), (head_queries, head_keys, head_values, attended_heads, split_heads(grad_attended), log_totals))
    grad_queries = join_heads(grad_heads[0])
    grad_keys = join_heads(grad_heads[1])
    grad_values = join_heads(grad_heads[2])
    query_bias_grad = lax.optimization_barrier(jnp.sum(grad_queries, axis=0))
    value_bias_grad = lax.optimization_barrier(jnp.sum(grad_values, axis=0))
    low_queries = grad_queries.astype(jnp.bfloat16)
    low_keys = grad_keys.astype(jnp.bfloat16)
    low_values = grad_values.astype(jnp.bfloat16)
    query_weight_grad = contract_rows(first_in, low_queries)
    key_weight_grad = contract_rows(first_in, low_keys)
    value_weight_grad = contract_rows(first_in, low_values)
    grad_first = contract_last(low_queries, query_weight) + contract_last(low_keys, key_weight) + contract_last(low_values, value_weight)
    first_gain_grad = lax.optimization_barrier(jnp.sum(grad_first * first_hat, axis=0))
    first_shift_grad = lax.optimization_barrier(jnp.sum(grad_first, axis=0))
    input_grad = grad_middle + norm_backward(grad_first, first_hat, first_inv, first_gain)
    gradients = (query_weight_grad, key_weight_grad, value_weight_grad, out_weight_grad, up_weight_grad, down_weight_grad, query_bias_grad, value_bias_grad, out_bias_grad, up_bias_grad, down_bias_grad, first_gain_grad, first_shift_grad, second_gain_grad, second_shift_grad)
    return (outputs, input_grad, gradients)

def reference(inputs, segment, cotangent, query_weight, key_weight, value_weight, out_weight, up_weight, down_weight, query_bias, value_bias, out_bias, up_bias, down_bias, first_gain, first_shift, second_gain, second_shift):
    params = (query_weight, key_weight, value_weight, out_weight, up_weight, down_weight, query_bias, value_bias, out_bias, up_bias, down_bias, first_gain, first_shift, second_gain, second_shift)

    def per_sequence(totals, slices):
        outputs, input_grad, gradients = layer_sequence(slices[0], slices[1], slices[2], params)
        return (jax.tree.map(jnp.add, totals, gradients), (outputs, input_grad))
    initial = tuple((jnp.zeros(parameter.shape, jnp.float32) for parameter in params))
    totals, stacked = lax.scan(per_sequence, initial, (inputs, segment, cotangent))
    return (stacked[0], stacked[1], totals[0], totals[1], totals[2], totals[3], totals[4], totals[5], totals[6], totals[7], totals[8], totals[9], totals[10], totals[11], totals[12], totals[13], totals[14])
```

```python
from functools import partial

import jax
import jax.numpy as jnp
from jax import lax
from jax.experimental import pallas as pl
from jax.experimental.pallas import tpu as pltpu
from jax.sharding import PartitionSpec as P

HEADS = 17
HD = 64
EPSILON = 1e-05
SCORE_SCALE = 0.125
MASKED_SCORE = -1e30
LANES = 128
MANY = 4


BF16 = jnp.bfloat16
F32 = jnp.float32


def normalise(values):
    average = jnp.mean(values, axis=-1, keepdims=True)
    centred = values - average
    variance = jnp.mean(centred * centred, axis=-1, keepdims=True)
    inv_std = lax.rsqrt(variance + EPSILON)
    return centred * inv_std, inv_std


def norm_backward(grad_normed, normed, inv_std, gain_vec):
    scaled = grad_normed * gain_vec
    first_mean = jnp.mean(scaled, axis=-1, keepdims=True)
    second_mean = jnp.mean(scaled * normed, axis=-1, keepdims=True)
    return inv_std * (scaled - first_mean - normed * second_mean)


def matmul(left_side, right_side):
    return jnp.dot(left_side, right_side, preferred_element_type=F32)


def contract_rows(left_side, right_side):
    return lax.dot_general(
        left_side, right_side, (((0,), (0,)), ((), ())), preferred_element_type=F32
    )


def contract_last(left_side, right_side):
    return lax.dot_general(
        left_side, right_side, (((1,), (1,)), ((), ())), preferred_element_type=F32
    )


def mask_bias(row_seg, row_pos, col_seg, col_pos):
    allowed = (row_seg == col_seg) & (col_pos <= row_pos)
    return jnp.where(allowed, 0.0, MASKED_SCORE)


def attention_forward(qkv, rows_info, cols_info, heads):
    tokens = qkv.shape[0]
    width = heads * HD
    block = min(256, tokens)

    def kernel(q_ref, kv_ref, rows_ref, cols_ref, out_ref, log_ref):
        bias = mask_bias(
            rows_ref[:, 0:1], rows_ref[:, 1:2], cols_ref[0:1, :], cols_ref[1:2, :]
        )
        lane = lax.broadcasted_iota(jnp.int32, (block, LANES), 1)
        logs = jnp.zeros((block, LANES), F32)
        for h in range(heads):
            query = q_ref[:, h * HD : (h + 1) * HD]
            keys = kv_ref[:, width + h * HD : width + (h + 1) * HD]
            vals = kv_ref[:, 2 * width + h * HD : 2 * width + (h + 1) * HD]
            scores = contract_last(query, keys) * SCORE_SCALE + bias
            largest = jnp.max(scores, axis=1, keepdims=True)
            grown = jnp.exp(scores - largest)
            total = jnp.sum(grown, axis=1, keepdims=True)
            probs = (grown * (1.0 / total)).astype(BF16)
            out_ref[:, h * HD : (h + 1) * HD] = matmul(probs, vals).astype(BF16)
            logs = jnp.where(lane == h, largest + jnp.log(total), logs)
        log_ref[...] = logs

    return pl.pallas_call(
        kernel,
        grid=(tokens // block,),
        in_specs=[
            pl.BlockSpec((block, 3 * width), lambda b: (b, 0)),
            pl.BlockSpec((tokens, 3 * width), lambda b: (0, 0)),
            pl.BlockSpec((block, 2), lambda b: (b, 0)),
            pl.BlockSpec((2, tokens), lambda b: (0, 0)),
        ],
        out_specs=[
            pl.BlockSpec((block, width), lambda b: (b, 0)),
            pl.BlockSpec((block, LANES), lambda b: (b, 0)),
        ],
        out_shape=[
            jax.ShapeDtypeStruct((tokens, width), BF16),
            jax.ShapeDtypeStruct((tokens, LANES), F32),
        ],
        name="attention_forward",
    )(qkv, qkv, rows_info, cols_info)


def attention_backward(qkv, grad_att, attended, logs, rows_info, cols_info, heads):
    tokens = qkv.shape[0]
    width = heads * HD
    block = min(256, tokens)
    steps = tokens // block

    def kernel(
        q_ref, kv_ref, grad_ref, att_ref, log_ref, rows_ref, cols_ref,
        gq_ref, gkv_ref, sums_ref, acc_ref, bias_ref,
    ):
        step = pl.program_id(0)

        @pl.when(step == 0)
        def _():
            acc_ref[...] = jnp.zeros_like(acc_ref)
            bias_ref[...] = jnp.zeros_like(bias_ref)

        bias = mask_bias(
            rows_ref[:, 0:1], rows_ref[:, 1:2], cols_ref[0:1, :], cols_ref[1:2, :]
        )
        for h in range(heads):
            own = slice(h * HD, (h + 1) * HD)
            query = q_ref[:, own]
            keys = kv_ref[:, width + h * HD : width + (h + 1) * HD]
            vals = kv_ref[:, 2 * width + h * HD : 2 * width + (h + 1) * HD]
            grad = grad_ref[:, own]
            delta = jnp.sum(
                grad.astype(F32) * att_ref[:, own].astype(F32), axis=1, keepdims=True
            )
            scores = contract_last(query, keys) * SCORE_SCALE + bias
            exact = jnp.exp(scores - log_ref[:, h : h + 1])
            grad_probs = contract_last(grad, vals)
            grad_scores = (exact * (grad_probs - delta) * SCORE_SCALE).astype(BF16)
            grad_query = matmul(grad_scores, keys)
            gq_ref[:, own] = grad_query.astype(BF16)
            bias_ref[0:1, own] += jnp.sum(grad_query, axis=0, keepdims=True)
            acc_ref[:, own] += contract_rows(grad_scores, query)
            acc_ref[:, width + h * HD : width + (h + 1) * HD] += contract_rows(
                exact.astype(BF16), grad
            )

        @pl.when(step == steps - 1)
        def _():
            gkv_ref[...] = acc_ref[...].astype(BF16)
            bias_ref[1:2, :] = jnp.sum(acc_ref[:, width:], axis=0, keepdims=True)
            sums_ref[...] = bias_ref[...]

    return pl.pallas_call(
        kernel,
        grid=(steps,),
        in_specs=[
            pl.BlockSpec((block, 3 * width), lambda b: (b, 0)),
            pl.BlockSpec((tokens, 3 * width), lambda b: (0, 0)),
            pl.BlockSpec((block, width), lambda b: (b, 0)),
            pl.BlockSpec((block, width), lambda b: (b, 0)),
            pl.BlockSpec((block, LANES), lambda b: (b, 0)),
            pl.BlockSpec((block, 2), lambda b: (b, 0)),
            pl.BlockSpec((2, tokens), lambda b: (0, 0)),
        ],
        out_specs=[
            pl.BlockSpec((block, width), lambda b: (b, 0)),
            pl.BlockSpec((tokens, 2 * width), lambda b: (0, 0)),
            pl.BlockSpec((8, width), lambda b: (0, 0)),
        ],
        out_shape=[
            jax.ShapeDtypeStruct((tokens, width), BF16),
            jax.ShapeDtypeStruct((tokens, 2 * width), BF16),
            jax.ShapeDtypeStruct((8, width), F32),
        ],
        scratch_shapes=[
            pltpu.VMEM((tokens, 2 * width), F32),
            pltpu.VMEM((8, width), F32),
        ],
        name="attention_backward",
    )(qkv, qkv, grad_att, attended, logs, rows_info, cols_info)


def on_device(
    count,
    inputs,
    segment,
    cotangent,
    query_weight,
    key_weight,
    value_weight,
    out_weight,
    up_weight,
    down_weight,
    query_bias,
    value_bias,
    out_bias,
    up_bias,
    down_bias,
    first_gain,
    first_shift,
    second_gain,
    second_shift,
):
    me = lax.axis_index("shard")
    others = range(1, count)
    order = me ^ jnp.arange(count, dtype=jnp.int32)
    length = inputs.shape[1]
    model = inputs.shape[2]
    own = query_weight.shape[0]
    hidden = down_weight.shape[0]
    per = -(-HEADS // count)
    width = per * HD
    padded = count * width

    def send(value, k):
        return lax.ppermute(value, "shard", [(j, j ^ k) for j in range(count)])

    def gather(value):
        if count > MANY:
            whole = lax.all_gather(value, "shard")
            return [lax.dynamic_index_in_dim(whole, me ^ k, 0, False) for k in range(count)]
        return [value] + [send(value, k) for k in others]

    def swap(pieces):
        if count > MANY:
            whole = jnp.stack(pieces)[order]
            whole = lax.all_to_all(whole, "shard", split_axis=0, concat_axis=0)[order]
            return [whole[k] for k in range(count)]
        return [pieces[0]] + [send(pieces[k], k) for k in others]

    def scatter_sum(partial_rows):
        blocks = [partial_rows[k * length : (k + 1) * length] for k in range(count)]
        got = swap([b.astype(BF16) for b in blocks])
        return sum((v.astype(F32) for v in got[1:]), blocks[0])

    def in_order(pieces):
        rows = pieces[0].shape[0]
        whole = jnp.zeros((count * rows,) + pieces[0].shape[1:], pieces[0].dtype)
        for k in range(count):
            start = ((me ^ k) * rows,) + (0,) * (pieces[0].ndim - 1)
            whole = lax.dynamic_update_slice(whole, pieces[k], start)
        return whole

    def exchange(stacked):
        return swap(
            [lax.dynamic_index_in_dim(stacked, me ^ k, 0, False) for k in range(count)]
        )

    vectors = jnp.stack(
        [
            query_bias, value_bias, out_bias, down_bias,
            first_gain, first_shift, second_gain, second_shift,
        ]
    )
    vectors = in_order([v[None] for v in gather(vectors)])
    vectors = vectors.transpose(1, 0, 2).reshape(8, model).astype(F32)
    all_inputs = jnp.concatenate(gather(inputs[0]), axis=0)
    pad_cols = lambda w: jnp.pad(w, ((0, 0), (0, padded - model)))
    stacked_qkv = jnp.concatenate(
        [
            pad_cols(w).reshape(own, count, width)
            for w in (query_weight, key_weight, value_weight)
        ],
        axis=2,
    ).transpose(1, 0, 2)
    qkv_cols = in_order(exchange(stacked_qkv))
    all_cot = jnp.concatenate(gather(cotangent[0]), axis=0)
    full_out = jnp.pad(in_order(gather(out_weight)), ((0, padded - model), (0, 0)))
    head_out = lax.dynamic_slice_in_dim(full_out, me * width, width, axis=0)
    mixed_out = full_out.reshape(count, width, model)[order].reshape(padded, model)
    up_cols = in_order(exchange(up_weight.reshape(own, count, hidden).transpose(1, 0, 2)))

    pos = (order[:, None] * length + jnp.arange(length, dtype=jnp.int32)[None, :]).reshape(-1)
    seg = segment[0].reshape(count, length)[order].reshape(-1)
    rows_info = jnp.stack([seg, pos], axis=1)
    cols_info = jnp.stack([seg, pos], axis=0)

    head_slice = lambda v: lax.dynamic_slice_in_dim(
        jnp.pad(v, (0, padded - model)), me * width, width
    )
    qkv_bias = jnp.concatenate(
        [head_slice(vectors[0]), jnp.zeros((width,), F32), head_slice(vectors[1])]
    )

    first_gain_full, first_shift_full = vectors[4], vectors[5]
    second_gain_full, second_shift_full = vectors[6], vectors[7]
    all_hat, _ = normalise(all_inputs.astype(F32))
    first_in = (all_hat * first_gain_full + first_shift_full).astype(BF16)
    qkv = (matmul(first_in, qkv_cols) + qkv_bias).astype(BF16)
    attended, logs = attention_forward(qkv, rows_info, cols_info, per)
    att_pieces = swap([attended[k * length : (k + 1) * length] for k in range(count)])
    residual_in = inputs[0].astype(F32)
    own_attended = jnp.concatenate(att_pieces, axis=1)
    middle = residual_in + matmul(own_attended, mixed_out) + vectors[2]
    second_hat, second_inv = normalise(middle)
    own_second_in = (second_hat * second_gain_full + second_shift_full).astype(BF16)
    second_in = jnp.concatenate(gather(own_second_in), axis=0)
    pre_act = matmul(second_in, up_cols) + up_bias.astype(F32)
    below = 0.5 * (1.0 + lax.erf(pre_act * (0.5**0.5)))
    activated = (pre_act * below).astype(BF16)
    slope = below + pre_act * (jnp.exp(-0.5 * pre_act * pre_act) * 0.3989422804014327)
    grad_pre = contract_last(all_cot, down_weight) * slope
    grad_pre_low = grad_pre.astype(BF16)
    up_bias_part = jnp.sum(grad_pre, axis=0)
    grad_second = scatter_sum(contract_last(grad_pre_low, up_cols))
    outputs = (
        middle + scatter_sum(matmul(activated, down_weight)) + vectors[3]
    ).astype(BF16)

    down_part = contract_rows(activated, all_cot).astype(BF16)
    up_part = contract_rows(second_in, grad_pre_low).astype(BF16)
    up_rows = exchange(up_part.reshape(count, own, hidden))

    def reduce_dp(part, dim):
        share = lax.psum_scatter(part, "dp", scatter_dimension=dim, tiled=True)
        return lax.all_gather(share, "dp", axis=dim, tiled=True).astype(F32)

    down_weight_grad = reduce_dp(down_part, 0)
    up_rows = in_order([v[None] for v in up_rows])
    up_total = reduce_dp(up_rows.reshape(count * own, hidden), 0)
    up_weight_grad = (
        up_total.reshape(count, own, hidden).transpose(1, 0, 2).reshape(own, count * hidden)
    )

    grad_middle = cotangent[0].astype(F32) + norm_backward(
        grad_second, second_hat, second_inv, second_gain_full
    )
    grad_middle_low = grad_middle.astype(BF16)
    all_grad_middle = jnp.concatenate(gather(grad_middle_low), axis=0)
    grad_attended = contract_last(all_grad_middle, head_out).astype(BF16)
    grad_queries, grad_kv, head_sums = attention_backward(
        qkv, grad_attended, attended, logs, rows_info, cols_info, per
    )
    grad_qkv = jnp.concatenate([grad_queries, grad_kv], axis=1)
    grad_first = scatter_sum(contract_last(grad_qkv, qkv_cols))
    first_hat, first_inv = normalise(residual_in)
    input_grad = grad_middle + norm_backward(grad_first, first_hat, first_inv, first_gain_full)

    true_attended = in_order([v[None] for v in att_pieces])
    true_attended = true_attended.transpose(1, 0, 2).reshape(length, padded)[:, :model]
    own_features = jnp.concatenate(
        exchange(true_attended.reshape(length, count, own).transpose(1, 0, 2)), axis=0
    )
    out_part = contract_rows(own_features, all_grad_middle).astype(BF16)
    qkv_part = contract_rows(first_in, grad_qkv).astype(BF16)
    qkv_rows = exchange(qkv_part.reshape(count, own, 3 * width))
    qkv_rows = in_order([v[None] for v in qkv_rows]).reshape(count, own, 3, width)
    qkv_rows = qkv_rows.transpose(2, 1, 0, 3).reshape(3, own, padded)[:, :, :model]
    square = reduce_dp(jnp.concatenate([out_part[None], qkv_rows]).reshape(4 * own, model), 0)
    square = square.reshape(4, own, model)

    to_full = lambda v: lax.dynamic_update_slice(
        jnp.zeros((padded,), F32), v, (me * width,)
    )[:model]
    partials = jnp.stack(
        [
            to_full(head_sums[0]),
            to_full(head_sums[1]),
            jnp.sum(grad_middle, axis=0),
            jnp.sum(cotangent[0].astype(F32), axis=0),
            jnp.sum(grad_first * first_hat, axis=0),
            jnp.sum(grad_first, axis=0),
            jnp.sum(grad_second * second_hat, axis=0),
            jnp.sum(grad_second, axis=0),
        ]
    )
    vector_rows = sum(exchange(partials.reshape(8, count, own).transpose(1, 0, 2)))
    summed, up_bias_grad = lax.psum((vector_rows, up_bias_part), "dp")
    return (
        outputs[None],
        input_grad[None],
        square[1],
        square[2],
        square[3],
        square[0],
        up_weight_grad,
        down_weight_grad,
        summed[0],
        summed[1],
        summed[2],
        up_bias_grad,
        summed[3],
        summed[4],
        summed[5],
        summed[6],
        summed[7],
    )


def solution(mesh):
    tokens = P("dp", "shard", None)
    matrix = P("shard", None)
    vector = P("shard")
    return jax.shard_map(
        partial(on_device, mesh.shape["shard"]),
        mesh=mesh,
        in_specs=(tokens, P("dp", None), tokens) + (matrix,) * 6 + (vector,) * 9,
        out_specs=(tokens, tokens) + (matrix,) * 6 + (vector,) * 9,
        check_vma=False,
    )
```

```python
from functools import partial

import jax
import jax.numpy as jnp
from jax import lax
from jax.experimental import pallas as pl
from jax.experimental.pallas import tpu as pltpu
from jax.sharding import PartitionSpec as P

HEADS = 17
HD = 64
EPSILON = 1e-05
SCORE_SCALE = 0.125
MASKED_SCORE = -1e30
LANES = 128
MANY = 4


BF16 = jnp.bfloat16
F32 = jnp.float32


def normalise(values):
    average = jnp.mean(values, axis=-1, keepdims=True)
    centred = values - average
    variance = jnp.mean(centred * centred, axis=-1, keepdims=True)
    inv_std = lax.rsqrt(variance + EPSILON)
    return centred * inv_std, inv_std


def norm_backward(grad_normed, normed, inv_std, gain_vec):
    scaled = grad_normed * gain_vec
    first_mean = jnp.mean(scaled, axis=-1, keepdims=True)
    second_mean = jnp.mean(scaled * normed, axis=-1, keepdims=True)
    return inv_std * (scaled - first_mean - normed * second_mean)


def matmul(left_side, right_side):
    return jnp.dot(left_side, right_side, preferred_element_type=F32)


def contract_rows(left_side, right_side):
    return lax.dot_general(
        left_side, right_side, (((0,), (0,)), ((), ())), preferred_element_type=F32
    )


def contract_last(left_side, right_side):
    return lax.dot_general(
        left_side, right_side, (((1,), (1,)), ((), ())), preferred_element_type=F32
    )


def mask_bias(row_seg, row_pos, col_seg, col_pos):
    allowed = (row_seg == col_seg) & (col_pos <= row_pos)
    return jnp.where(allowed, 0.0, MASKED_SCORE)


def attention_forward(qkv, rows_info, cols_info, heads):
    tokens = qkv.shape[0]
    width = heads * HD
    block = min(256, tokens)

    def kernel(q_ref, kv_ref, rows_ref, cols_ref, out_ref, log_ref):
        bias = mask_bias(
            rows_ref[:, 0:1], rows_ref[:, 1:2], cols_ref[0:1, :], cols_ref[1:2, :]
        )
        lane = lax.broadcasted_iota(jnp.int32, (block, LANES), 1)
        logs = jnp.zeros((block, LANES), F32)
        for h in range(heads):
            query = q_ref[:, h * HD : (h + 1) * HD]
            keys = kv_ref[:, width + h * HD : width + (h + 1) * HD]
            vals = kv_ref[:, 2 * width + h * HD : 2 * width + (h + 1) * HD]
            scores = contract_last(query, keys) * SCORE_SCALE + bias
            largest = jnp.max(scores, axis=1, keepdims=True)
            grown = jnp.exp(scores - largest)
            total = jnp.sum(grown, axis=1, keepdims=True)
            probs = (grown * (1.0 / total)).astype(BF16)
            out_ref[:, h * HD : (h + 1) * HD] = matmul(probs, vals).astype(BF16)
            logs = jnp.where(lane == h, largest + jnp.log(total), logs)
        log_ref[...] = logs

    return pl.pallas_call(
        kernel,
        grid=(tokens // block,),
        in_specs=[
            pl.BlockSpec((block, 3 * width), lambda b: (b, 0)),
            pl.BlockSpec((tokens, 3 * width), lambda b: (0, 0)),
            pl.BlockSpec((block, 2), lambda b: (b, 0)),
            pl.BlockSpec((2, tokens), lambda b: (0, 0)),
        ],
        out_specs=[
            pl.BlockSpec((block, width), lambda b: (b, 0)),
            pl.BlockSpec((block, LANES), lambda b: (b, 0)),
        ],
        out_shape=[
            jax.ShapeDtypeStruct((tokens, width), BF16),
            jax.ShapeDtypeStruct((tokens, LANES), F32),
        ],
        name="attention_forward",
    )(qkv, qkv, rows_info, cols_info)


def attention_backward(qkv, grad_att, attended, logs, rows_info, cols_info, heads):
    tokens = qkv.shape[0]
    width = heads * HD
    block = min(256, tokens)
    steps = tokens // block

    def kernel(
        q_ref, kv_ref, grad_ref, att_ref, log_ref, rows_ref, cols_ref,
        gq_ref, gkv_ref, sums_ref, acc_ref, bias_ref,
    ):
        step = pl.program_id(0)

        @pl.when(step == 0)
        def _():
            acc_ref[...] = jnp.zeros_like(acc_ref)
            bias_ref[...] = jnp.zeros_like(bias_ref)

        bias = mask_bias(
            rows_ref[:, 0:1], rows_ref[:, 1:2], cols_ref[0:1, :], cols_ref[1:2, :]
        )
        for h in range(heads):
            own = slice(h * HD, (h + 1) * HD)
            query = q_ref[:, own]
            keys = kv_ref[:, width + h * HD : width + (h + 1) * HD]
            vals = kv_ref[:, 2 * width + h * HD : 2 * width + (h + 1) * HD]
            grad = grad_ref[:, own]
            delta = jnp.sum(
                grad.astype(F32) * att_ref[:, own].astype(F32), axis=1, keepdims=True
            )
            scores = contract_last(query, keys) * SCORE_SCALE + bias
            exact = jnp.exp(scores - log_ref[:, h : h + 1])
            grad_probs = contract_last(grad, vals)
            grad_scores = (exact * (grad_probs - delta) * SCORE_SCALE).astype(BF16)
            grad_query = matmul(grad_scores, keys)
            gq_ref[:, own] = grad_query.astype(BF16)
            bias_ref[0:1, own] += jnp.sum(grad_query, axis=0, keepdims=True)
            acc_ref[:, own] += contract_rows(grad_scores, query)
            acc_ref[:, width + h * HD : width + (h + 1) * HD] += contract_rows(
                exact.astype(BF16), grad
            )

        @pl.when(step == steps - 1)
        def _():
            gkv_ref[...] = acc_ref[...].astype(BF16)
            bias_ref[1:2, :] = jnp.sum(acc_ref[:, width:], axis=0, keepdims=True)
            sums_ref[...] = bias_ref[...]

    return pl.pallas_call(
        kernel,
        grid=(steps,),
        in_specs=[
            pl.BlockSpec((block, 3 * width), lambda b: (b, 0)),
            pl.BlockSpec((tokens, 3 * width), lambda b: (0, 0)),
            pl.BlockSpec((block, width), lambda b: (b, 0)),
            pl.BlockSpec((block, width), lambda b: (b, 0)),
            pl.BlockSpec((block, LANES), lambda b: (b, 0)),
            pl.BlockSpec((block, 2), lambda b: (b, 0)),
            pl.BlockSpec((2, tokens), lambda b: (0, 0)),
        ],
        out_specs=[
            pl.BlockSpec((block, width), lambda b: (b, 0)),
            pl.BlockSpec((tokens, 2 * width), lambda b: (0, 0)),
            pl.BlockSpec((8, width), lambda b: (0, 0)),
        ],
        out_shape=[
            jax.ShapeDtypeStruct((tokens, width), BF16),
            jax.ShapeDtypeStruct((tokens, 2 * width), BF16),
            jax.ShapeDtypeStruct((8, width), F32),
        ],
        scratch_shapes=[
            pltpu.VMEM((tokens, 2 * width), F32),
            pltpu.VMEM((8, width), F32),
        ],
        name="attention_backward",
    )(qkv, qkv, grad_att, attended, logs, rows_info, cols_info)


def on_device_general(
    count,
    inputs,
    segment,
    cotangent,
    query_weight,
    key_weight,
    value_weight,
    out_weight,
    up_weight,
    down_weight,
    query_bias,
    value_bias,
    out_bias,
    up_bias,
    down_bias,
    first_gain,
    first_shift,
    second_gain,
    second_shift,
):
    me = lax.axis_index("shard")
    others = range(1, count)
    order = me ^ jnp.arange(count, dtype=jnp.int32)
    length = inputs.shape[1]
    model = inputs.shape[2]
    own = query_weight.shape[0]
    hidden = down_weight.shape[0]
    per = -(-HEADS // count)
    width = per * HD
    padded = count * width

    def send(value, k):
        return lax.ppermute(value, "shard", [(j, j ^ k) for j in range(count)])

    def gather(value):
        if count > MANY:
            whole = lax.all_gather(value, "shard")
            return [lax.dynamic_index_in_dim(whole, me ^ k, 0, False) for k in range(count)]
        return [value] + [send(value, k) for k in others]

    def swap(pieces):
        if count > MANY:
            whole = jnp.stack(pieces)[order]
            whole = lax.all_to_all(whole, "shard", split_axis=0, concat_axis=0)[order]
            return [whole[k] for k in range(count)]
        return [pieces[0]] + [send(pieces[k], k) for k in others]

    def scatter_sum(partial_rows):
        blocks = [partial_rows[k * length : (k + 1) * length] for k in range(count)]
        got = swap([b.astype(BF16) for b in blocks])
        return sum((v.astype(F32) for v in got[1:]), blocks[0])

    def in_order(pieces):
        rows = pieces[0].shape[0]
        whole = jnp.zeros((count * rows,) + pieces[0].shape[1:], pieces[0].dtype)
        for k in range(count):
            start = ((me ^ k) * rows,) + (0,) * (pieces[0].ndim - 1)
            whole = lax.dynamic_update_slice(whole, pieces[k], start)
        return whole

    def exchange(stacked):
        return swap(
            [lax.dynamic_index_in_dim(stacked, me ^ k, 0, False) for k in range(count)]
        )

    vectors = jnp.stack(
        [
            query_bias, value_bias, out_bias, down_bias,
            first_gain, first_shift, second_gain, second_shift,
        ]
    )
    vectors = in_order([v[None] for v in gather(vectors)])
    vectors = vectors.transpose(1, 0, 2).reshape(8, model).astype(F32)
    all_inputs = jnp.concatenate(gather(inputs[0]), axis=0)
    pad_cols = lambda w: jnp.pad(w, ((0, 0), (0, padded - model)))
    stacked_qkv = jnp.concatenate(
        [
            pad_cols(w).reshape(own, count, width)
            for w in (query_weight, key_weight, value_weight)
        ],
        axis=2,
    ).transpose(1, 0, 2)
    qkv_cols = in_order(exchange(stacked_qkv))
    all_cot = jnp.concatenate(gather(cotangent[0]), axis=0)
    full_out = jnp.pad(in_order(gather(out_weight)), ((0, padded - model), (0, 0)))
    head_out = lax.dynamic_slice_in_dim(full_out, me * width, width, axis=0)
    mixed_out = full_out.reshape(count, width, model)[order].reshape(padded, model)
    up_cols = in_order(exchange(up_weight.reshape(own, count, hidden).transpose(1, 0, 2)))

    pos = (order[:, None] * length + jnp.arange(length, dtype=jnp.int32)[None, :]).reshape(-1)
    seg = segment[0].reshape(count, length)[order].reshape(-1)
    rows_info = jnp.stack([seg, pos], axis=1)
    cols_info = jnp.stack([seg, pos], axis=0)

    head_slice = lambda v: lax.dynamic_slice_in_dim(
        jnp.pad(v, (0, padded - model)), me * width, width
    )
    qkv_bias = jnp.concatenate(
        [head_slice(vectors[0]), jnp.zeros((width,), F32), head_slice(vectors[1])]
    )

    first_gain_full, first_shift_full = vectors[4], vectors[5]
    second_gain_full, second_shift_full = vectors[6], vectors[7]
    all_hat, _ = normalise(all_inputs.astype(F32))
    first_in = (all_hat * first_gain_full + first_shift_full).astype(BF16)
    qkv = (matmul(first_in, qkv_cols) + qkv_bias).astype(BF16)
    attended, logs = attention_forward(qkv, rows_info, cols_info, per)
    att_pieces = swap([attended[k * length : (k + 1) * length] for k in range(count)])
    residual_in = inputs[0].astype(F32)
    own_attended = jnp.concatenate(att_pieces, axis=1)
    middle = residual_in + matmul(own_attended, mixed_out) + vectors[2]
    second_hat, second_inv = normalise(middle)
    own_second_in = (second_hat * second_gain_full + second_shift_full).astype(BF16)
    second_in = jnp.concatenate(gather(own_second_in), axis=0)
    pre_act = matmul(second_in, up_cols) + up_bias.astype(F32)
    below = 0.5 * (1.0 + lax.erf(pre_act * (0.5**0.5)))
    activated = (pre_act * below).astype(BF16)
    slope = below + pre_act * (jnp.exp(-0.5 * pre_act * pre_act) * 0.3989422804014327)
    grad_pre = contract_last(all_cot, down_weight) * slope
    grad_pre_low = grad_pre.astype(BF16)
    up_bias_part = jnp.sum(grad_pre, axis=0)
    grad_second = scatter_sum(contract_last(grad_pre_low, up_cols))
    outputs = (
        middle + scatter_sum(matmul(activated, down_weight)) + vectors[3]
    ).astype(BF16)

    down_part = contract_rows(activated, all_cot).astype(BF16)
    up_part = contract_rows(second_in, grad_pre_low).astype(BF16)
    up_rows = exchange(up_part.reshape(count, own, hidden))

    def reduce_dp(part, dim):
        share = lax.psum_scatter(part, "dp", scatter_dimension=dim, tiled=True)
        return lax.all_gather(share, "dp", axis=dim, tiled=True).astype(F32)

    down_weight_grad = reduce_dp(down_part, 0)
    up_rows = in_order([v[None] for v in up_rows])
    up_total = reduce_dp(up_rows.reshape(count * own, hidden), 0)
    up_weight_grad = (
        up_total.reshape(count, own, hidden).transpose(1, 0, 2).reshape(own, count * hidden)
    )

    grad_middle = cotangent[0].astype(F32) + norm_backward(
        grad_second, second_hat, second_inv, second_gain_full
    )
    grad_middle_low = grad_middle.astype(BF16)
    all_grad_middle = jnp.concatenate(gather(grad_middle_low), axis=0)
    grad_attended = contract_last(all_grad_middle, head_out).astype(BF16)
    grad_queries, grad_kv, head_sums = attention_backward(
        qkv, grad_attended, attended, logs, rows_info, cols_info, per
    )
    grad_qkv = jnp.concatenate([grad_queries, grad_kv], axis=1)
    grad_first = scatter_sum(contract_last(grad_qkv, qkv_cols))
    first_hat, first_inv = normalise(residual_in)
    input_grad = grad_middle + norm_backward(grad_first, first_hat, first_inv, first_gain_full)

    true_attended = in_order([v[None] for v in att_pieces])
    true_attended = true_attended.transpose(1, 0, 2).reshape(length, padded)[:, :model]
    own_features = jnp.concatenate(
        exchange(true_attended.reshape(length, count, own).transpose(1, 0, 2)), axis=0
    )
    out_part = contract_rows(own_features, all_grad_middle).astype(BF16)
    qkv_part = contract_rows(first_in, grad_qkv).astype(BF16)
    qkv_rows = exchange(qkv_part.reshape(count, own, 3 * width))
    qkv_rows = in_order([v[None] for v in qkv_rows]).reshape(count, own, 3, width)
    qkv_rows = qkv_rows.transpose(2, 1, 0, 3).reshape(3, own, padded)[:, :, :model]
    square = reduce_dp(jnp.concatenate([out_part[None], qkv_rows]).reshape(4 * own, model), 0)
    square = square.reshape(4, own, model)

    to_full = lambda v: lax.dynamic_update_slice(
        jnp.zeros((padded,), F32), v, (me * width,)
    )[:model]
    partials = jnp.stack(
        [
            to_full(head_sums[0]),
            to_full(head_sums[1]),
            jnp.sum(grad_middle, axis=0),
            jnp.sum(cotangent[0].astype(F32), axis=0),
            jnp.sum(grad_first * first_hat, axis=0),
            jnp.sum(grad_first, axis=0),
            jnp.sum(grad_second * second_hat, axis=0),
            jnp.sum(grad_second, axis=0),
        ]
    )
    vector_rows = sum(exchange(partials.reshape(8, count, own).transpose(1, 0, 2)))
    summed, up_bias_grad = lax.psum((vector_rows, up_bias_part), "dp")
    return (
        outputs[None],
        input_grad[None],
        square[1],
        square[2],
        square[3],
        square[0],
        up_weight_grad,
        down_weight_grad,
        summed[0],
        summed[1],
        summed[2],
        up_bias_grad,
        summed[3],
        summed[4],
        summed[5],
        summed[6],
        summed[7],
    )


def call(kernel, out_shape, out_specs, name, in_specs, scratch=(), grid=()):
    return pl.pallas_call(
        kernel,
        grid=grid,
        in_specs=in_specs,
        out_specs=out_specs,
        out_shape=out_shape,
        scratch_shapes=scratch,
        name=name,
    )


def assemble(pieces, slots, total):
    amount = len(pieces)

    def kernel(slot_ref, *refs):
        out_ref, sems = refs[amount], refs[amount + 1]
        copies = [
            pltpu.make_async_copy(refs[k], out_ref.at[slot_ref[k]], sems.at[k])
            for k in range(amount)
        ]
        for copy in copies:
            copy.start()
        for copy in copies:
            copy.wait()

    return call(
        kernel,
        jax.ShapeDtypeStruct((total,) + pieces[0].shape, pieces[0].dtype),
        pl.BlockSpec(memory_space=pl.ANY),
        "assemble",
        [pl.BlockSpec(memory_space=pltpu.SMEM)]
        + [pl.BlockSpec(memory_space=pl.ANY)] * amount,
        [pltpu.SemaphoreType.DMA((amount,))],
    )(jnp.stack(slots).astype(jnp.int32), *pieces)


def place_heads(pieces, last, slots, wide):
    amount = len(pieces)
    rows = pieces[0].shape[0]
    model = amount * wide + HD

    def kernel(slot_ref, *refs):
        out_ref = refs[amount + 1]
        for k in range(amount):
            start = pl.multiple_of(slot_ref[k] * wide, LANES)
            out_ref[:, pl.ds(start, wide)] = refs[k][...]
        out_ref[:, amount * wide :] = refs[amount][...]

    return call(
        kernel,
        jax.ShapeDtypeStruct((rows, model), BF16),
        pl.BlockSpec(memory_space=pltpu.VMEM),
        "place_heads",
        [pl.BlockSpec(memory_space=pltpu.SMEM)]
        + [pl.BlockSpec(memory_space=pltpu.VMEM)] * (amount + 1),
    )(jnp.stack(slots).astype(jnp.int32), *pieces, last)


def place_grads(out_part, pieces, slots, wide):
    amount = len(pieces)
    rows, model = out_part.shape

    def kernel(slot_ref, *refs):
        out_ref = refs[amount + 1]
        out_ref[0] = refs[0][...]
        for m in range(3):
            extra = slice(3 * wide + m * HD, 3 * wide + (m + 1) * HD)
            shared = refs[1][:, extra].astype(F32)
            for k in range(amount):
                start = pl.multiple_of(slot_ref[k] * wide, LANES)
                out_ref[1 + m, :, pl.ds(start, wide)] = refs[1 + k][:, m * wide : (m + 1) * wide]
                if k > 0:
                    shared = shared + refs[1 + k][:, extra].astype(F32)
            out_ref[1 + m, :, amount * wide :] = shared.astype(BF16)

    return call(
        kernel,
        jax.ShapeDtypeStruct((4, rows, model), BF16),
        pl.BlockSpec(memory_space=pltpu.VMEM),
        "place_grads",
        [pl.BlockSpec(memory_space=pltpu.SMEM)]
        + [pl.BlockSpec(memory_space=pltpu.VMEM)] * (amount + 1),
    )(jnp.stack(slots).astype(jnp.int32), out_part, *pieces)


def split_forward(qkv, rows_info, cols_info, heads, length):
    tokens = qkv.shape[0]
    wide = heads * HD
    block = min(256, tokens)
    full = qkv.shape[1]

    def kernel(q_ref, kv_ref, rows_ref, cols_ref, out_ref, last_ref, log_ref):
        bias = mask_bias(
            rows_ref[:, 0:1], rows_ref[:, 1:2], cols_ref[0:1, :], cols_ref[1:2, :]
        )
        lane = lax.broadcasted_iota(jnp.int32, (block, LANES), 1)

        def head(query, keys, vals, seen):
            scores = contract_last(query, keys) * SCORE_SCALE + seen
            largest = jnp.max(scores, axis=1, keepdims=True)
            grown = jnp.exp(scores - largest)
            total = jnp.sum(grown, axis=1, keepdims=True)
            probs = (grown * (1.0 / total)).astype(BF16)
            return matmul(probs, vals).astype(BF16), largest + jnp.log(total)

        logs = jnp.zeros((block, LANES), F32)
        for h in range(heads):
            own = slice(h * HD, (h + 1) * HD)
            got, log = head(
                q_ref[:, own],
                kv_ref[:, wide + h * HD : wide + (h + 1) * HD],
                kv_ref[:, 2 * wide + h * HD : 2 * wide + (h + 1) * HD],
                bias,
            )
            out_ref[:, own] = got
            logs = jnp.where(lane == h, log, logs)
        log_ref[...] = logs

        @pl.when(pl.program_id(0) == 0)
        def _():
            base = 3 * wide
            got, log = head(
                q_ref[0:length, base : base + HD],
                kv_ref[:, base + HD : base + 2 * HD],
                kv_ref[:, base + 2 * HD : base + 3 * HD],
                bias[0:length],
            )
            last_ref[...] = got
            log_ref[0:length, :] = jnp.where(lane[0:length] == heads, log, logs[0:length])

    return call(
        kernel,
        [
            jax.ShapeDtypeStruct((tokens, wide), BF16),
            jax.ShapeDtypeStruct((length, HD), BF16),
            jax.ShapeDtypeStruct((tokens, LANES), F32),
        ],
        [
            pl.BlockSpec((block, wide), lambda b: (b, 0)),
            pl.BlockSpec((length, HD), lambda b: (0, 0)),
            pl.BlockSpec((block, LANES), lambda b: (b, 0)),
        ],
        "split_forward",
        [
            pl.BlockSpec((block, full), lambda b: (b, 0)),
            pl.BlockSpec((tokens, full), lambda b: (0, 0)),
            pl.BlockSpec((block, 2), lambda b: (b, 0)),
            pl.BlockSpec((2, tokens), lambda b: (0, 0)),
        ],
        grid=(tokens // block,),
    )(qkv, qkv, rows_info, cols_info)


def split_backward(qkv, grad_att, grad_last, attended, last, logs, rows_info, cols_info, heads):
    tokens, full = qkv.shape
    length = last.shape[0]
    wide = heads * HD
    block = min(256, tokens)
    steps = tokens // block
    base = 3 * wide

    def kernel(
        q_ref, kv_ref, grad_ref, glast_ref, att_ref, last_ref, log_ref, rows_ref, cols_ref,
        out_ref, sums_ref, acc_ref, bias_ref,
    ):
        step = pl.program_id(0)
        start = pl.multiple_of(step * block, block)

        @pl.when(step == 0)
        def _():
            acc_ref[...] = jnp.zeros_like(acc_ref)
            bias_ref[...] = jnp.zeros_like(bias_ref)
            out_ref[:, base : base + HD] = jnp.zeros((tokens, HD), BF16)

        seen = mask_bias(
            rows_ref[:, 0:1], rows_ref[:, 1:2], cols_ref[0:1, :], cols_ref[1:2, :]
        )

        def head(query, keys, vals, grad, got, log, bias):
            delta = jnp.sum(grad.astype(F32) * got.astype(F32), axis=1, keepdims=True)
            scores = contract_last(query, keys) * SCORE_SCALE + bias
            exact = jnp.exp(scores - log)
            grad_probs = contract_last(grad, vals)
            grad_scores = (exact * (grad_probs - delta) * SCORE_SCALE).astype(BF16)
            return (
                matmul(grad_scores, keys),
                contract_rows(grad_scores, query),
                contract_rows(exact.astype(BF16), grad),
            )

        for h in range(heads):
            own = slice(h * HD, (h + 1) * HD)
            keys_at = slice(wide + h * HD, wide + (h + 1) * HD)
            vals_at = slice(2 * wide + h * HD, 2 * wide + (h + 1) * HD)
            grad_query, grad_key, grad_value = head(
                q_ref[:, own], kv_ref[:, keys_at], kv_ref[:, vals_at],
                grad_ref[:, own], att_ref[:, own], log_ref[:, h : h + 1], seen,
            )
            out_ref[pl.ds(start, block), own] = grad_query.astype(BF16)
            bias_ref[0:1, own] += jnp.sum(grad_query, axis=0, keepdims=True)
            acc_ref[:, own] += grad_key
            acc_ref[:, keys_at] += grad_value

        @pl.when(step == 0)
        def _():
            grad_query, grad_key, grad_value = head(
                q_ref[0:length, base : base + HD],
                kv_ref[:, base + HD : base + 2 * HD],
                kv_ref[:, base + 2 * HD : base + 3 * HD],
                glast_ref[...], last_ref[...], log_ref[0:length, heads : heads + 1],
                seen[0:length],
            )
            out_ref[0:length, base : base + HD] = grad_query.astype(BF16)
            out_ref[:, base + HD : base + 2 * HD] = grad_key.astype(BF16)
            out_ref[:, base + 2 * HD : base + 3 * HD] = grad_value.astype(BF16)
            bias_ref[0:1, wide : wide + HD] = jnp.sum(grad_query, axis=0, keepdims=True)
            bias_ref[1:2, wide : wide + HD] = jnp.sum(grad_value, axis=0, keepdims=True)

        @pl.when(step == steps - 1)
        def _():
            out_ref[:, wide:base] = acc_ref[...].astype(BF16)
            bias_ref[1:2, 0:wide] = jnp.sum(acc_ref[:, wide:], axis=0, keepdims=True)
            sums_ref[...] = bias_ref[...]

    return call(
        kernel,
        [
            jax.ShapeDtypeStruct((tokens, full), BF16),
            jax.ShapeDtypeStruct((8, wide + HD), F32),
        ],
        [
            pl.BlockSpec((tokens, full), lambda b: (0, 0)),
            pl.BlockSpec((8, wide + HD), lambda b: (0, 0)),
        ],
        "split_backward",
        [
            pl.BlockSpec((block, full), lambda b: (b, 0)),
            pl.BlockSpec((tokens, full), lambda b: (0, 0)),
            pl.BlockSpec((block, wide), lambda b: (b, 0)),
            pl.BlockSpec((length, HD), lambda b: (0, 0)),
            pl.BlockSpec((block, wide), lambda b: (b, 0)),
            pl.BlockSpec((length, HD), lambda b: (0, 0)),
            pl.BlockSpec((block, LANES), lambda b: (b, 0)),
            pl.BlockSpec((block, 2), lambda b: (b, 0)),
            pl.BlockSpec((2, tokens), lambda b: (0, 0)),
        ],
        [pltpu.VMEM((tokens, 2 * wide), F32), pltpu.VMEM((8, wide + HD), F32)],
        grid=(steps,),
    )(qkv, qkv, grad_att, grad_last, attended, last, logs, rows_info, cols_info)


def after(value, *others):
    return lax.optimization_barrier((value,) + others)[0]


def on_device_paired(
    count,
    inputs,
    segment,
    cotangent,
    query_weight,
    key_weight,
    value_weight,
    out_weight,
    up_weight,
    down_weight,
    query_bias,
    value_bias,
    out_bias,
    up_bias,
    down_bias,
    first_gain,
    first_shift,
    second_gain,
    second_shift,
):
    me = lax.axis_index("shard")
    copy_index = lax.axis_index("dp")
    core = copy_index & 1
    near = (copy_index >> 1) & 1
    far = (copy_index >> 2) & 1
    others = range(1, count)
    order = me ^ jnp.arange(count, dtype=jnp.int32)
    slots = [me ^ k for k in range(count)]
    length = inputs.shape[1]
    model = inputs.shape[2]
    own = query_weight.shape[0]
    half = own // 2
    hidden = down_weight.shape[0]
    heads = HEADS // count
    wide = heads * HD
    full = 3 * (wide + HD)

    def send(value, k):
        return lax.ppermute(value, "shard", [(j, j ^ k) for j in range(count)])

    def cross(value, k):
        return lax.ppermute(value, "dp", [(j, j ^ k) for j in range(8)])

    def gather(value):
        return [value] + [send(value, k) for k in others]

    def pick(value, index):
        return lax.dynamic_index_in_dim(value, index, 0, False)

    def added(left, right):
        return (left.astype(F32) + right.astype(F32)).astype(BF16)

    def scatter_sum(partial_rows):
        total = partial_rows[0:length]
        for k in others:
            piece = partial_rows[k * length : (k + 1) * length].astype(BF16)
            total = total + send(piece, k).astype(F32)
        return total

    def rows_of_core(value, which):
        return lax.dynamic_slice_in_dim(value, which * half, half, axis=value.ndim - 2)

    def fetch(stacked, mine):
        got = [send(pick(stacked, slots[k]), k) for k in others]
        swapped = cross(jnp.concatenate([g[None] for g in got]), 1)
        pieces, places = [], []
        for k in others:
            pieces += [got[k - 1], swapped[k - 1]]
            places += [2 * slots[k] + core, 2 * slots[k] + 1 - core]
        for side in range(2):
            pieces.append(mine[side * half : (side + 1) * half])
            places.append(2 * me + side)
        return assemble(pieces, places, 2 * count)

    vectors = jnp.stack(
        [
            query_bias, value_bias, out_bias, down_bias,
            first_gain, first_shift, second_gain, second_shift,
        ]
    )
    input_pieces = gather(inputs[0])
    vector_pieces = gather(vectors)
    all_inputs = jnp.concatenate(input_pieces, axis=0)
    vectors = jnp.stack(vector_pieces)[order].transpose(1, 0, 2).reshape(8, model).astype(F32)

    squares = (query_weight, key_weight, value_weight)
    lasts = [w[:, count * wide :] for w in squares]
    stacked_qkv = jnp.stack(
        [
            jnp.concatenate([w[:, j * wide : (j + 1) * wide] for w in squares] + lasts, axis=1)
            for j in range(count)
        ]
    )
    qkv_cols = fetch(rows_of_core(stacked_qkv, core), pick(stacked_qkv, me))
    qkv_cols = qkv_cols.reshape(model, full)

    stacked_up = jnp.stack([up_weight[:, j * hidden : (j + 1) * hidden] for j in range(count)])
    stacked_up = after(stacked_up, *input_pieces[1:])
    up_cols = fetch(rows_of_core(stacked_up, core), pick(stacked_up, me)).reshape(model, hidden)
    out_half = after(rows_of_core(out_weight, core), *input_pieces[1:])
    full_out = fetch(
        jnp.broadcast_to(out_half[None], (count, half, model)), out_weight
    ).reshape(model, model)
    head_out = lax.dynamic_slice_in_dim(full_out, me * wide, wide, axis=0)
    last_out = full_out[count * wide :]
    cot_pieces = gather(after(cotangent[0], qkv_cols))
    all_cot = jnp.concatenate(cot_pieces, axis=0)

    pos = (order[:, None] * length + jnp.arange(length, dtype=jnp.int32)[None, :]).reshape(-1)
    seg = segment[0].reshape(count, length)[order].reshape(-1)
    rows_info = jnp.stack([seg, pos], axis=1)
    cols_info = jnp.stack([seg, pos], axis=0)

    head_slice = lambda v: lax.dynamic_slice_in_dim(v, me * wide, wide)
    tail = lambda v: v[count * wide :]
    qkv_bias = jnp.concatenate(
        [
            head_slice(vectors[0]), jnp.zeros((wide,), F32), head_slice(vectors[1]),
            tail(vectors[0]), jnp.zeros((HD,), F32), tail(vectors[1]),
        ]
    )

    first_gain_full, first_shift_full = vectors[4], vectors[5]
    second_gain_full, second_shift_full = vectors[6], vectors[7]
    all_hat, _ = normalise(all_inputs.astype(F32))
    first_in = (all_hat * first_gain_full + first_shift_full).astype(BF16)
    qkv = (matmul(first_in, qkv_cols) + qkv_bias).astype(BF16)
    attended, last, logs = split_forward(qkv, rows_info, cols_info, heads, length)
    att_pieces = [attended[0:length]] + [
        send(attended[k * length : (k + 1) * length], k) for k in others
    ]
    own_attended = place_heads(att_pieces, last, slots, wide)
    residual_in = inputs[0].astype(F32)
    middle = residual_in + matmul(own_attended, full_out) + vectors[2]
    second_hat, second_inv = normalise(middle)
    own_second_in = (second_hat * second_gain_full + second_shift_full).astype(BF16)
    second_in = jnp.concatenate(gather(own_second_in), axis=0)
    pre_act = matmul(second_in, up_cols) + up_bias.astype(F32)
    below = 0.5 * (1.0 + lax.erf(pre_act * (0.5**0.5)))
    activated = (pre_act * below).astype(BF16)
    slope = below + pre_act * (jnp.exp(-0.5 * pre_act * pre_act) * 0.3989422804014327)
    grad_pre = contract_last(all_cot, down_weight) * slope
    grad_pre_low = grad_pre.astype(BF16)
    up_bias_part = jnp.sum(grad_pre, axis=0)
    grad_second = scatter_sum(contract_last(grad_pre_low, up_cols))

    def reduce_far(part):
        keep = lax.dynamic_slice_in_dim(part, 2 * near, 2, axis=0)
        give = lax.dynamic_slice_in_dim(part, 2 - 2 * near, 2, axis=0)
        pair = added(keep, cross(give, 2))
        one = added(pick(pair, far), cross(pick(pair, 1 - far), 4))
        pair = assemble([one, cross(one, 4)], [far, 1 - far], 2)
        whole = assemble([pair, cross(pair, 2)], [near, 1 - near], 2)
        whole = whole.reshape((4,) + part.shape[1:])
        return assemble([whole, cross(whole, 1)], [core, 1 - core], 2)

    down_part = contract_rows(activated, all_cot).astype(BF16)
    down_part = down_part.reshape(2, 4, hidden // 8, model)
    down_sum = reduce_far(added(pick(down_part, core), cross(pick(down_part, 1 - core), 1)))
    down_weight_grad = down_sum.reshape(hidden, model).astype(F32)

    up_part = contract_rows(second_in, grad_pre_low).astype(BF16).reshape(count, own, hidden)
    up_part = added(rows_of_core(up_part, core), cross(rows_of_core(up_part, 1 - core), 1))
    up_pieces = [pick(up_part, me)] + [send(pick(up_part, slots[k]), k) for k in others]
    up_sum = reduce_far(assemble(up_pieces, slots, count))
    up_weight_grad = (
        up_sum.transpose(0, 2, 1, 3).reshape(own, count * hidden).astype(F32)
    )

    cot_float = cotangent[0].astype(F32)
    grad_middle = cot_float + norm_backward(
        grad_second, second_hat, second_inv, second_gain_full
    )
    grad_middle_low = grad_middle.astype(BF16)
    all_grad_middle = jnp.concatenate(gather(grad_middle_low), axis=0)
    grad_attended = contract_last(all_grad_middle, head_out).astype(BF16)
    grad_last = contract_last(grad_middle_low, last_out).astype(BF16)
    grad_qkv, head_sums = split_backward(
        qkv, grad_attended, grad_last, attended, last, logs, rows_info, cols_info, heads
    )
    qkv_part = contract_rows(first_in, grad_qkv).astype(BF16).reshape(count, own, full)
    grad_first = scatter_sum(contract_last(grad_qkv, qkv_cols))
    first_hat, first_inv = normalise(residual_in)
    input_grad = grad_middle + norm_backward(grad_first, first_hat, first_inv, first_gain_full)

    features = jnp.stack([own_attended[:, j * own : (j + 1) * own] for j in range(count)])
    own_features = jnp.concatenate(
        [pick(features, me)] + [send(pick(features, slots[k]), k) for k in others], axis=0
    )
    out_part = contract_rows(own_features, all_grad_middle).astype(BF16)
    out_part = added(rows_of_core(out_part, core), cross(rows_of_core(out_part, 1 - core), 1))
    qkv_part = added(rows_of_core(qkv_part, core), cross(rows_of_core(qkv_part, 1 - core), 1))
    qkv_pieces = [pick(qkv_part, me)] + [send(pick(qkv_part, slots[k]), k) for k in others]
    square = reduce_far(place_grads(out_part, qkv_pieces, slots, wide))
    square = square.transpose(1, 0, 2, 3).reshape(4, own, model).astype(F32)
    outputs = (
        middle + scatter_sum(matmul(activated, down_weight)) + vectors[3]
    ).astype(BF16)

    def to_full(row):
        main = lax.dynamic_update_slice(
            jnp.zeros((count * wide,), F32), row[:wide], (me * wide,)
        )
        return jnp.concatenate([main, row[wide:]])

    partials = jnp.stack(
        [
            to_full(head_sums[0]),
            to_full(head_sums[1]),
            jnp.sum(grad_middle, axis=0),
            jnp.sum(cot_float, axis=0),
            jnp.sum(grad_first * first_hat, axis=0),
            jnp.sum(grad_first, axis=0),
            jnp.sum(grad_second * second_hat, axis=0),
            jnp.sum(grad_second, axis=0),
        ]
    )
    rows = partials.reshape(8, count, own).transpose(1, 0, 2)
    mine = pick(rows, me)
    for k in others:
        mine = mine + send(pick(rows, slots[k]), k)
    summed = jnp.concatenate([mine, up_bias_part.reshape(count, own)], axis=0)
    for k in (1, 2, 4):
        summed = summed + cross(summed, k)
    return (
        outputs[None],
        input_grad[None],
        square[1],
        square[2],
        square[3],
        square[0],
        up_weight_grad,
        down_weight_grad,
        summed[0],
        summed[1],
        summed[2],
        summed[8:].reshape(hidden),
        summed[3],
        summed[4],
        summed[5],
        summed[6],
        summed[7],
    )


def on_device(count, copies, *args):
    model = args[0].shape[2]
    heads = HEADS // count
    paired = (
        count == 4
        and copies == 8
        and HEADS == count * heads + 1
        and (heads * HD) % LANES == 0
        and model % (count * 16) == 0
        and args[0].shape[1] <= 256
        and args[8].shape[0] == model
    )
    if paired:
        return on_device_paired(count, *args)
    return on_device_general(count, *args)


def solution(mesh):
    tokens = P("dp", "shard", None)
    matrix = P("shard", None)
    vector = P("shard")
    return jax.shard_map(
        partial(on_device, mesh.shape["shard"], mesh.shape["dp"]),
        mesh=mesh,
        in_specs=(tokens, P("dp", None), tokens) + (matrix,) * 6 + (vector,) * 9,
        out_specs=(tokens, tokens) + (matrix,) * 6 + (vector,) * 9,
        check_vma=False,
    )
```

```python
from functools import partial

import jax
import jax.numpy as jnp
from jax import lax
from jax.experimental import pallas as pl
from jax.experimental.pallas import tpu as pltpu
from jax.sharding import PartitionSpec as P


HEADS = 17
HD = 64
EPSILON = 1e-05
SCORE_SCALE = 0.125
MASKED_SCORE = -1e30
LANES = 128
MANY = 4


BF16 = jnp.bfloat16
F32 = jnp.float32


def normalise(values):
    average = jnp.mean(values, axis=-1, keepdims=True)
    centred = values - average
    variance = jnp.mean(centred * centred, axis=-1, keepdims=True)
    inv_std = lax.rsqrt(variance + EPSILON)
    return centred * inv_std, inv_std


def norm_backward(grad_normed, normed, inv_std, gain_vec):
    scaled = grad_normed * gain_vec
    first_mean = jnp.mean(scaled, axis=-1, keepdims=True)
    second_mean = jnp.mean(scaled * normed, axis=-1, keepdims=True)
    return inv_std * (scaled - first_mean - normed * second_mean)


def matmul(left_side, right_side):
    return jnp.dot(left_side, right_side, preferred_element_type=F32)


def contract_rows(left_side, right_side):
    return lax.dot_general(
        left_side, right_side, (((0,), (0,)), ((), ())), preferred_element_type=F32
    )


def contract_last(left_side, right_side):
    return lax.dot_general(
        left_side, right_side, (((1,), (1,)), ((), ())), preferred_element_type=F32
    )


def mask_bias(row_seg, row_pos, col_seg, col_pos):
    allowed = (row_seg == col_seg) & (col_pos <= row_pos)
    return jnp.where(allowed, 0.0, MASKED_SCORE)


def attention_forward(qkv, rows_info, cols_info, heads):
    tokens = qkv.shape[0]
    width = heads * HD
    block = min(256, tokens)

    def kernel(q_ref, kv_ref, rows_ref, cols_ref, out_ref, log_ref):
        bias = mask_bias(
            rows_ref[:, 0:1], rows_ref[:, 1:2], cols_ref[0:1, :], cols_ref[1:2, :]
        )
        lane = lax.broadcasted_iota(jnp.int32, (block, LANES), 1)
        logs = jnp.zeros((block, LANES), F32)
        for h in range(heads):
            query = q_ref[:, h * HD : (h + 1) * HD]
            keys = kv_ref[:, width + h * HD : width + (h + 1) * HD]
            vals = kv_ref[:, 2 * width + h * HD : 2 * width + (h + 1) * HD]
            scores = contract_last(query, keys) * SCORE_SCALE + bias
            largest = jnp.max(scores, axis=1, keepdims=True)
            grown = jnp.exp(scores - largest)
            total = jnp.sum(grown, axis=1, keepdims=True)
            probs = (grown * (1.0 / total)).astype(BF16)
            out_ref[:, h * HD : (h + 1) * HD] = matmul(probs, vals).astype(BF16)
            logs = jnp.where(lane == h, largest + jnp.log(total), logs)
        log_ref[...] = logs

    return pl.pallas_call(
        kernel,
        grid=(tokens // block,),
        in_specs=[
            pl.BlockSpec((block, 3 * width), lambda b: (b, 0)),
            pl.BlockSpec((tokens, 3 * width), lambda b: (0, 0)),
            pl.BlockSpec((block, 2), lambda b: (b, 0)),
            pl.BlockSpec((2, tokens), lambda b: (0, 0)),
        ],
        out_specs=[
            pl.BlockSpec((block, width), lambda b: (b, 0)),
            pl.BlockSpec((block, LANES), lambda b: (b, 0)),
        ],
        out_shape=[
            jax.ShapeDtypeStruct((tokens, width), BF16),
            jax.ShapeDtypeStruct((tokens, LANES), F32),
        ],
        name="attention_forward",
    )(qkv, qkv, rows_info, cols_info)


def attention_backward(qkv, grad_att, attended, logs, rows_info, cols_info, heads):
    tokens = qkv.shape[0]
    width = heads * HD
    block = min(256, tokens)
    steps = tokens // block

    def kernel(
        q_ref, kv_ref, grad_ref, att_ref, log_ref, rows_ref, cols_ref,
        gq_ref, gkv_ref, sums_ref, acc_ref, bias_ref,
    ):
        step = pl.program_id(0)

        @pl.when(step == 0)
        def _():
            acc_ref[...] = jnp.zeros_like(acc_ref)
            bias_ref[...] = jnp.zeros_like(bias_ref)

        bias = mask_bias(
            rows_ref[:, 0:1], rows_ref[:, 1:2], cols_ref[0:1, :], cols_ref[1:2, :]
        )
        for h in range(heads):
            own = slice(h * HD, (h + 1) * HD)
            query = q_ref[:, own]
            keys = kv_ref[:, width + h * HD : width + (h + 1) * HD]
            vals = kv_ref[:, 2 * width + h * HD : 2 * width + (h + 1) * HD]
            grad = grad_ref[:, own]
            delta = jnp.sum(
                grad.astype(F32) * att_ref[:, own].astype(F32), axis=1, keepdims=True
            )
            scores = contract_last(query, keys) * SCORE_SCALE + bias
            exact = jnp.exp(scores - log_ref[:, h : h + 1])
            grad_probs = contract_last(grad, vals)
            grad_scores = (exact * (grad_probs - delta) * SCORE_SCALE).astype(BF16)
            grad_query = matmul(grad_scores, keys)
            gq_ref[:, own] = grad_query.astype(BF16)
            bias_ref[0:1, own] += jnp.sum(grad_query, axis=0, keepdims=True)
            acc_ref[:, own] += contract_rows(grad_scores, query)
            acc_ref[:, width + h * HD : width + (h + 1) * HD] += contract_rows(
                exact.astype(BF16), grad
            )

        @pl.when(step == steps - 1)
        def _():
            gkv_ref[...] = acc_ref[...].astype(BF16)
            bias_ref[1:2, :] = jnp.sum(acc_ref[:, width:], axis=0, keepdims=True)
            sums_ref[...] = bias_ref[...]

    return pl.pallas_call(
        kernel,
        grid=(steps,),
        in_specs=[
            pl.BlockSpec((block, 3 * width), lambda b: (b, 0)),
            pl.BlockSpec((tokens, 3 * width), lambda b: (0, 0)),
            pl.BlockSpec((block, width), lambda b: (b, 0)),
            pl.BlockSpec((block, width), lambda b: (b, 0)),
            pl.BlockSpec((block, LANES), lambda b: (b, 0)),
            pl.BlockSpec((block, 2), lambda b: (b, 0)),
            pl.BlockSpec((2, tokens), lambda b: (0, 0)),
        ],
        out_specs=[
            pl.BlockSpec((block, width), lambda b: (b, 0)),
            pl.BlockSpec((tokens, 2 * width), lambda b: (0, 0)),
            pl.BlockSpec((8, width), lambda b: (0, 0)),
        ],
        out_shape=[
            jax.ShapeDtypeStruct((tokens, width), BF16),
            jax.ShapeDtypeStruct((tokens, 2 * width), BF16),
            jax.ShapeDtypeStruct((8, width), F32),
        ],
        scratch_shapes=[
            pltpu.VMEM((tokens, 2 * width), F32),
            pltpu.VMEM((8, width), F32),
        ],
        name="attention_backward",
    )(qkv, qkv, grad_att, attended, logs, rows_info, cols_info)


def on_device_general(
    count,
    inputs,
    segment,
    cotangent,
    query_weight,
    key_weight,
    value_weight,
    out_weight,
    up_weight,
    down_weight,
    query_bias,
    value_bias,
    out_bias,
    up_bias,
    down_bias,
    first_gain,
    first_shift,
    second_gain,
    second_shift,
):
    me = lax.axis_index("shard")
    others = range(1, count)
    order = me ^ jnp.arange(count, dtype=jnp.int32)
    length = inputs.shape[1]
    model = inputs.shape[2]
    own = query_weight.shape[0]
    hidden = down_weight.shape[0]
    per = -(-HEADS // count)
    width = per * HD
    padded = count * width

    def send(value, k):
        return lax.ppermute(value, "shard", [(j, j ^ k) for j in range(count)])

    def gather(value):
        if count > MANY:
            whole = lax.all_gather(value, "shard")
            return [lax.dynamic_index_in_dim(whole, me ^ k, 0, False) for k in range(count)]
        return [value] + [send(value, k) for k in others]

    def swap(pieces):
        if count > MANY:
            whole = jnp.stack(pieces)[order]
            whole = lax.all_to_all(whole, "shard", split_axis=0, concat_axis=0)[order]
            return [whole[k] for k in range(count)]
        return [pieces[0]] + [send(pieces[k], k) for k in others]

    def scatter_sum(partial_rows):
        blocks = [partial_rows[k * length : (k + 1) * length] for k in range(count)]
        got = swap([b.astype(BF16) for b in blocks])
        return sum((v.astype(F32) for v in got[1:]), blocks[0])

    def in_order(pieces):
        rows = pieces[0].shape[0]
        whole = jnp.zeros((count * rows,) + pieces[0].shape[1:], pieces[0].dtype)
        for k in range(count):
            start = ((me ^ k) * rows,) + (0,) * (pieces[0].ndim - 1)
            whole = lax.dynamic_update_slice(whole, pieces[k], start)
        return whole

    def exchange(stacked):
        return swap(
            [lax.dynamic_index_in_dim(stacked, me ^ k, 0, False) for k in range(count)]
        )

    vectors = jnp.stack(
        [
            query_bias, value_bias, out_bias, down_bias,
            first_gain, first_shift, second_gain, second_shift,
        ]
    )
    vectors = in_order([v[None] for v in gather(vectors)])
    vectors = vectors.transpose(1, 0, 2).reshape(8, model).astype(F32)
    all_inputs = jnp.concatenate(gather(inputs[0]), axis=0)
    pad_cols = lambda w: jnp.pad(w, ((0, 0), (0, padded - model)))
    stacked_qkv = jnp.concatenate(
        [
            pad_cols(w).reshape(own, count, width)
            for w in (query_weight, key_weight, value_weight)
        ],
        axis=2,
    ).transpose(1, 0, 2)
    qkv_cols = in_order(exchange(stacked_qkv))
    all_cot = jnp.concatenate(gather(cotangent[0]), axis=0)
    full_out = jnp.pad(in_order(gather(out_weight)), ((0, padded - model), (0, 0)))
    head_out = lax.dynamic_slice_in_dim(full_out, me * width, width, axis=0)
    mixed_out = full_out.reshape(count, width, model)[order].reshape(padded, model)
    up_cols = in_order(exchange(up_weight.reshape(own, count, hidden).transpose(1, 0, 2)))

    pos = (order[:, None] * length + jnp.arange(length, dtype=jnp.int32)[None, :]).reshape(-1)
    seg = segment[0].reshape(count, length)[order].reshape(-1)
    rows_info = jnp.stack([seg, pos], axis=1)
    cols_info = jnp.stack([seg, pos], axis=0)

    head_slice = lambda v: lax.dynamic_slice_in_dim(
        jnp.pad(v, (0, padded - model)), me * width, width
    )
    qkv_bias = jnp.concatenate(
        [head_slice(vectors[0]), jnp.zeros((width,), F32), head_slice(vectors[1])]
    )

    first_gain_full, first_shift_full = vectors[4], vectors[5]
    second_gain_full, second_shift_full = vectors[6], vectors[7]
    all_hat, _ = normalise(all_inputs.astype(F32))
    first_in = (all_hat * first_gain_full + first_shift_full).astype(BF16)
    qkv = (matmul(first_in, qkv_cols) + qkv_bias).astype(BF16)
    attended, logs = attention_forward(qkv, rows_info, cols_info, per)
    att_pieces = swap([attended[k * length : (k + 1) * length] for k in range(count)])
    residual_in = inputs[0].astype(F32)
    own_attended = jnp.concatenate(att_pieces, axis=1)
    middle = residual_in + matmul(own_attended, mixed_out) + vectors[2]
    second_hat, second_inv = normalise(middle)
    own_second_in = (second_hat * second_gain_full + second_shift_full).astype(BF16)
    second_in = jnp.concatenate(gather(own_second_in), axis=0)
    pre_act = matmul(second_in, up_cols) + up_bias.astype(F32)
    below = 0.5 * (1.0 + lax.erf(pre_act * (0.5**0.5)))
    activated = (pre_act * below).astype(BF16)
    slope = below + pre_act * (jnp.exp(-0.5 * pre_act * pre_act) * 0.3989422804014327)
    grad_pre = contract_last(all_cot, down_weight) * slope
    grad_pre_low = grad_pre.astype(BF16)
    up_bias_part = jnp.sum(grad_pre, axis=0)
    grad_second = scatter_sum(contract_last(grad_pre_low, up_cols))
    outputs = (
        middle + scatter_sum(matmul(activated, down_weight)) + vectors[3]
    ).astype(BF16)

    down_part = contract_rows(activated, all_cot).astype(BF16)
    up_part = contract_rows(second_in, grad_pre_low).astype(BF16)
    up_rows = exchange(up_part.reshape(count, own, hidden))

    def reduce_dp(part, dim):
        share = lax.psum_scatter(part, "dp", scatter_dimension=dim, tiled=True)
        return lax.all_gather(share, "dp", axis=dim, tiled=True).astype(F32)

    down_weight_grad = reduce_dp(down_part, 0)
    up_rows = in_order([v[None] for v in up_rows])
    up_total = reduce_dp(up_rows.reshape(count * own, hidden), 0)
    up_weight_grad = (
        up_total.reshape(count, own, hidden).transpose(1, 0, 2).reshape(own, count * hidden)
    )

    grad_middle = cotangent[0].astype(F32) + norm_backward(
        grad_second, second_hat, second_inv, second_gain_full
    )
    grad_middle_low = grad_middle.astype(BF16)
    all_grad_middle = jnp.concatenate(gather(grad_middle_low), axis=0)
    grad_attended = contract_last(all_grad_middle, head_out).astype(BF16)
    grad_queries, grad_kv, head_sums = attention_backward(
        qkv, grad_attended, attended, logs, rows_info, cols_info, per
    )
    grad_qkv = jnp.concatenate([grad_queries, grad_kv], axis=1)
    grad_first = scatter_sum(contract_last(grad_qkv, qkv_cols))
    first_hat, first_inv = normalise(residual_in)
    input_grad = grad_middle + norm_backward(grad_first, first_hat, first_inv, first_gain_full)

    true_attended = in_order([v[None] for v in att_pieces])
    true_attended = true_attended.transpose(1, 0, 2).reshape(length, padded)[:, :model]
    own_features = jnp.concatenate(
        exchange(true_attended.reshape(length, count, own).transpose(1, 0, 2)), axis=0
    )
    out_part = contract_rows(own_features, all_grad_middle).astype(BF16)
    qkv_part = contract_rows(first_in, grad_qkv).astype(BF16)
    qkv_rows = exchange(qkv_part.reshape(count, own, 3 * width))
    qkv_rows = in_order([v[None] for v in qkv_rows]).reshape(count, own, 3, width)
    qkv_rows = qkv_rows.transpose(2, 1, 0, 3).reshape(3, own, padded)[:, :, :model]
    square = reduce_dp(jnp.concatenate([out_part[None], qkv_rows]).reshape(4 * own, model), 0)
    square = square.reshape(4, own, model)

    to_full = lambda v: lax.dynamic_update_slice(
        jnp.zeros((padded,), F32), v, (me * width,)
    )[:model]
    partials = jnp.stack(
        [
            to_full(head_sums[0]),
            to_full(head_sums[1]),
            jnp.sum(grad_middle, axis=0),
            jnp.sum(cotangent[0].astype(F32), axis=0),
            jnp.sum(grad_first * first_hat, axis=0),
            jnp.sum(grad_first, axis=0),
            jnp.sum(grad_second * second_hat, axis=0),
            jnp.sum(grad_second, axis=0),
        ]
    )
    vector_rows = sum(exchange(partials.reshape(8, count, own).transpose(1, 0, 2)))
    summed, up_bias_grad = lax.psum((vector_rows, up_bias_part), "dp")
    return (
        outputs[None],
        input_grad[None],
        square[1],
        square[2],
        square[3],
        square[0],
        up_weight_grad,
        down_weight_grad,
        summed[0],
        summed[1],
        summed[2],
        up_bias_grad,
        summed[3],
        summed[4],
        summed[5],
        summed[6],
        summed[7],
    )


def call(kernel, out_shape, out_specs, in_specs, scratch=(), grid=()):
    return pl.pallas_call(
        kernel,
        grid=grid,
        in_specs=in_specs,
        out_specs=out_specs,
        out_shape=out_shape,
        scratch_shapes=scratch,
    )


def assemble(pieces, slots, total):
    amount = len(pieces)
    shape = pieces[0].shape[-2:]

    def kernel(slot_ref, *refs):
        out_ref = refs[amount]
        at = 0
        for ref in refs[:amount]:
            parts = [ref[...]] if len(ref.shape) == 2 else [ref[k] for k in range(ref.shape[0])]
            for part in parts:
                out_ref[slot_ref[at]] = part
                at += 1

    return call(
        kernel,
        jax.ShapeDtypeStruct((total,) + shape, pieces[0].dtype),
        pl.BlockSpec(memory_space=pltpu.VMEM),
        [pl.BlockSpec(memory_space=pltpu.SMEM)]
        + [pl.BlockSpec(memory_space=pltpu.VMEM)] * amount,
    )(jnp.stack(slots).astype(jnp.int32), *pieces)


def grad_columns(first_in, grad_qkv, core, count):
    model = first_in.shape[1]
    full = grad_qkv.shape[1]
    own = model // count
    half = own // 2

    def kernel(core_ref, in_ref, grad_ref, keep_ref, give_ref, acc_ref):
        acc_ref[...] = contract_rows(in_ref[...], grad_ref[...])
        for j in range(count):
            for side, ref in enumerate((keep_ref, give_ref)):
                which = core_ref[0] if side == 0 else 1 - core_ref[0]
                start = pl.multiple_of(j * own + which * half, 8)
                ref[j] = acc_ref[pl.ds(start, half), :].astype(BF16)

    return call(
        kernel,
        [jax.ShapeDtypeStruct((count, half, full), BF16)] * 2,
        [pl.BlockSpec(memory_space=pltpu.VMEM)] * 2,
        [pl.BlockSpec(memory_space=pltpu.SMEM)] + [pl.BlockSpec(memory_space=pltpu.VMEM)] * 2,
        [pltpu.VMEM((model, full), F32)],
    )(core[None].astype(jnp.int32), first_in, grad_qkv)


def unfold(mine, theirs, core, near, far, mode):
    blocks = len(mine)
    half, model = mine[0].shape
    shapes = {
        "rows": [(2 * blocks, half, model)],
        "columns": [(2 * half, blocks * model)],
        "arrays": [(2 * half, model)] * blocks,
    }[mode]

    def kernel(bits_ref, *refs):
        out_refs = refs[2 * blocks :]
        mask = bits_ref[1] * 2 + bits_ref[2]
        for side in range(2):
            where = bits_ref[0] if side == 0 else 1 - bits_ref[0]
            rows = pl.ds(pl.multiple_of(where * half, 8), half)
            values = [refs[side * blocks + k][...] for k in range(blocks)]
            for slot in range(blocks):
                if mode == "rows":
                    out_refs[0][where * blocks + (slot ^ mask)] = values[slot].astype(F32)
                    continue
                block = values[slot]
                for k in range(1, blocks):
                    block = jnp.where(mask == k, values[slot ^ k], block)
                if mode == "columns":
                    out_refs[0][rows, slot * model : (slot + 1) * model] = block.astype(F32)
                else:
                    out_refs[slot][rows, :] = block.astype(F32)

    return call(
        kernel,
        [jax.ShapeDtypeStruct(shape, F32) for shape in shapes],
        [pl.BlockSpec(memory_space=pltpu.VMEM)] * len(shapes),
        [pl.BlockSpec(memory_space=pltpu.SMEM)]
        + [pl.BlockSpec(memory_space=pltpu.VMEM)] * (2 * blocks),
    )(jnp.stack([core, near, far]).astype(jnp.int32), *mine, *theirs)


def cut_columns(weights, me, core, count, wide):
    rows, _ = weights[0].shape
    half = rows // 2
    full = 3 * (wide + HD)

    def kernel(place_ref, *refs):
        outs = refs[3:]
        for k in range(count):
            start = pl.multiple_of((place_ref[0] ^ k) * wide, LANES)
            for m in range(3):
                main = refs[m][:, pl.ds(start, wide)]
                extra = refs[m][:, count * wide :]
                if k > 0:
                    main = jnp.where(place_ref[1] == 0, main[:half], main[half:])
                    extra = jnp.where(place_ref[1] == 0, extra[:half], extra[half:])
                outs[k][:, m * wide : (m + 1) * wide] = main
                outs[k][:, 3 * wide + m * HD : 3 * wide + (m + 1) * HD] = extra

    return call(
        kernel,
        [
            jax.ShapeDtypeStruct((rows if k == 0 else half, full), BF16)
            for k in range(count)
        ],
        [pl.BlockSpec(memory_space=pltpu.VMEM)] * count,
        [pl.BlockSpec(memory_space=pltpu.SMEM)] + [pl.BlockSpec(memory_space=pltpu.VMEM)] * 3,
    )(jnp.stack([me, core]).astype(jnp.int32), *weights)


def place_heads(pieces, last, slots, wide):
    amount = len(pieces)
    rows = pieces[0].shape[0]
    model = amount * wide + HD

    def kernel(slot_ref, *refs):
        out_ref = refs[amount + 1]
        for k in range(amount):
            start = pl.multiple_of(slot_ref[k] * wide, LANES)
            out_ref[:, pl.ds(start, wide)] = refs[k][...]
        out_ref[:, amount * wide :] = refs[amount][...]

    return call(
        kernel,
        jax.ShapeDtypeStruct((rows, model), BF16),
        pl.BlockSpec(memory_space=pltpu.VMEM),
        [pl.BlockSpec(memory_space=pltpu.SMEM)]
        + [pl.BlockSpec(memory_space=pltpu.VMEM)] * (amount + 1),
    )(jnp.stack(slots).astype(jnp.int32), *pieces, last)


def place_grads(out_part, pieces, slots, wide):
    amount = len(pieces)
    rows, model = out_part.shape

    def kernel(slot_ref, *refs):
        out_ref = refs[amount + 1]
        out_ref[0] = refs[0][...]
        for m in range(3):
            extra = slice(3 * wide + m * HD, 3 * wide + (m + 1) * HD)
            shared = refs[1][:, extra].astype(F32)
            for k in range(amount):
                start = pl.multiple_of(slot_ref[k] * wide, LANES)
                out_ref[1 + m, :, pl.ds(start, wide)] = refs[1 + k][:, m * wide : (m + 1) * wide]
                if k > 0:
                    shared = shared + refs[1 + k][:, extra].astype(F32)
            out_ref[1 + m, :, amount * wide :] = shared.astype(BF16)

    return call(
        kernel,
        jax.ShapeDtypeStruct((4, rows, model), BF16),
        pl.BlockSpec(memory_space=pltpu.VMEM),
        [pl.BlockSpec(memory_space=pltpu.SMEM)]
        + [pl.BlockSpec(memory_space=pltpu.VMEM)] * (amount + 1),
    )(jnp.stack(slots).astype(jnp.int32), out_part, *pieces)


def split_forward(qkv, rows_info, cols_info, heads, length):
    tokens = qkv.shape[0]
    wide = heads * HD
    block = min(256, tokens)
    full = qkv.shape[1]

    def kernel(q_ref, kv_ref, rows_ref, cols_ref, out_ref, last_ref, log_ref):
        bias = mask_bias(
            rows_ref[:, 0:1], rows_ref[:, 1:2], cols_ref[0:1, :], cols_ref[1:2, :]
        )
        lane = lax.broadcasted_iota(jnp.int32, (block, LANES), 1)

        def head(query, keys, vals, seen):
            scores = contract_last(query, keys) * SCORE_SCALE + seen
            largest = jnp.max(scores, axis=1, keepdims=True)
            grown = jnp.exp(scores - largest)
            total = jnp.sum(grown, axis=1, keepdims=True)
            probs = (grown * (1.0 / total)).astype(BF16)
            return matmul(probs, vals).astype(BF16), largest + jnp.log(total)

        logs = jnp.zeros((block, LANES), F32)
        for h in range(heads):
            own = slice(h * HD, (h + 1) * HD)
            got, log = head(
                q_ref[:, own],
                kv_ref[:, wide + h * HD : wide + (h + 1) * HD],
                kv_ref[:, 2 * wide + h * HD : 2 * wide + (h + 1) * HD],
                bias,
            )
            out_ref[:, own] = got
            logs = jnp.where(lane == h, log, logs)
        log_ref[...] = logs

        @pl.when(pl.program_id(0) == 0)
        def _():
            base = 3 * wide
            got, log = head(
                q_ref[0:length, base : base + HD],
                kv_ref[:, base + HD : base + 2 * HD],
                kv_ref[:, base + 2 * HD : base + 3 * HD],
                bias[0:length],
            )
            last_ref[...] = got
            log_ref[0:length, :] = jnp.where(lane[0:length] == heads, log, logs[0:length])

    return call(
        kernel,
        [
            jax.ShapeDtypeStruct((tokens, wide), BF16),
            jax.ShapeDtypeStruct((length, HD), BF16),
            jax.ShapeDtypeStruct((tokens, LANES), F32),
        ],
        [
            pl.BlockSpec((block, wide), lambda b: (b, 0)),
            pl.BlockSpec((length, HD), lambda b: (0, 0)),
            pl.BlockSpec((block, LANES), lambda b: (b, 0)),
        ],
        [
            pl.BlockSpec((block, full), lambda b: (b, 0)),
            pl.BlockSpec((tokens, full), lambda b: (0, 0)),
            pl.BlockSpec((block, 2), lambda b: (b, 0)),
            pl.BlockSpec((2, tokens), lambda b: (0, 0)),
        ],
        grid=(tokens // block,),
    )(qkv, qkv, rows_info, cols_info)


def split_backward(qkv, grad_att, grad_last, attended, last, logs, rows_info, cols_info, heads):
    tokens, full = qkv.shape
    length = last.shape[0]
    wide = heads * HD
    block = min(256, tokens)
    steps = tokens // block
    base = 3 * wide

    def kernel(
        q_ref, kv_ref, grad_ref, glast_ref, att_ref, last_ref, log_ref, rows_ref, cols_ref,
        out_ref, sums_ref, acc_ref, bias_ref,
    ):
        step = pl.program_id(0)
        start = pl.multiple_of(step * block, block)

        @pl.when(step == 0)
        def _():
            acc_ref[...] = jnp.zeros_like(acc_ref)
            bias_ref[...] = jnp.zeros_like(bias_ref)
            out_ref[:, base : base + HD] = jnp.zeros((tokens, HD), BF16)

        seen = mask_bias(
            rows_ref[:, 0:1], rows_ref[:, 1:2], cols_ref[0:1, :], cols_ref[1:2, :]
        )

        def head(query, keys, vals, grad, got, log, bias):
            delta = jnp.sum(grad.astype(F32) * got.astype(F32), axis=1, keepdims=True)
            scores = contract_last(query, keys) * SCORE_SCALE + bias
            exact = jnp.exp(scores - log)
            grad_probs = contract_last(grad, vals)
            grad_scores = (exact * (grad_probs - delta) * SCORE_SCALE).astype(BF16)
            return (
                matmul(grad_scores, keys),
                contract_rows(grad_scores, query),
                contract_rows(exact.astype(BF16), grad),
            )

        for h in range(heads):
            own = slice(h * HD, (h + 1) * HD)
            keys_at = slice(wide + h * HD, wide + (h + 1) * HD)
            vals_at = slice(2 * wide + h * HD, 2 * wide + (h + 1) * HD)
            grad_query, grad_key, grad_value = head(
                q_ref[:, own], kv_ref[:, keys_at], kv_ref[:, vals_at],
                grad_ref[:, own], att_ref[:, own], log_ref[:, h : h + 1], seen,
            )
            out_ref[pl.ds(start, block), own] = grad_query.astype(BF16)
            bias_ref[0:1, own] += jnp.sum(grad_query, axis=0, keepdims=True)
            acc_ref[:, own] += grad_key
            acc_ref[:, keys_at] += grad_value

        @pl.when(step == 0)
        def _():
            grad_query, grad_key, grad_value = head(
                q_ref[0:length, base : base + HD],
                kv_ref[:, base + HD : base + 2 * HD],
                kv_ref[:, base + 2 * HD : base + 3 * HD],
                glast_ref[...], last_ref[...], log_ref[0:length, heads : heads + 1],
                seen[0:length],
            )
            out_ref[0:length, base : base + HD] = grad_query.astype(BF16)
            out_ref[:, base + HD : base + 2 * HD] = grad_key.astype(BF16)
            out_ref[:, base + 2 * HD : base + 3 * HD] = grad_value.astype(BF16)
            bias_ref[0:1, wide : wide + HD] = jnp.sum(grad_query, axis=0, keepdims=True)
            bias_ref[1:2, wide : wide + HD] = jnp.sum(grad_value, axis=0, keepdims=True)

        @pl.when(step == steps - 1)
        def _():
            out_ref[:, wide:base] = acc_ref[...].astype(BF16)
            bias_ref[1:2, 0:wide] = jnp.sum(acc_ref[:, wide:], axis=0, keepdims=True)
            sums_ref[...] = bias_ref[...]

    return call(
        kernel,
        [
            jax.ShapeDtypeStruct((tokens, full), BF16),
            jax.ShapeDtypeStruct((8, wide + HD), F32),
        ],
        [
            pl.BlockSpec((tokens, full), lambda b: (0, 0)),
            pl.BlockSpec((8, wide + HD), lambda b: (0, 0)),
        ],
        [
            pl.BlockSpec((block, full), lambda b: (b, 0)),
            pl.BlockSpec((tokens, full), lambda b: (0, 0)),
            pl.BlockSpec((block, wide), lambda b: (b, 0)),
            pl.BlockSpec((length, HD), lambda b: (0, 0)),
            pl.BlockSpec((block, wide), lambda b: (b, 0)),
            pl.BlockSpec((length, HD), lambda b: (0, 0)),
            pl.BlockSpec((block, LANES), lambda b: (b, 0)),
            pl.BlockSpec((block, 2), lambda b: (b, 0)),
            pl.BlockSpec((2, tokens), lambda b: (0, 0)),
        ],
        [pltpu.VMEM((tokens, 2 * wide), F32), pltpu.VMEM((8, wide + HD), F32)],
        grid=(steps,),
    )(qkv, qkv, grad_att, grad_last, attended, last, logs, rows_info, cols_info)


def on_device_paired(
    count,
    inputs,
    segment,
    cotangent,
    query_weight,
    key_weight,
    value_weight,
    out_weight,
    up_weight,
    down_weight,
    query_bias,
    value_bias,
    out_bias,
    up_bias,
    down_bias,
    first_gain,
    first_shift,
    second_gain,
    second_shift,
):
    me = lax.axis_index("shard")
    copy_index = lax.axis_index("dp")
    core = copy_index & 1
    near = (copy_index >> 1) & 1
    far = (copy_index >> 2) & 1
    others = range(1, count)
    order = me ^ jnp.arange(count, dtype=jnp.int32)
    slots = [me ^ k for k in range(count)]
    length = inputs.shape[1]
    model = inputs.shape[2]
    own = query_weight.shape[0]
    half = own // 2
    hidden = down_weight.shape[0]
    heads = HEADS // count
    wide = heads * HD
    full = 3 * (wide + HD)

    def send(value, k):
        return lax.ppermute(value, "shard", [(j, j ^ k) for j in range(count)])

    def cross(value, k):
        return lax.ppermute(value, "dp", [(j, j ^ k) for j in range(8)])

    def gather(value):
        return [value] + [send(value, k) for k in others]

    def pick(value, index):
        return lax.dynamic_index_in_dim(value, index, 0, False)

    def added(left, right):
        return (left.astype(F32) + right.astype(F32)).astype(BF16)

    def scatter_sum(partial_rows):
        total = partial_rows[0:length]
        for k in others:
            piece = partial_rows[k * length : (k + 1) * length].astype(BF16)
            total = total + send(piece, k).astype(F32)
        return total

    def rows_of_core(value, which):
        return lax.dynamic_slice_in_dim(value, which * half, half, axis=value.ndim - 2)

    def fetch(cuts, hold=None):
        got = [send(cuts[k], k) for k in others]
        if hold is not None:
            got = list(lax.optimization_barrier((*got, hold)))[:-1]
        swapped = [cross(g, 1) for g in got]
        pieces, places = [], []
        for k in others:
            pieces += [got[k - 1], swapped[k - 1]]
            places += [2 * slots[k] + core, 2 * slots[k] + 1 - core]
        pieces.append(cuts[0].reshape(2, half, -1))
        places += [2 * me, 2 * me + 1]
        return assemble(pieces, places, 2 * count)

    vectors = jnp.stack(
        [
            query_bias, value_bias, out_bias, down_bias,
            first_gain, first_shift, second_gain, second_shift,
        ]
    )
    input_pieces = gather(inputs[0])
    vector_pieces = gather(vectors)
    all_inputs = jnp.concatenate(input_pieces, axis=0)
    vectors = jnp.stack(vector_pieces)[order].transpose(1, 0, 2).reshape(8, model).astype(F32)

    squares = (query_weight, key_weight, value_weight)
    qkv_cols = fetch(cut_columns(squares, me, core, count, wide)).reshape(model, full)
    cot_pieces = gather(cotangent[0])
    all_cot = jnp.concatenate(cot_pieces, axis=0)

    pos = (order[:, None] * length + jnp.arange(length, dtype=jnp.int32)[None, :]).reshape(-1)
    seg = segment[0].reshape(count, length)[order].reshape(-1)
    rows_info = jnp.stack([seg, pos], axis=1)
    cols_info = jnp.stack([seg, pos], axis=0)

    head_slice = lambda v: lax.dynamic_slice_in_dim(v, me * wide, wide)
    tail = lambda v: v[count * wide :]
    qkv_bias = jnp.concatenate(
        [
            head_slice(vectors[0]), jnp.zeros((wide,), F32), head_slice(vectors[1]),
            tail(vectors[0]), jnp.zeros((HD,), F32), tail(vectors[1]),
        ]
    )

    first_gain_full, first_shift_full = vectors[4], vectors[5]
    second_gain_full, second_shift_full = vectors[6], vectors[7]
    all_hat, _ = normalise(all_inputs.astype(F32))
    first_in = (all_hat * first_gain_full + first_shift_full).astype(BF16)
    qkv = (matmul(first_in, qkv_cols) + qkv_bias).astype(BF16)
    out_half = rows_of_core(out_weight, core)
    full_out = fetch([out_weight] + [out_half] * 3, qkv).reshape(model, model)
    head_out = lax.dynamic_slice_in_dim(full_out, me * wide, wide, axis=0)
    last_out = full_out[count * wide :]
    attended, last, logs = split_forward(qkv, rows_info, cols_info, heads, length)
    att_pieces = [attended[0:length]] + [
        send(attended[k * length : (k + 1) * length], k) for k in others
    ]
    stacked_up = jnp.stack([up_weight[:, j * hidden : (j + 1) * hidden] for j in range(count)])
    up_halves = rows_of_core(stacked_up, core)
    up_cuts = [pick(stacked_up, me)] + [pick(up_halves, slots[k]) for k in others]
    up_cols = fetch(up_cuts, attended).reshape(model, hidden)
    own_attended = place_heads(att_pieces, last, slots, wide)
    residual_in = inputs[0].astype(F32)
    middle = residual_in + matmul(own_attended, full_out) + vectors[2]
    second_hat, second_inv = normalise(middle)
    own_second_in = (second_hat * second_gain_full + second_shift_full).astype(BF16)
    second_in = jnp.concatenate(gather(own_second_in), axis=0)
    pre_act = matmul(second_in, up_cols) + up_bias.astype(F32)
    below = 0.5 * (1.0 + lax.erf(pre_act * (0.5**0.5)))
    activated = (pre_act * below).astype(BF16)
    slope = below + pre_act * (jnp.exp(-0.5 * pre_act * pre_act) * 0.3989422804014327)
    grad_pre = contract_last(all_cot, down_weight) * slope
    grad_pre_low = grad_pre.astype(BF16)
    up_bias_part = jnp.sum(grad_pre, axis=0)
    grad_second = scatter_sum(contract_last(grad_pre_low, up_cols))

    def reduce_far(part, mode):
        keep = lax.dynamic_slice_in_dim(part, 2 * near, 2, axis=0)
        give = lax.dynamic_slice_in_dim(part, 2 - 2 * near, 2, axis=0)
        pair = added(keep, cross(give, 2))
        one = added(pick(pair, far), cross(pick(pair, 1 - far), 4))
        back = cross(one, 4)
        mine = [one, back, cross(one, 2), cross(back, 2)]
        theirs = [cross(v, 1) for v in mine]
        return unfold(mine, theirs, core, near, far, mode), pair

    down_part = contract_rows(activated, all_cot).astype(BF16)
    down_part = down_part.reshape(2, 4, hidden // 8, model)
    (down_sum,), _ = reduce_far(added(pick(down_part, core), cross(pick(down_part, 1 - core), 1)), "rows")
    down_weight_grad = down_sum.reshape(hidden, model)

    up_part = contract_rows(second_in, grad_pre_low).astype(BF16).reshape(count, own, hidden)
    up_part = added(rows_of_core(up_part, core), cross(rows_of_core(up_part, 1 - core), 1))
    up_pieces = [pick(up_part, me)] + [send(pick(up_part, slots[k]), k) for k in others]
    cot_float = cotangent[0].astype(F32)
    grad_middle = cot_float + norm_backward(
        grad_second, second_hat, second_inv, second_gain_full
    )
    grad_middle_low = grad_middle.astype(BF16)
    all_grad_middle = jnp.concatenate(gather(grad_middle_low), axis=0)
    grad_attended = contract_last(all_grad_middle, head_out).astype(BF16)
    grad_last = contract_last(grad_middle_low, last_out).astype(BF16)
    grad_qkv, head_sums = split_backward(
        qkv, grad_attended, grad_last, attended, last, logs, rows_info, cols_info, heads
    )
    up_pieces = list(lax.optimization_barrier((*up_pieces, head_sums)))[:-1]
    (up_weight_grad,), _ = reduce_far(assemble(up_pieces, slots, count), "columns")
    qkv_keep, qkv_give = grad_columns(first_in, grad_qkv, core, count)
    late_qkv, _ = lax.optimization_barrier((grad_qkv, qkv_give))
    grad_first = scatter_sum(contract_last(late_qkv, qkv_cols))
    first_hat, first_inv = normalise(residual_in)
    input_grad = grad_middle + norm_backward(grad_first, first_hat, first_inv, first_gain_full)

    features = jnp.stack([own_attended[:, j * own : (j + 1) * own] for j in range(count)])
    own_features = jnp.concatenate(
        [pick(features, me)] + [send(pick(features, slots[k]), k) for k in others], axis=0
    )
    out_part = contract_rows(own_features, all_grad_middle).astype(BF16)
    out_part = added(rows_of_core(out_part, core), cross(rows_of_core(out_part, 1 - core), 1))
    qkv_part = added(qkv_keep, cross(qkv_give, 1))
    qkv_pieces = [pick(qkv_part, me)] + [send(pick(qkv_part, slots[k]), k) for k in others]
    placed = place_grads(out_part, qkv_pieces, slots, wide)
    square, square_pair = reduce_far(placed, "arrays")
    late_activated, _ = lax.optimization_barrier((activated, square_pair))
    outputs = (middle + scatter_sum(matmul(late_activated, down_weight)) + vectors[3]).astype(BF16)

    def to_full(row):
        main = lax.dynamic_update_slice(
            jnp.zeros((count * wide,), F32), row[:wide], (me * wide,)
        )
        return jnp.concatenate([main, row[wide:]])

    partials = jnp.stack(
        [
            to_full(head_sums[0]),
            to_full(head_sums[1]),
            jnp.sum(grad_middle, axis=0),
            jnp.sum(cot_float, axis=0),
            jnp.sum(grad_first * first_hat, axis=0),
            jnp.sum(grad_first, axis=0),
            jnp.sum(grad_second * second_hat, axis=0),
            jnp.sum(grad_second, axis=0),
        ]
    )
    rows = partials.reshape(8, count, own).transpose(1, 0, 2)
    mine = pick(rows, me)
    for k in others:
        mine = mine + send(pick(rows, slots[k]), k)
    summed = jnp.concatenate([mine, up_bias_part.reshape(count, own)], axis=0)
    for k in (1, 2, 4):
        summed = summed + cross(summed, k)
    return (
        outputs[None],
        input_grad[None],
        square[1],
        square[2],
        square[3],
        square[0],
        up_weight_grad,
        down_weight_grad,
        summed[0],
        summed[1],
        summed[2],
        summed[8:].reshape(hidden),
        summed[3],
        summed[4],
        summed[5],
        summed[6],
        summed[7],
    )


def on_device(count, copies, *args):
    model = args[0].shape[2]
    heads = HEADS // count
    paired = (
        count == 4
        and copies == 8
        and HEADS == count * heads + 1
        and (heads * HD) % LANES == 0
        and model % (count * 16) == 0
        and args[0].shape[1] <= 256
        and args[8].shape[0] == model
    )
    if paired:
        return on_device_paired(count, *args)
    return on_device_general(count, *args)


def solution(mesh):
    tokens = P("dp", "shard", None)
    matrix = P("shard", None)
    vector = P("shard")
    return jax.shard_map(
        partial(on_device, mesh.shape["shard"], mesh.shape["dp"]),
        mesh=mesh,
        in_specs=(tokens, P("dp", None), tokens) + (matrix,) * 6 + (vector,) * 9,
        out_specs=(tokens, tokens) + (matrix,) * 6 + (vector,) * 9,
        check_vma=False,
    )
```

```python
from functools import partial

import jax
import jax.numpy as jnp
from jax import lax
from jax.experimental import pallas as pl
from jax.experimental.pallas import tpu as pltpu
from jax.sharding import PartitionSpec as P


HEADS = 17
HD = 64
EPSILON = 1e-05
SCORE_SCALE = 0.125
MASKED_SCORE = -1e30
LANES = 128
MANY = 4


BF16 = jnp.bfloat16
F32 = jnp.float32


def normalise(values):
    average = jnp.mean(values, axis=-1, keepdims=True)
    centred = values - average
    variance = jnp.mean(centred * centred, axis=-1, keepdims=True)
    inv_std = lax.rsqrt(variance + EPSILON)
    return centred * inv_std, inv_std


def norm_backward(grad_normed, normed, inv_std, gain_vec):
    scaled = grad_normed * gain_vec
    first_mean = jnp.mean(scaled, axis=-1, keepdims=True)
    second_mean = jnp.mean(scaled * normed, axis=-1, keepdims=True)
    return inv_std * (scaled - first_mean - normed * second_mean)


def matmul(left_side, right_side):
    return jnp.dot(left_side, right_side, preferred_element_type=F32)


def contract_rows(left_side, right_side):
    return lax.dot_general(
        left_side, right_side, (((0,), (0,)), ((), ())), preferred_element_type=F32
    )


def contract_last(left_side, right_side):
    return lax.dot_general(
        left_side, right_side, (((1,), (1,)), ((), ())), preferred_element_type=F32
    )


def mask_bias(row_seg, row_pos, col_seg, col_pos):
    allowed = (row_seg == col_seg) & (col_pos <= row_pos)
    return jnp.where(allowed, 0.0, MASKED_SCORE)


def attention_forward(qkv, rows_info, cols_info, heads):
    tokens = qkv.shape[0]
    width = heads * HD
    block = min(256, tokens)

    def kernel(q_ref, kv_ref, rows_ref, cols_ref, out_ref, log_ref):
        bias = mask_bias(
            rows_ref[:, 0:1], rows_ref[:, 1:2], cols_ref[0:1, :], cols_ref[1:2, :]
        )
        lane = lax.broadcasted_iota(jnp.int32, (block, LANES), 1)
        logs = jnp.zeros((block, LANES), F32)
        for h in range(heads):
            query = q_ref[:, h * HD : (h + 1) * HD]
            keys = kv_ref[:, width + h * HD : width + (h + 1) * HD]
            vals = kv_ref[:, 2 * width + h * HD : 2 * width + (h + 1) * HD]
            scores = contract_last(query, keys) * SCORE_SCALE + bias
            largest = jnp.max(scores, axis=1, keepdims=True)
            grown = jnp.exp(scores - largest)
            total = jnp.sum(grown, axis=1, keepdims=True)
            probs = (grown * (1.0 / total)).astype(BF16)
            out_ref[:, h * HD : (h + 1) * HD] = matmul(probs, vals).astype(BF16)
            logs = jnp.where(lane == h, largest + jnp.log(total), logs)
        log_ref[...] = logs

    return pl.pallas_call(
        kernel,
        grid=(tokens // block,),
        in_specs=[
            pl.BlockSpec((block, 3 * width), lambda b: (b, 0)),
            pl.BlockSpec((tokens, 3 * width), lambda b: (0, 0)),
            pl.BlockSpec((block, 2), lambda b: (b, 0)),
            pl.BlockSpec((2, tokens), lambda b: (0, 0)),
        ],
        out_specs=[
            pl.BlockSpec((block, width), lambda b: (b, 0)),
            pl.BlockSpec((block, LANES), lambda b: (b, 0)),
        ],
        out_shape=[
            jax.ShapeDtypeStruct((tokens, width), BF16),
            jax.ShapeDtypeStruct((tokens, LANES), F32),
        ],
        name="attention_forward",
    )(qkv, qkv, rows_info, cols_info)


def attention_backward(qkv, grad_att, attended, logs, rows_info, cols_info, heads):
    tokens = qkv.shape[0]
    width = heads * HD
    block = min(256, tokens)
    steps = tokens // block

    def kernel(
        q_ref, kv_ref, grad_ref, att_ref, log_ref, rows_ref, cols_ref,
        gq_ref, gkv_ref, sums_ref, acc_ref, bias_ref,
    ):
        step = pl.program_id(0)

        @pl.when(step == 0)
        def _():
            acc_ref[...] = jnp.zeros_like(acc_ref)
            bias_ref[...] = jnp.zeros_like(bias_ref)

        bias = mask_bias(
            rows_ref[:, 0:1], rows_ref[:, 1:2], cols_ref[0:1, :], cols_ref[1:2, :]
        )
        for h in range(heads):
            own = slice(h * HD, (h + 1) * HD)
            query = q_ref[:, own]
            keys = kv_ref[:, width + h * HD : width + (h + 1) * HD]
            vals = kv_ref[:, 2 * width + h * HD : 2 * width + (h + 1) * HD]
            grad = grad_ref[:, own]
            delta = jnp.sum(
                grad.astype(F32) * att_ref[:, own].astype(F32), axis=1, keepdims=True
            )
            scores = contract_last(query, keys) * SCORE_SCALE + bias
            exact = jnp.exp(scores - log_ref[:, h : h + 1])
            grad_probs = contract_last(grad, vals)
            grad_scores = (exact * (grad_probs - delta) * SCORE_SCALE).astype(BF16)
            grad_query = matmul(grad_scores, keys)
            gq_ref[:, own] = grad_query.astype(BF16)
            bias_ref[0:1, own] += jnp.sum(grad_query, axis=0, keepdims=True)
            acc_ref[:, own] += contract_rows(grad_scores, query)
            acc_ref[:, width + h * HD : width + (h + 1) * HD] += contract_rows(
                exact.astype(BF16), grad
            )

        @pl.when(step == steps - 1)
        def _():
            gkv_ref[...] = acc_ref[...].astype(BF16)
            bias_ref[1:2, :] = jnp.sum(acc_ref[:, width:], axis=0, keepdims=True)
            sums_ref[...] = bias_ref[...]

    return pl.pallas_call(
        kernel,
        grid=(steps,),
        in_specs=[
            pl.BlockSpec((block, 3 * width), lambda b: (b, 0)),
            pl.BlockSpec((tokens, 3 * width), lambda b: (0, 0)),
            pl.BlockSpec((block, width), lambda b: (b, 0)),
            pl.BlockSpec((block, width), lambda b: (b, 0)),
            pl.BlockSpec((block, LANES), lambda b: (b, 0)),
            pl.BlockSpec((block, 2), lambda b: (b, 0)),
            pl.BlockSpec((2, tokens), lambda b: (0, 0)),
        ],
        out_specs=[
            pl.BlockSpec((block, width), lambda b: (b, 0)),
            pl.BlockSpec((tokens, 2 * width), lambda b: (0, 0)),
            pl.BlockSpec((8, width), lambda b: (0, 0)),
        ],
        out_shape=[
            jax.ShapeDtypeStruct((tokens, width), BF16),
            jax.ShapeDtypeStruct((tokens, 2 * width), BF16),
            jax.ShapeDtypeStruct((8, width), F32),
        ],
        scratch_shapes=[
            pltpu.VMEM((tokens, 2 * width), F32),
            pltpu.VMEM((8, width), F32),
        ],
        name="attention_backward",
    )(qkv, qkv, grad_att, attended, logs, rows_info, cols_info)


def on_device_general(
    count,
    inputs,
    segment,
    cotangent,
    query_weight,
    key_weight,
    value_weight,
    out_weight,
    up_weight,
    down_weight,
    query_bias,
    value_bias,
    out_bias,
    up_bias,
    down_bias,
    first_gain,
    first_shift,
    second_gain,
    second_shift,
):
    me = lax.axis_index("shard")
    others = range(1, count)
    order = me ^ jnp.arange(count, dtype=jnp.int32)
    length = inputs.shape[1]
    model = inputs.shape[2]
    own = query_weight.shape[0]
    hidden = down_weight.shape[0]
    per = -(-HEADS // count)
    width = per * HD
    padded = count * width

    def send(value, k):
        return lax.ppermute(value, "shard", [(j, j ^ k) for j in range(count)])

    def gather(value):
        if count > MANY:
            whole = lax.all_gather(value, "shard")
            return [lax.dynamic_index_in_dim(whole, me ^ k, 0, False) for k in range(count)]
        return [value] + [send(value, k) for k in others]

    def swap(pieces):
        if count > MANY:
            whole = jnp.stack(pieces)[order]
            whole = lax.all_to_all(whole, "shard", split_axis=0, concat_axis=0)[order]
            return [whole[k] for k in range(count)]
        return [pieces[0]] + [send(pieces[k], k) for k in others]

    def scatter_sum(partial_rows):
        blocks = [partial_rows[k * length : (k + 1) * length] for k in range(count)]
        got = swap([b.astype(BF16) for b in blocks])
        return sum((v.astype(F32) for v in got[1:]), blocks[0])

    def in_order(pieces):
        rows = pieces[0].shape[0]
        whole = jnp.zeros((count * rows,) + pieces[0].shape[1:], pieces[0].dtype)
        for k in range(count):
            start = ((me ^ k) * rows,) + (0,) * (pieces[0].ndim - 1)
            whole = lax.dynamic_update_slice(whole, pieces[k], start)
        return whole

    def exchange(stacked):
        return swap(
            [lax.dynamic_index_in_dim(stacked, me ^ k, 0, False) for k in range(count)]
        )

    vectors = jnp.stack(
        [
            query_bias, value_bias, out_bias, down_bias,
            first_gain, first_shift, second_gain, second_shift,
        ]
    )
    vectors = in_order([v[None] for v in gather(vectors)])
    vectors = vectors.transpose(1, 0, 2).reshape(8, model).astype(F32)
    all_inputs = jnp.concatenate(gather(inputs[0]), axis=0)
    pad_cols = lambda w: jnp.pad(w, ((0, 0), (0, padded - model)))
    stacked_qkv = jnp.concatenate(
        [
            pad_cols(w).reshape(own, count, width)
            for w in (query_weight, key_weight, value_weight)
        ],
        axis=2,
    ).transpose(1, 0, 2)
    qkv_cols = in_order(exchange(stacked_qkv))
    all_cot = jnp.concatenate(gather(cotangent[0]), axis=0)
    full_out = jnp.pad(in_order(gather(out_weight)), ((0, padded - model), (0, 0)))
    head_out = lax.dynamic_slice_in_dim(full_out, me * width, width, axis=0)
    mixed_out = full_out.reshape(count, width, model)[order].reshape(padded, model)
    up_cols = in_order(exchange(up_weight.reshape(own, count, hidden).transpose(1, 0, 2)))

    pos = (order[:, None] * length + jnp.arange(length, dtype=jnp.int32)[None, :]).reshape(-1)
    seg = segment[0].reshape(count, length)[order].reshape(-1)
    rows_info = jnp.stack([seg, pos], axis=1)
    cols_info = jnp.stack([seg, pos], axis=0)

    head_slice = lambda v: lax.dynamic_slice_in_dim(
        jnp.pad(v, (0, padded - model)), me * width, width
    )
    qkv_bias = jnp.concatenate(
        [head_slice(vectors[0]), jnp.zeros((width,), F32), head_slice(vectors[1])]
    )

    first_gain_full, first_shift_full = vectors[4], vectors[5]
    second_gain_full, second_shift_full = vectors[6], vectors[7]
    all_hat, _ = normalise(all_inputs.astype(F32))
    first_in = (all_hat * first_gain_full + first_shift_full).astype(BF16)
    qkv = (matmul(first_in, qkv_cols) + qkv_bias).astype(BF16)
    attended, logs = attention_forward(qkv, rows_info, cols_info, per)
    att_pieces = swap([attended[k * length : (k + 1) * length] for k in range(count)])
    residual_in = inputs[0].astype(F32)
    own_attended = jnp.concatenate(att_pieces, axis=1)
    middle = residual_in + matmul(own_attended, mixed_out) + vectors[2]
    second_hat, second_inv = normalise(middle)
    own_second_in = (second_hat * second_gain_full + second_shift_full).astype(BF16)
    second_in = jnp.concatenate(gather(own_second_in), axis=0)
    pre_act = matmul(second_in, up_cols) + up_bias.astype(F32)
    below = 0.5 * (1.0 + lax.erf(pre_act * (0.5**0.5)))
    activated = (pre_act * below).astype(BF16)
    slope = below + pre_act * (jnp.exp(-0.5 * pre_act * pre_act) * 0.3989422804014327)
    grad_pre = contract_last(all_cot, down_weight) * slope
    grad_pre_low = grad_pre.astype(BF16)
    up_bias_part = jnp.sum(grad_pre, axis=0)
    grad_second = scatter_sum(contract_last(grad_pre_low, up_cols))
    outputs = (
        middle + scatter_sum(matmul(activated, down_weight)) + vectors[3]
    ).astype(BF16)

    down_part = contract_rows(activated, all_cot).astype(BF16)
    up_part = contract_rows(second_in, grad_pre_low).astype(BF16)
    up_rows = exchange(up_part.reshape(count, own, hidden))

    def reduce_dp(part, dim):
        share = lax.psum_scatter(part, "dp", scatter_dimension=dim, tiled=True)
        return lax.all_gather(share, "dp", axis=dim, tiled=True).astype(F32)

    down_weight_grad = reduce_dp(down_part, 0)
    up_rows = in_order([v[None] for v in up_rows])
    up_total = reduce_dp(up_rows.reshape(count * own, hidden), 0)
    up_weight_grad = (
        up_total.reshape(count, own, hidden).transpose(1, 0, 2).reshape(own, count * hidden)
    )

    grad_middle = cotangent[0].astype(F32) + norm_backward(
        grad_second, second_hat, second_inv, second_gain_full
    )
    grad_middle_low = grad_middle.astype(BF16)
    all_grad_middle = jnp.concatenate(gather(grad_middle_low), axis=0)
    grad_attended = contract_last(all_grad_middle, head_out).astype(BF16)
    grad_queries, grad_kv, head_sums = attention_backward(
        qkv, grad_attended, attended, logs, rows_info, cols_info, per
    )
    grad_qkv = jnp.concatenate([grad_queries, grad_kv], axis=1)
    grad_first = scatter_sum(contract_last(grad_qkv, qkv_cols))
    first_hat, first_inv = normalise(residual_in)
    input_grad = grad_middle + norm_backward(grad_first, first_hat, first_inv, first_gain_full)

    true_attended = in_order([v[None] for v in att_pieces])
    true_attended = true_attended.transpose(1, 0, 2).reshape(length, padded)[:, :model]
    own_features = jnp.concatenate(
        exchange(true_attended.reshape(length, count, own).transpose(1, 0, 2)), axis=0
    )
    out_part = contract_rows(own_features, all_grad_middle).astype(BF16)
    qkv_part = contract_rows(first_in, grad_qkv).astype(BF16)
    qkv_rows = exchange(qkv_part.reshape(count, own, 3 * width))
    qkv_rows = in_order([v[None] for v in qkv_rows]).reshape(count, own, 3, width)
    qkv_rows = qkv_rows.transpose(2, 1, 0, 3).reshape(3, own, padded)[:, :, :model]
    square = reduce_dp(jnp.concatenate([out_part[None], qkv_rows]).reshape(4 * own, model), 0)
    square = square.reshape(4, own, model)

    to_full = lambda v: lax.dynamic_update_slice(
        jnp.zeros((padded,), F32), v, (me * width,)
    )[:model]
    partials = jnp.stack(
        [
            to_full(head_sums[0]),
            to_full(head_sums[1]),
            jnp.sum(grad_middle, axis=0),
            jnp.sum(cotangent[0].astype(F32), axis=0),
            jnp.sum(grad_first * first_hat, axis=0),
            jnp.sum(grad_first, axis=0),
            jnp.sum(grad_second * second_hat, axis=0),
            jnp.sum(grad_second, axis=0),
        ]
    )
    vector_rows = sum(exchange(partials.reshape(8, count, own).transpose(1, 0, 2)))
    summed, up_bias_grad = lax.psum((vector_rows, up_bias_part), "dp")
    return (
        outputs[None],
        input_grad[None],
        square[1],
        square[2],
        square[3],
        square[0],
        up_weight_grad,
        down_weight_grad,
        summed[0],
        summed[1],
        summed[2],
        up_bias_grad,
        summed[3],
        summed[4],
        summed[5],
        summed[6],
        summed[7],
    )


def call(kernel, out_shape, out_specs, in_specs, scratch=(), grid=()):
    return pl.pallas_call(
        kernel,
        grid=grid,
        in_specs=in_specs,
        out_specs=out_specs,
        out_shape=out_shape,
        scratch_shapes=scratch,
    )


def assemble(pieces, slots, total):
    amount = len(pieces)
    shape = pieces[0].shape[-2:]

    def kernel(slot_ref, *refs):
        out_ref = refs[amount]
        at = 0
        for ref in refs[:amount]:
            parts = [ref[...]] if len(ref.shape) == 2 else [ref[k] for k in range(ref.shape[0])]
            for part in parts:
                out_ref[slot_ref[at]] = part
                at += 1

    return call(
        kernel,
        jax.ShapeDtypeStruct((total,) + shape, pieces[0].dtype),
        pl.BlockSpec(memory_space=pltpu.VMEM),
        [pl.BlockSpec(memory_space=pltpu.SMEM)]
        + [pl.BlockSpec(memory_space=pltpu.VMEM)] * amount,
    )(jnp.stack(slots).astype(jnp.int32), *pieces)


def grad_columns(first_in, grad_qkv, core, count):
    model = first_in.shape[1]
    full = grad_qkv.shape[1]
    own = model // count
    half = own // 2

    def kernel(core_ref, in_ref, grad_ref, keep_ref, give_ref, acc_ref):
        acc_ref[...] = contract_rows(in_ref[...], grad_ref[...])
        for j in range(count):
            for side, ref in enumerate((keep_ref, give_ref)):
                which = core_ref[0] if side == 0 else 1 - core_ref[0]
                start = pl.multiple_of(j * own + which * half, 8)
                ref[j] = acc_ref[pl.ds(start, half), :].astype(BF16)

    return call(
        kernel,
        [jax.ShapeDtypeStruct((count, half, full), BF16)] * 2,
        [pl.BlockSpec(memory_space=pltpu.VMEM)] * 2,
        [pl.BlockSpec(memory_space=pltpu.SMEM)] + [pl.BlockSpec(memory_space=pltpu.VMEM)] * 2,
        [pltpu.VMEM((model, full), F32)],
    )(core[None].astype(jnp.int32), first_in, grad_qkv)


def unfold(mine, theirs, core, near, far, mode):
    blocks = len(mine)
    half, model = mine[0].shape
    shapes = {
        "rows": [(2 * blocks, half, model)],
        "columns": [(2 * half, blocks * model)],
        "arrays": [(2 * half, model)] * blocks,
    }[mode]

    def kernel(bits_ref, *refs):
        out_refs = refs[2 * blocks :]
        mask = bits_ref[1] * 2 + bits_ref[2]
        for side in range(2):
            where = bits_ref[0] if side == 0 else 1 - bits_ref[0]
            rows = pl.ds(pl.multiple_of(where * half, 8), half)
            values = [refs[side * blocks + k][...] for k in range(blocks)]
            for slot in range(blocks):
                if mode == "rows":
                    out_refs[0][where * blocks + (slot ^ mask)] = values[slot].astype(F32)
                    continue
                block = values[slot]
                for k in range(1, blocks):
                    block = jnp.where(mask == k, values[slot ^ k], block)
                if mode == "columns":
                    out_refs[0][rows, slot * model : (slot + 1) * model] = block.astype(F32)
                else:
                    out_refs[slot][rows, :] = block.astype(F32)

    return call(
        kernel,
        [jax.ShapeDtypeStruct(shape, F32) for shape in shapes],
        [pl.BlockSpec(memory_space=pltpu.VMEM)] * len(shapes),
        [pl.BlockSpec(memory_space=pltpu.SMEM)]
        + [pl.BlockSpec(memory_space=pltpu.VMEM)] * (2 * blocks),
    )(jnp.stack([core, near, far]).astype(jnp.int32), *mine, *theirs)


def cut_columns(weights, me, core, count, wide):
    rows, _ = weights[0].shape
    half = rows // 2
    full = 3 * (wide + HD)

    def kernel(place_ref, *refs):
        outs = refs[3:]
        for k in range(count):
            start = pl.multiple_of((place_ref[0] ^ k) * wide, LANES)
            for m in range(3):
                main = refs[m][:, pl.ds(start, wide)]
                extra = refs[m][:, count * wide :]
                if k > 0:
                    main = jnp.where(place_ref[1] == 0, main[:half], main[half:])
                    extra = jnp.where(place_ref[1] == 0, extra[:half], extra[half:])
                outs[k][:, m * wide : (m + 1) * wide] = main
                outs[k][:, 3 * wide + m * HD : 3 * wide + (m + 1) * HD] = extra

    return call(
        kernel,
        [
            jax.ShapeDtypeStruct((rows if k == 0 else half, full), BF16)
            for k in range(count)
        ],
        [pl.BlockSpec(memory_space=pltpu.VMEM)] * count,
        [pl.BlockSpec(memory_space=pltpu.SMEM)] + [pl.BlockSpec(memory_space=pltpu.VMEM)] * 3,
    )(jnp.stack([me, core]).astype(jnp.int32), *weights)


def mid_forward(pieces, last, slots, wide, full_out, residual, rows):
    amount = len(pieces)
    length = pieces[0].shape[0]
    model = full_out.shape[0]

    def kernel(slot_ref, *refs):
        last_ref, weight_ref, res_ref, row_ref = refs[amount : amount + 4]
        att_ref, mid_ref, hat_ref, inv_ref, low_ref = refs[amount + 4 :]
        for k in range(amount):
            start = pl.multiple_of(slot_ref[k] * wide, LANES)
            att_ref[:, pl.ds(start, wide)] = refs[k][...]
        att_ref[:, amount * wide :] = last_ref[...]
        middle = res_ref[...].astype(F32) + matmul(att_ref[...], weight_ref[...]) + row_ref[0:1]
        mid_ref[...] = middle
        hat, inv_std = normalise(middle)
        hat_ref[...] = hat
        inv_ref[...] = jnp.broadcast_to(inv_std, (length, LANES))
        low_ref[...] = (hat * row_ref[1:2] + row_ref[2:3]).astype(BF16)

    shape = lambda width, kind: jax.ShapeDtypeStruct((length, width), kind)
    return call(
        kernel,
        [shape(model, BF16), shape(model, F32), shape(model, F32), shape(LANES, F32),
         shape(model, BF16)],
        [pl.BlockSpec(memory_space=pltpu.VMEM)] * 5,
        [pl.BlockSpec(memory_space=pltpu.SMEM)]
        + [pl.BlockSpec(memory_space=pltpu.VMEM)] * (amount + 4),
    )(jnp.stack(slots).astype(jnp.int32), *pieces, last, full_out, residual, rows)


def mid_backward(whole, pieces, hat, inv_std, cot, gain):
    length, model = hat.shape
    amount = len(pieces)

    def kernel(whole_ref, *refs):
        hat_ref, inv_ref, cot_ref, gain_ref = refs[amount : amount + 4]
        grad_ref, low_ref, sums_ref = refs[amount + 4 :]
        grad = whole_ref[...]
        for ref in refs[:amount]:
            grad = grad + ref[...].astype(F32)
        normed = hat_ref[...]
        cot_float = cot_ref[...].astype(F32)
        grad_mid = cot_float + norm_backward(grad, normed, inv_ref[:, 0:1], gain_ref[...])
        grad_ref[...] = grad_mid
        low_ref[...] = grad_mid.astype(BF16)
        total = lambda v: jnp.sum(v, axis=0, keepdims=True)
        sums_ref[0:1] = total(grad_mid)
        sums_ref[1:2] = total(cot_float)
        sums_ref[2:3] = total(grad * normed)
        sums_ref[3:4] = total(grad)
        sums_ref[4:8] = jnp.zeros((4, model), F32)

    flat = lambda rows, width: pl.BlockSpec((rows, width), lambda b: (0, 0))
    return call(
        kernel,
        [
            jax.ShapeDtypeStruct((length, model), F32),
            jax.ShapeDtypeStruct((length, model), BF16),
            jax.ShapeDtypeStruct((8, model), F32),
        ],
        [flat(length, model), flat(length, model), flat(8, model)],
        [flat(length, model)] * (amount + 2)
        + [flat(length, LANES), flat(length, model), flat(1, model)],
        grid=(1,),
    )(whole, *pieces, hat, inv_std, cot, gain[None])


def place_grads(out_part, pieces, slots, wide):
    amount = len(pieces)
    rows, model = out_part.shape

    def kernel(slot_ref, *refs):
        out_ref = refs[amount + 1]
        out_ref[0] = refs[0][...]
        for m in range(3):
            extra = slice(3 * wide + m * HD, 3 * wide + (m + 1) * HD)
            shared = refs[1][:, extra].astype(F32)
            for k in range(amount):
                start = pl.multiple_of(slot_ref[k] * wide, LANES)
                out_ref[1 + m, :, pl.ds(start, wide)] = refs[1 + k][:, m * wide : (m + 1) * wide]
                if k > 0:
                    shared = shared + refs[1 + k][:, extra].astype(F32)
            out_ref[1 + m, :, amount * wide :] = shared.astype(BF16)

    return call(
        kernel,
        jax.ShapeDtypeStruct((4, rows, model), BF16),
        pl.BlockSpec(memory_space=pltpu.VMEM),
        [pl.BlockSpec(memory_space=pltpu.SMEM)]
        + [pl.BlockSpec(memory_space=pltpu.VMEM)] * (amount + 1),
    )(jnp.stack(slots).astype(jnp.int32), out_part, *pieces)


def split_forward(qkv, rows_info, cols_info, heads, length):
    tokens = qkv.shape[0]
    wide = heads * HD
    block = min(256, tokens)
    full = qkv.shape[1]

    count = tokens // length
    piece = jax.ShapeDtypeStruct((length, wide), BF16)

    def kernel(q_ref, kv_ref, rows_ref, cols_ref, out_ref, last_ref, log_ref, *piece_refs):
        bias = mask_bias(
            rows_ref[:, 0:1], rows_ref[:, 1:2], cols_ref[0:1, :], cols_ref[1:2, :]
        )
        lane = lax.broadcasted_iota(jnp.int32, (block, LANES), 1)

        def head(query, keys, vals, seen):
            scores = contract_last(query, keys) * SCORE_SCALE + seen
            largest = jnp.max(scores, axis=1, keepdims=True)
            grown = jnp.exp(scores - largest)
            total = jnp.sum(grown, axis=1, keepdims=True)
            probs = (grown * (1.0 / total)).astype(BF16)
            return matmul(probs, vals).astype(BF16), largest + jnp.log(total)

        logs = jnp.zeros((block, LANES), F32)
        for h in range(heads):
            own = slice(h * HD, (h + 1) * HD)
            got, log = head(
                q_ref[:, own],
                kv_ref[:, wide + h * HD : wide + (h + 1) * HD],
                kv_ref[:, 2 * wide + h * HD : 2 * wide + (h + 1) * HD],
                bias,
            )
            out_ref[:, own] = got
            logs = jnp.where(lane == h, log, logs)
        log_ref[...] = logs

        @pl.when(pl.program_id(0) == 0)
        def _():
            base = 3 * wide
            got, log = head(
                q_ref[0:length, base : base + HD],
                kv_ref[:, base + HD : base + 2 * HD],
                kv_ref[:, base + 2 * HD : base + 3 * HD],
                bias[0:length],
            )
            last_ref[...] = got
            log_ref[0:length, :] = jnp.where(lane[0:length] == heads, log, logs[0:length])

        for k in range(1, count):
            at = k * length

            @pl.when(pl.program_id(0) == at // block)
            def _():
                piece_refs[k - 1][...] = out_ref[at % block : at % block + length, :]

    return call(
        kernel,
        [
            jax.ShapeDtypeStruct((tokens, wide), BF16),
            jax.ShapeDtypeStruct((length, HD), BF16),
            jax.ShapeDtypeStruct((tokens, LANES), F32),
        ]
        + [piece] * (count - 1),
        [
            pl.BlockSpec((block, wide), lambda b: (b, 0)),
            pl.BlockSpec((length, HD), lambda b: (0, 0)),
            pl.BlockSpec((block, LANES), lambda b: (b, 0)),
        ]
        + [pl.BlockSpec((length, wide), lambda b: (0, 0))] * (count - 1),
        [
            pl.BlockSpec((block, full), lambda b: (b, 0)),
            pl.BlockSpec((tokens, full), lambda b: (0, 0)),
            pl.BlockSpec((block, 2), lambda b: (b, 0)),
            pl.BlockSpec((2, tokens), lambda b: (0, 0)),
        ],
        grid=(tokens // block,),
    )(qkv, qkv, rows_info, cols_info)


def att_grads(pieces, head_out, last_out):
    amount = len(pieces)
    length, model = pieces[0].shape
    wide = head_out.shape[0]

    def kernel(*refs):
        head_ref, last_ref = refs[amount : amount + 2]
        all_ref, grad_ref, glast_ref = refs[amount + 2 :]
        for k in range(amount):
            rows = slice(k * length, (k + 1) * length)
            all_ref[rows, :] = refs[k][...]
        grad_ref[...] = contract_last(all_ref[...], head_ref[...]).astype(BF16)
        glast_ref[...] = contract_last(refs[0][...], last_ref[...]).astype(BF16)

    return call(
        kernel,
        [
            jax.ShapeDtypeStruct((amount * length, model), BF16),
            jax.ShapeDtypeStruct((amount * length, wide), BF16),
            jax.ShapeDtypeStruct((length, HD), BF16),
        ],
        [pl.BlockSpec(memory_space=pltpu.VMEM)] * 3,
        [pl.BlockSpec(memory_space=pltpu.VMEM)] * (amount + 2),
    )(*pieces, head_out, last_out)


def split_backward(qkv, grad_att, grad_last, attended, last, logs, rows_info, cols_info, heads):
    tokens, full = qkv.shape
    length = last.shape[0]
    wide = heads * HD
    block = min(256, tokens)
    steps = tokens // block
    base = 3 * wide

    def kernel(
        q_ref, kv_ref, grad_ref, glast_ref, att_ref, last_ref, log_ref, rows_ref, cols_ref,
        out_ref, sums_ref, acc_ref, bias_ref,
    ):
        step = pl.program_id(0)
        start = pl.multiple_of(step * block, block)

        @pl.when(step == 0)
        def _():
            acc_ref[...] = jnp.zeros_like(acc_ref)
            bias_ref[...] = jnp.zeros_like(bias_ref)
            out_ref[:, base : base + HD] = jnp.zeros((tokens, HD), BF16)

        seen = mask_bias(
            rows_ref[:, 0:1], rows_ref[:, 1:2], cols_ref[0:1, :], cols_ref[1:2, :]
        )

        def head(query, keys, vals, grad, got, log, bias):
            delta = jnp.sum(grad.astype(F32) * got.astype(F32), axis=1, keepdims=True)
            scores = contract_last(query, keys) * SCORE_SCALE + bias
            exact = jnp.exp(scores - log)
            grad_probs = contract_last(grad, vals)
            grad_scores = (exact * (grad_probs - delta) * SCORE_SCALE).astype(BF16)
            return (
                matmul(grad_scores, keys),
                contract_rows(grad_scores, query),
                contract_rows(exact.astype(BF16), grad),
            )

        for h in range(heads):
            own = slice(h * HD, (h + 1) * HD)
            keys_at = slice(wide + h * HD, wide + (h + 1) * HD)
            vals_at = slice(2 * wide + h * HD, 2 * wide + (h + 1) * HD)
            grad_query, grad_key, grad_value = head(
                q_ref[:, own], kv_ref[:, keys_at], kv_ref[:, vals_at],
                grad_ref[:, own], att_ref[:, own], log_ref[:, h : h + 1], seen,
            )
            out_ref[pl.ds(start, block), own] = grad_query.astype(BF16)
            bias_ref[0:1, own] += jnp.sum(grad_query, axis=0, keepdims=True)
            acc_ref[:, own] += grad_key
            acc_ref[:, keys_at] += grad_value

        @pl.when(step == 0)
        def _():
            grad_query, grad_key, grad_value = head(
                q_ref[0:length, base : base + HD],
                kv_ref[:, base + HD : base + 2 * HD],
                kv_ref[:, base + 2 * HD : base + 3 * HD],
                glast_ref[...], last_ref[...], log_ref[0:length, heads : heads + 1],
                seen[0:length],
            )
            out_ref[0:length, base : base + HD] = grad_query.astype(BF16)
            out_ref[:, base + HD : base + 2 * HD] = grad_key.astype(BF16)
            out_ref[:, base + 2 * HD : base + 3 * HD] = grad_value.astype(BF16)
            bias_ref[0:1, wide : wide + HD] = jnp.sum(grad_query, axis=0, keepdims=True)
            bias_ref[1:2, wide : wide + HD] = jnp.sum(grad_value, axis=0, keepdims=True)

        @pl.when(step == steps - 1)
        def _():
            out_ref[:, wide:base] = acc_ref[...].astype(BF16)
            bias_ref[1:2, 0:wide] = jnp.sum(acc_ref[:, wide:], axis=0, keepdims=True)
            sums_ref[...] = bias_ref[...]

    return call(
        kernel,
        [
            jax.ShapeDtypeStruct((tokens, full), BF16),
            jax.ShapeDtypeStruct((8, wide + HD), F32),
        ],
        [
            pl.BlockSpec((tokens, full), lambda b: (0, 0)),
            pl.BlockSpec((8, wide + HD), lambda b: (0, 0)),
        ],
        [
            pl.BlockSpec((block, full), lambda b: (b, 0)),
            pl.BlockSpec((tokens, full), lambda b: (0, 0)),
            pl.BlockSpec((block, wide), lambda b: (b, 0)),
            pl.BlockSpec((length, HD), lambda b: (0, 0)),
            pl.BlockSpec((block, wide), lambda b: (b, 0)),
            pl.BlockSpec((length, HD), lambda b: (0, 0)),
            pl.BlockSpec((block, LANES), lambda b: (b, 0)),
            pl.BlockSpec((block, 2), lambda b: (b, 0)),
            pl.BlockSpec((2, tokens), lambda b: (0, 0)),
        ],
        [pltpu.VMEM((tokens, 2 * wide), F32), pltpu.VMEM((8, wide + HD), F32)],
        grid=(steps,),
    )(qkv, qkv, grad_att, grad_last, attended, last, logs, rows_info, cols_info)


def on_device_paired(
    count,
    inputs,
    segment,
    cotangent,
    query_weight,
    key_weight,
    value_weight,
    out_weight,
    up_weight,
    down_weight,
    query_bias,
    value_bias,
    out_bias,
    up_bias,
    down_bias,
    first_gain,
    first_shift,
    second_gain,
    second_shift,
):
    me = lax.axis_index("shard")
    copy_index = lax.axis_index("dp")
    core = copy_index & 1
    near = (copy_index >> 1) & 1
    far = (copy_index >> 2) & 1
    others = range(1, count)
    order = me ^ jnp.arange(count, dtype=jnp.int32)
    slots = [me ^ k for k in range(count)]
    length = inputs.shape[1]
    model = inputs.shape[2]
    own = query_weight.shape[0]
    half = own // 2
    hidden = down_weight.shape[0]
    heads = HEADS // count
    wide = heads * HD
    full = 3 * (wide + HD)

    def send(value, k):
        return lax.ppermute(value, "shard", [(j, j ^ k) for j in range(count)])

    def cross(value, k):
        return lax.ppermute(value, "dp", [(j, j ^ k) for j in range(8)])

    def gather(value):
        return [value] + [send(value, k) for k in others]

    def pick(value, index):
        return lax.dynamic_index_in_dim(value, index, 0, False)

    def added(left, right):
        return (left.astype(F32) + right.astype(F32)).astype(BF16)

    def scatter_sum(partial_rows):
        total = partial_rows[0:length]
        for k in others:
            piece = partial_rows[k * length : (k + 1) * length].astype(BF16)
            total = total + send(piece, k).astype(F32)
        return total

    def rows_of_core(value, which):
        return lax.dynamic_slice_in_dim(value, which * half, half, axis=value.ndim - 2)

    def fetch(cuts, hold=None):
        got = [send(cuts[k], k) for k in others]
        if hold is not None:
            got = list(lax.optimization_barrier((*got, hold)))[:-1]
        swapped = [cross(g, 1) for g in got]
        pieces, places = [], []
        for k in others:
            pieces += [got[k - 1], swapped[k - 1]]
            places += [2 * slots[k] + core, 2 * slots[k] + 1 - core]
        pieces.append(cuts[0].reshape(2, half, -1))
        places += [2 * me, 2 * me + 1]
        return assemble(pieces, places, 2 * count)

    vectors = jnp.stack(
        [
            query_bias, value_bias, out_bias, down_bias,
            first_gain, first_shift, second_gain, second_shift,
        ]
    )
    input_pieces = gather(inputs[0])
    vector_pieces = gather(vectors)
    all_inputs = jnp.concatenate(input_pieces, axis=0)
    vectors = jnp.stack(vector_pieces)[order].transpose(1, 0, 2).reshape(8, model).astype(F32)

    squares = (query_weight, key_weight, value_weight)
    qkv_cols = fetch(cut_columns(squares, me, core, count, wide)).reshape(model, full)
    cot_pieces = gather(cotangent[0])
    all_cot = jnp.concatenate(cot_pieces, axis=0)

    pos = (order[:, None] * length + jnp.arange(length, dtype=jnp.int32)[None, :]).reshape(-1)
    seg = segment[0].reshape(count, length)[order].reshape(-1)
    rows_info = jnp.stack([seg, pos], axis=1)
    cols_info = jnp.stack([seg, pos], axis=0)

    head_slice = lambda v: lax.dynamic_slice_in_dim(v, me * wide, wide)
    tail = lambda v: v[count * wide :]
    qkv_bias = jnp.concatenate(
        [
            head_slice(vectors[0]), jnp.zeros((wide,), F32), head_slice(vectors[1]),
            tail(vectors[0]), jnp.zeros((HD,), F32), tail(vectors[1]),
        ]
    )

    first_gain_full, first_shift_full = vectors[4], vectors[5]
    second_gain_full, second_shift_full = vectors[6], vectors[7]
    all_hat, _ = normalise(all_inputs.astype(F32))
    first_in = (all_hat * first_gain_full + first_shift_full).astype(BF16)
    qkv = (matmul(first_in, qkv_cols) + qkv_bias).astype(BF16)
    out_half = rows_of_core(out_weight, core)
    full_out = fetch([out_weight] + [out_half] * 3, qkv).reshape(model, model)
    head_out = lax.dynamic_slice_in_dim(full_out, me * wide, wide, axis=0)
    last_out = full_out[count * wide :]
    attended, last, logs, *others_rows = split_forward(qkv, rows_info, cols_info, heads, length)
    att_pieces = [attended[0:length]] + [send(others_rows[k - 1], k) for k in others]
    stacked_up = jnp.stack([up_weight[:, j * hidden : (j + 1) * hidden] for j in range(count)])
    up_halves = rows_of_core(stacked_up, core)
    up_cuts = [pick(stacked_up, me)] + [pick(up_halves, slots[k]) for k in others]
    up_cols = fetch(up_cuts, attended).reshape(model, hidden)
    own_attended, middle, second_hat, second_inv, own_second_in = mid_forward(
        att_pieces, last, slots, wide, full_out, inputs[0],
        jnp.stack([vectors[2], second_gain_full, second_shift_full]),
    )
    residual_in = inputs[0].astype(F32)
    second_in = jnp.concatenate(gather(own_second_in), axis=0)
    pre_act = matmul(second_in, up_cols) + up_bias.astype(F32)
    below = 0.5 * (1.0 + lax.erf(pre_act * (0.5**0.5)))
    activated = (pre_act * below).astype(BF16)
    slope = below + pre_act * (jnp.exp(-0.5 * pre_act * pre_act) * 0.3989422804014327)
    grad_pre = contract_last(all_cot, down_weight) * slope
    grad_pre_low = grad_pre.astype(BF16)
    up_bias_part = jnp.sum(grad_pre, axis=0)
    second_rows = contract_last(grad_pre_low, up_cols)
    second_pieces = [
        send(second_rows[k * length : (k + 1) * length].astype(BF16), k) for k in others
    ]

    def reduce_far(part, mode):
        keep = lax.dynamic_slice_in_dim(part, 2 * near, 2, axis=0)
        give = lax.dynamic_slice_in_dim(part, 2 - 2 * near, 2, axis=0)
        pair = added(keep, cross(give, 2))
        one = added(pick(pair, far), cross(pick(pair, 1 - far), 4))
        back = cross(one, 4)
        mine = [one, back, cross(one, 2), cross(back, 2)]
        theirs = [cross(v, 1) for v in mine]
        return unfold(mine, theirs, core, near, far, mode), one

    down_part = contract_rows(activated, all_cot).astype(BF16)
    down_part = down_part.reshape(2, 4, hidden // 8, model)
    down_given = cross(pick(down_part, 1 - core), 1)
    down_half = added(pick(down_part, core), down_given)
    (down_sum,), _ = reduce_far(down_half, "rows")
    down_weight_grad = down_sum.reshape(hidden, model)

    up_part = contract_rows(second_in, grad_pre_low).astype(BF16)
    up_part = up_part.reshape(count, own, hidden)
    up_given = cross(rows_of_core(up_part, 1 - core), 1)
    up_part = added(rows_of_core(up_part, core), up_given)
    up_pieces = [pick(up_part, me)] + [send(pick(up_part, slots[k]), k) for k in others]
    grad_middle, grad_middle_low, mid_sums = mid_backward(
        second_rows, second_pieces, second_hat, second_inv, cotangent[0], second_gain_full
    )
    all_grad_middle, grad_attended, grad_last = att_grads(
        gather(grad_middle_low), head_out, last_out
    )
    grad_qkv, head_sums = split_backward(
        qkv, grad_attended, grad_last, attended, last, logs, rows_info, cols_info, heads
    )
    up_pieces = list(lax.optimization_barrier((*up_pieces, head_sums)))[:-1]
    (up_weight_grad,), up_one = reduce_far(assemble(up_pieces, slots, count), "columns")
    qkv_keep, qkv_give = grad_columns(first_in, grad_qkv, core, count)
    qkv_part = added(qkv_keep, cross(qkv_give, 1))
    late_qkv, _ = lax.optimization_barrier((grad_qkv, qkv_part))
    first_rows = contract_last(late_qkv, qkv_cols)
    first_pieces = [send(first_rows[k * length : (k + 1) * length].astype(BF16), k) for k in others]
    features = jnp.stack([own_attended[:, j * own : (j + 1) * own] for j in range(count)])
    feature_pieces = [send(pick(features, slots[k]), k) for k in others]
    *feature_pieces, _ = lax.optimization_barrier((*feature_pieces, qkv_give))
    own_features = jnp.concatenate([pick(features, me)] + feature_pieces, axis=0)
    out_part = contract_rows(own_features, all_grad_middle).astype(BF16)
    out_part = added(rows_of_core(out_part, core), cross(rows_of_core(out_part, 1 - core), 1))
    qkv_pieces = [pick(qkv_part, me)] + [send(pick(qkv_part, slots[k]), k) for k in others]
    placed = place_grads(out_part, qkv_pieces, slots, wide)
    *first_pieces, _ = lax.optimization_barrier((*first_pieces, placed))
    grad_first = sum((v.astype(F32) for v in first_pieces), first_rows[0:length])
    first_hat, first_inv = normalise(residual_in)
    input_grad = grad_middle + norm_backward(grad_first, first_hat, first_inv, first_gain_full)
    square, _ = reduce_far(placed, "arrays")
    late_activated, _ = lax.optimization_barrier((activated, up_one))
    output_rows = matmul(late_activated, down_weight)
    outputs = (middle + scatter_sum(output_rows) + vectors[3]).astype(BF16)

    def to_full(row):
        main = lax.dynamic_update_slice(
            jnp.zeros((count * wide,), F32), row[:wide], (me * wide,)
        )
        return jnp.concatenate([main, row[wide:]])

    partials = jnp.stack(
        [
            to_full(head_sums[0]),
            to_full(head_sums[1]),
            mid_sums[0],
            mid_sums[1],
            jnp.sum(grad_first * first_hat, axis=0),
            jnp.sum(grad_first, axis=0),
            mid_sums[2],
            mid_sums[3],
        ]
    )
    rows = partials.reshape(8, count, own).transpose(1, 0, 2)
    mine = pick(rows, me)
    for k in others:
        mine = mine + send(pick(rows, slots[k]), k)
    summed = jnp.concatenate([mine, up_bias_part.reshape(count, own)], axis=0)
    for k in (1, 2, 4):
        summed = summed + cross(summed, k)
    return (
        outputs[None],
        input_grad[None],
        square[1],
        square[2],
        square[3],
        square[0],
        up_weight_grad,
        down_weight_grad,
        summed[0],
        summed[1],
        summed[2],
        summed[8:].reshape(hidden),
        summed[3],
        summed[4],
        summed[5],
        summed[6],
        summed[7],
    )


def on_device(count, copies, *args):
    model = args[0].shape[2]
    heads = HEADS // count
    paired = (
        count == 4
        and copies == 8
        and HEADS == count * heads + 1
        and (heads * HD) % LANES == 0
        and model % (count * 16) == 0
        and args[0].shape[1] <= 256
        and args[8].shape[0] == model
    )
    if paired:
        return on_device_paired(count, *args)
    return on_device_general(count, *args)


def solution(mesh):
    tokens = P("dp", "shard", None)
    matrix = P("shard", None)
    vector = P("shard")
    return jax.shard_map(
        partial(on_device, mesh.shape["shard"], mesh.shape["dp"]),
        mesh=mesh,
        in_specs=(tokens, P("dp", None), tokens) + (matrix,) * 6 + (vector,) * 9,
        out_specs=(tokens, tokens) + (matrix,) * 6 + (vector,) * 9,
        check_vma=False,
    )
```

```python
from functools import partial

import jax
import jax.numpy as jnp
from jax import lax
from jax.experimental import pallas as pl
from jax.experimental.pallas import tpu as pltpu
from jax.sharding import PartitionSpec as P


HEADS = 17
HD = 64
EPSILON = 1e-05
SCORE_SCALE = 0.125
MASKED_SCORE = -1e30
LANES = 128
MANY = 4


BF16 = jnp.bfloat16
F32 = jnp.float32


def normalise(values):
    average = jnp.mean(values, axis=-1, keepdims=True)
    centred = values - average
    variance = jnp.mean(centred * centred, axis=-1, keepdims=True)
    inv_std = lax.rsqrt(variance + EPSILON)
    return centred * inv_std, inv_std


def norm_backward(grad_normed, normed, inv_std, gain_vec):
    scaled = grad_normed * gain_vec
    first_mean = jnp.mean(scaled, axis=-1, keepdims=True)
    second_mean = jnp.mean(scaled * normed, axis=-1, keepdims=True)
    return inv_std * (scaled - first_mean - normed * second_mean)


def matmul(left_side, right_side):
    return jnp.dot(left_side, right_side, preferred_element_type=F32)


def contract_rows(left_side, right_side):
    return lax.dot_general(
        left_side, right_side, (((0,), (0,)), ((), ())), preferred_element_type=F32
    )


def contract_last(left_side, right_side):
    return lax.dot_general(
        left_side, right_side, (((1,), (1,)), ((), ())), preferred_element_type=F32
    )


def mask_bias(row_seg, row_pos, col_seg, col_pos):
    allowed = (row_seg == col_seg) & (col_pos <= row_pos)
    return jnp.where(allowed, 0.0, MASKED_SCORE)


def attention_forward(qkv, rows_info, cols_info, heads):
    tokens = qkv.shape[0]
    width = heads * HD
    block = min(256, tokens)

    def kernel(q_ref, kv_ref, rows_ref, cols_ref, out_ref, log_ref):
        bias = mask_bias(
            rows_ref[:, 0:1], rows_ref[:, 1:2], cols_ref[0:1, :], cols_ref[1:2, :]
        )
        lane = lax.broadcasted_iota(jnp.int32, (block, LANES), 1)
        logs = jnp.zeros((block, LANES), F32)
        for h in range(heads):
            query = q_ref[:, h * HD : (h + 1) * HD]
            keys = kv_ref[:, width + h * HD : width + (h + 1) * HD]
            vals = kv_ref[:, 2 * width + h * HD : 2 * width + (h + 1) * HD]
            scores = contract_last(query, keys) * SCORE_SCALE + bias
            largest = jnp.max(scores, axis=1, keepdims=True)
            grown = jnp.exp(scores - largest)
            total = jnp.sum(grown, axis=1, keepdims=True)
            probs = (grown * (1.0 / total)).astype(BF16)
            out_ref[:, h * HD : (h + 1) * HD] = matmul(probs, vals).astype(BF16)
            logs = jnp.where(lane == h, largest + jnp.log(total), logs)
        log_ref[...] = logs

    return pl.pallas_call(
        kernel,
        grid=(tokens // block,),
        in_specs=[
            pl.BlockSpec((block, 3 * width), lambda b: (b, 0)),
            pl.BlockSpec((tokens, 3 * width), lambda b: (0, 0)),
            pl.BlockSpec((block, 2), lambda b: (b, 0)),
            pl.BlockSpec((2, tokens), lambda b: (0, 0)),
        ],
        out_specs=[
            pl.BlockSpec((block, width), lambda b: (b, 0)),
            pl.BlockSpec((block, LANES), lambda b: (b, 0)),
        ],
        out_shape=[
            jax.ShapeDtypeStruct((tokens, width), BF16),
            jax.ShapeDtypeStruct((tokens, LANES), F32),
        ],
        name="attention_forward",
    )(qkv, qkv, rows_info, cols_info)


def attention_backward(qkv, grad_att, attended, logs, rows_info, cols_info, heads):
    tokens = qkv.shape[0]
    width = heads * HD
    block = min(256, tokens)
    steps = tokens // block

    def kernel(
        q_ref, kv_ref, grad_ref, att_ref, log_ref, rows_ref, cols_ref,
        gq_ref, gkv_ref, sums_ref, acc_ref, bias_ref,
    ):
        step = pl.program_id(0)

        @pl.when(step == 0)
        def _():
            acc_ref[...] = jnp.zeros_like(acc_ref)
            bias_ref[...] = jnp.zeros_like(bias_ref)

        bias = mask_bias(
            rows_ref[:, 0:1], rows_ref[:, 1:2], cols_ref[0:1, :], cols_ref[1:2, :]
        )
        for h in range(heads):
            own = slice(h * HD, (h + 1) * HD)
            query = q_ref[:, own]
            keys = kv_ref[:, width + h * HD : width + (h + 1) * HD]
            vals = kv_ref[:, 2 * width + h * HD : 2 * width + (h + 1) * HD]
            grad = grad_ref[:, own]
            delta = jnp.sum(
                grad.astype(F32) * att_ref[:, own].astype(F32), axis=1, keepdims=True
            )
            scores = contract_last(query, keys) * SCORE_SCALE + bias
            exact = jnp.exp(scores - log_ref[:, h : h + 1])
            grad_probs = contract_last(grad, vals)
            grad_scores = (exact * (grad_probs - delta) * SCORE_SCALE).astype(BF16)
            grad_query = matmul(grad_scores, keys)
            gq_ref[:, own] = grad_query.astype(BF16)
            bias_ref[0:1, own] += jnp.sum(grad_query, axis=0, keepdims=True)
            acc_ref[:, own] += contract_rows(grad_scores, query)
            acc_ref[:, width + h * HD : width + (h + 1) * HD] += contract_rows(
                exact.astype(BF16), grad
            )

        @pl.when(step == steps - 1)
        def _():
            gkv_ref[...] = acc_ref[...].astype(BF16)
            bias_ref[1:2, :] = jnp.sum(acc_ref[:, width:], axis=0, keepdims=True)
            sums_ref[...] = bias_ref[...]

    return pl.pallas_call(
        kernel,
        grid=(steps,),
        in_specs=[
            pl.BlockSpec((block, 3 * width), lambda b: (b, 0)),
            pl.BlockSpec((tokens, 3 * width), lambda b: (0, 0)),
            pl.BlockSpec((block, width), lambda b: (b, 0)),
            pl.BlockSpec((block, width), lambda b: (b, 0)),
            pl.BlockSpec((block, LANES), lambda b: (b, 0)),
            pl.BlockSpec((block, 2), lambda b: (b, 0)),
            pl.BlockSpec((2, tokens), lambda b: (0, 0)),
        ],
        out_specs=[
            pl.BlockSpec((block, width), lambda b: (b, 0)),
            pl.BlockSpec((tokens, 2 * width), lambda b: (0, 0)),
            pl.BlockSpec((8, width), lambda b: (0, 0)),
        ],
        out_shape=[
            jax.ShapeDtypeStruct((tokens, width), BF16),
            jax.ShapeDtypeStruct((tokens, 2 * width), BF16),
            jax.ShapeDtypeStruct((8, width), F32),
        ],
        scratch_shapes=[
            pltpu.VMEM((tokens, 2 * width), F32),
            pltpu.VMEM((8, width), F32),
        ],
        name="attention_backward",
    )(qkv, qkv, grad_att, attended, logs, rows_info, cols_info)


def on_device_general(
    count,
    inputs,
    segment,
    cotangent,
    query_weight,
    key_weight,
    value_weight,
    out_weight,
    up_weight,
    down_weight,
    query_bias,
    value_bias,
    out_bias,
    up_bias,
    down_bias,
    first_gain,
    first_shift,
    second_gain,
    second_shift,
):
    me = lax.axis_index("shard")
    others = range(1, count)
    order = me ^ jnp.arange(count, dtype=jnp.int32)
    length = inputs.shape[1]
    model = inputs.shape[2]
    own = query_weight.shape[0]
    hidden = down_weight.shape[0]
    per = -(-HEADS // count)
    width = per * HD
    padded = count * width

    def send(value, k):
        return lax.ppermute(value, "shard", [(j, j ^ k) for j in range(count)])

    def gather(value):
        if count > MANY:
            whole = lax.all_gather(value, "shard")
            return [lax.dynamic_index_in_dim(whole, me ^ k, 0, False) for k in range(count)]
        return [value] + [send(value, k) for k in others]

    def swap(pieces):
        if count > MANY:
            whole = jnp.stack(pieces)[order]
            whole = lax.all_to_all(whole, "shard", split_axis=0, concat_axis=0)[order]
            return [whole[k] for k in range(count)]
        return [pieces[0]] + [send(pieces[k], k) for k in others]

    def scatter_sum(partial_rows):
        blocks = [partial_rows[k * length : (k + 1) * length] for k in range(count)]
        got = swap([b.astype(BF16) for b in blocks])
        return sum((v.astype(F32) for v in got[1:]), blocks[0])

    def in_order(pieces):
        rows = pieces[0].shape[0]
        whole = jnp.zeros((count * rows,) + pieces[0].shape[1:], pieces[0].dtype)
        for k in range(count):
            start = ((me ^ k) * rows,) + (0,) * (pieces[0].ndim - 1)
            whole = lax.dynamic_update_slice(whole, pieces[k], start)
        return whole

    def exchange(stacked):
        return swap(
            [lax.dynamic_index_in_dim(stacked, me ^ k, 0, False) for k in range(count)]
        )

    vectors = jnp.stack(
        [
            query_bias, value_bias, out_bias, down_bias,
            first_gain, first_shift, second_gain, second_shift,
        ]
    )
    vectors = in_order([v[None] for v in gather(vectors)])
    vectors = vectors.transpose(1, 0, 2).reshape(8, model).astype(F32)
    all_inputs = jnp.concatenate(gather(inputs[0]), axis=0)
    pad_cols = lambda w: jnp.pad(w, ((0, 0), (0, padded - model)))
    stacked_qkv = jnp.concatenate(
        [
            pad_cols(w).reshape(own, count, width)
            for w in (query_weight, key_weight, value_weight)
        ],
        axis=2,
    ).transpose(1, 0, 2)
    qkv_cols = in_order(exchange(stacked_qkv))
    all_cot = jnp.concatenate(gather(cotangent[0]), axis=0)
    full_out = jnp.pad(in_order(gather(out_weight)), ((0, padded - model), (0, 0)))
    head_out = lax.dynamic_slice_in_dim(full_out, me * width, width, axis=0)
    mixed_out = full_out.reshape(count, width, model)[order].reshape(padded, model)
    up_cols = in_order(exchange(up_weight.reshape(own, count, hidden).transpose(1, 0, 2)))

    pos = (order[:, None] * length + jnp.arange(length, dtype=jnp.int32)[None, :]).reshape(-1)
    seg = segment[0].reshape(count, length)[order].reshape(-1)
    rows_info = jnp.stack([seg, pos], axis=1)
    cols_info = jnp.stack([seg, pos], axis=0)

    head_slice = lambda v: lax.dynamic_slice_in_dim(
        jnp.pad(v, (0, padded - model)), me * width, width
    )
    qkv_bias = jnp.concatenate(
        [head_slice(vectors[0]), jnp.zeros((width,), F32), head_slice(vectors[1])]
    )

    first_gain_full, first_shift_full = vectors[4], vectors[5]
    second_gain_full, second_shift_full = vectors[6], vectors[7]
    all_hat, _ = normalise(all_inputs.astype(F32))
    first_in = (all_hat * first_gain_full + first_shift_full).astype(BF16)
    qkv = (matmul(first_in, qkv_cols) + qkv_bias).astype(BF16)
    attended, logs = attention_forward(qkv, rows_info, cols_info, per)
    att_pieces = swap([attended[k * length : (k + 1) * length] for k in range(count)])
    residual_in = inputs[0].astype(F32)
    own_attended = jnp.concatenate(att_pieces, axis=1)
    middle = residual_in + matmul(own_attended, mixed_out) + vectors[2]
    second_hat, second_inv = normalise(middle)
    own_second_in = (second_hat * second_gain_full + second_shift_full).astype(BF16)
    second_in = jnp.concatenate(gather(own_second_in), axis=0)
    pre_act = matmul(second_in, up_cols) + up_bias.astype(F32)
    below = 0.5 * (1.0 + lax.erf(pre_act * (0.5**0.5)))
    activated = (pre_act * below).astype(BF16)
    slope = below + pre_act * (jnp.exp(-0.5 * pre_act * pre_act) * 0.3989422804014327)
    grad_pre = contract_last(all_cot, down_weight) * slope
    grad_pre_low = grad_pre.astype(BF16)
    up_bias_part = jnp.sum(grad_pre, axis=0)
    grad_second = scatter_sum(contract_last(grad_pre_low, up_cols))
    outputs = (
        middle + scatter_sum(matmul(activated, down_weight)) + vectors[3]
    ).astype(BF16)

    down_part = contract_rows(activated, all_cot).astype(BF16)
    up_part = contract_rows(second_in, grad_pre_low).astype(BF16)
    up_rows = exchange(up_part.reshape(count, own, hidden))

    def reduce_dp(part, dim):
        share = lax.psum_scatter(part, "dp", scatter_dimension=dim, tiled=True)
        return lax.all_gather(share, "dp", axis=dim, tiled=True).astype(F32)

    down_weight_grad = reduce_dp(down_part, 0)
    up_rows = in_order([v[None] for v in up_rows])
    up_total = reduce_dp(up_rows.reshape(count * own, hidden), 0)
    up_weight_grad = (
        up_total.reshape(count, own, hidden).transpose(1, 0, 2).reshape(own, count * hidden)
    )

    grad_middle = cotangent[0].astype(F32) + norm_backward(
        grad_second, second_hat, second_inv, second_gain_full
    )
    grad_middle_low = grad_middle.astype(BF16)
    all_grad_middle = jnp.concatenate(gather(grad_middle_low), axis=0)
    grad_attended = contract_last(all_grad_middle, head_out).astype(BF16)
    grad_queries, grad_kv, head_sums = attention_backward(
        qkv, grad_attended, attended, logs, rows_info, cols_info, per
    )
    grad_qkv = jnp.concatenate([grad_queries, grad_kv], axis=1)
    grad_first = scatter_sum(contract_last(grad_qkv, qkv_cols))
    first_hat, first_inv = normalise(residual_in)
    input_grad = grad_middle + norm_backward(grad_first, first_hat, first_inv, first_gain_full)

    true_attended = in_order([v[None] for v in att_pieces])
    true_attended = true_attended.transpose(1, 0, 2).reshape(length, padded)[:, :model]
    own_features = jnp.concatenate(
        exchange(true_attended.reshape(length, count, own).transpose(1, 0, 2)), axis=0
    )
    out_part = contract_rows(own_features, all_grad_middle).astype(BF16)
    qkv_part = contract_rows(first_in, grad_qkv).astype(BF16)
    qkv_rows = exchange(qkv_part.reshape(count, own, 3 * width))
    qkv_rows = in_order([v[None] for v in qkv_rows]).reshape(count, own, 3, width)
    qkv_rows = qkv_rows.transpose(2, 1, 0, 3).reshape(3, own, padded)[:, :, :model]
    square = reduce_dp(jnp.concatenate([out_part[None], qkv_rows]).reshape(4 * own, model), 0)
    square = square.reshape(4, own, model)

    to_full = lambda v: lax.dynamic_update_slice(
        jnp.zeros((padded,), F32), v, (me * width,)
    )[:model]
    partials = jnp.stack(
        [
            to_full(head_sums[0]),
            to_full(head_sums[1]),
            jnp.sum(grad_middle, axis=0),
            jnp.sum(cotangent[0].astype(F32), axis=0),
            jnp.sum(grad_first * first_hat, axis=0),
            jnp.sum(grad_first, axis=0),
            jnp.sum(grad_second * second_hat, axis=0),
            jnp.sum(grad_second, axis=0),
        ]
    )
    vector_rows = sum(exchange(partials.reshape(8, count, own).transpose(1, 0, 2)))
    summed, up_bias_grad = lax.psum((vector_rows, up_bias_part), "dp")
    return (
        outputs[None],
        input_grad[None],
        square[1],
        square[2],
        square[3],
        square[0],
        up_weight_grad,
        down_weight_grad,
        summed[0],
        summed[1],
        summed[2],
        up_bias_grad,
        summed[3],
        summed[4],
        summed[5],
        summed[6],
        summed[7],
    )


def call(kernel, out_shape, out_specs, in_specs, scratch=(), grid=()):
    return pl.pallas_call(
        kernel,
        grid=grid,
        in_specs=in_specs,
        out_specs=out_specs,
        out_shape=out_shape,
        scratch_shapes=scratch,
    )


def assemble(pieces, slots, total):
    amount = len(pieces)
    shape = pieces[0].shape[-2:]

    def kernel(slot_ref, *refs):
        out_ref = refs[amount]
        at = 0
        for ref in refs[:amount]:
            parts = [ref[...]] if len(ref.shape) == 2 else [ref[k] for k in range(ref.shape[0])]
            for part in parts:
                out_ref[slot_ref[at]] = part
                at += 1

    return call(
        kernel,
        jax.ShapeDtypeStruct((total,) + shape, pieces[0].dtype),
        pl.BlockSpec(memory_space=pltpu.VMEM),
        [pl.BlockSpec(memory_space=pltpu.SMEM)]
        + [pl.BlockSpec(memory_space=pltpu.VMEM)] * amount,
    )(jnp.stack(slots).astype(jnp.int32), *pieces)


def grad_columns(first_in, grad_qkv, core, count):
    model = first_in.shape[1]
    full = grad_qkv.shape[1]
    own = model // count
    half = own // 2

    def kernel(core_ref, in_ref, grad_ref, keep_ref, give_ref, acc_ref):
        acc_ref[...] = contract_rows(in_ref[...], grad_ref[...])
        for j in range(count):
            for side, ref in enumerate((keep_ref, give_ref)):
                which = core_ref[0] if side == 0 else 1 - core_ref[0]
                start = pl.multiple_of(j * own + which * half, 8)
                ref[j] = acc_ref[pl.ds(start, half), :].astype(BF16)

    return call(
        kernel,
        [jax.ShapeDtypeStruct((count, half, full), BF16)] * 2,
        [pl.BlockSpec(memory_space=pltpu.VMEM)] * 2,
        [pl.BlockSpec(memory_space=pltpu.SMEM)] + [pl.BlockSpec(memory_space=pltpu.VMEM)] * 2,
        [pltpu.VMEM((model, full), F32)],
    )(core[None].astype(jnp.int32), first_in, grad_qkv)


def unfold(mine, theirs, core, near, far, mode):
    blocks = len(mine)
    half, model = mine[0].shape
    shapes = {
        "rows": [(2 * blocks, half, model)],
        "columns": [(2 * half, blocks * model)],
        "arrays": [(2 * half, model)] * blocks,
    }[mode]

    def kernel(bits_ref, *refs):
        out_refs = refs[2 * blocks :]
        mask = bits_ref[1] * 2 + bits_ref[2]
        for side in range(2):
            where = bits_ref[0] if side == 0 else 1 - bits_ref[0]
            rows = pl.ds(pl.multiple_of(where * half, 8), half)
            values = [refs[side * blocks + k][...] for k in range(blocks)]
            for slot in range(blocks):
                if mode == "rows":
                    out_refs[0][where * blocks + (slot ^ mask)] = values[slot].astype(F32)
                    continue
                block = values[slot]
                for k in range(1, blocks):
                    block = jnp.where(mask == k, values[slot ^ k], block)
                if mode == "columns":
                    out_refs[0][rows, slot * model : (slot + 1) * model] = block.astype(F32)
                else:
                    out_refs[slot][rows, :] = block.astype(F32)

    return call(
        kernel,
        [jax.ShapeDtypeStruct(shape, F32) for shape in shapes],
        [pl.BlockSpec(memory_space=pltpu.VMEM)] * len(shapes),
        [pl.BlockSpec(memory_space=pltpu.SMEM)]
        + [pl.BlockSpec(memory_space=pltpu.VMEM)] * (2 * blocks),
    )(jnp.stack([core, near, far]).astype(jnp.int32), *mine, *theirs)


def cut_columns(weights, me, core, count, wide):
    rows, _ = weights[0].shape
    half = rows // 2
    full = 3 * (wide + HD)

    def kernel(place_ref, *refs):
        outs = refs[3:]
        for k in range(count):
            start = pl.multiple_of((place_ref[0] ^ k) * wide, LANES)
            for m in range(3):
                main = refs[m][:, pl.ds(start, wide)]
                extra = refs[m][:, count * wide :]
                if k > 0:
                    main = jnp.where(place_ref[1] == 0, main[:half], main[half:])
                    extra = jnp.where(place_ref[1] == 0, extra[:half], extra[half:])
                outs[k][:, m * wide : (m + 1) * wide] = main
                outs[k][:, 3 * wide + m * HD : 3 * wide + (m + 1) * HD] = extra

    return call(
        kernel,
        [
            jax.ShapeDtypeStruct((rows if k == 0 else half, full), BF16)
            for k in range(count)
        ],
        [pl.BlockSpec(memory_space=pltpu.VMEM)] * count,
        [pl.BlockSpec(memory_space=pltpu.SMEM)] + [pl.BlockSpec(memory_space=pltpu.VMEM)] * 3,
    )(jnp.stack([me, core]).astype(jnp.int32), *weights)


def mid_forward(pieces, last, slots, wide, full_out, residual, rows):
    amount = len(pieces)
    length = pieces[0].shape[0]
    model = full_out.shape[0]

    def kernel(slot_ref, *refs):
        last_ref, weight_ref, res_ref, row_ref = refs[amount : amount + 4]
        att_ref, mid_ref, hat_ref, inv_ref, low_ref = refs[amount + 4 :]
        for k in range(amount):
            start = pl.multiple_of(slot_ref[k] * wide, LANES)
            att_ref[:, pl.ds(start, wide)] = refs[k][...]
        att_ref[:, amount * wide :] = last_ref[...]
        middle = res_ref[...].astype(F32) + matmul(att_ref[...], weight_ref[...]) + row_ref[0:1]
        mid_ref[...] = middle
        hat, inv_std = normalise(middle)
        hat_ref[...] = hat
        inv_ref[...] = jnp.broadcast_to(inv_std, (length, LANES))
        low_ref[...] = (hat * row_ref[1:2] + row_ref[2:3]).astype(BF16)

    shape = lambda width, kind: jax.ShapeDtypeStruct((length, width), kind)
    return call(
        kernel,
        [shape(model, BF16), shape(model, F32), shape(model, F32), shape(LANES, F32),
         shape(model, BF16)],
        [pl.BlockSpec(memory_space=pltpu.VMEM)] * 5,
        [pl.BlockSpec(memory_space=pltpu.SMEM)]
        + [pl.BlockSpec(memory_space=pltpu.VMEM)] * (amount + 4),
    )(jnp.stack(slots).astype(jnp.int32), *pieces, last, full_out, residual, rows)


def mid_backward(whole, pieces, hat, inv_std, cot, gain):
    length, model = hat.shape
    amount = len(pieces)

    def kernel(whole_ref, *refs):
        hat_ref, inv_ref, cot_ref, gain_ref = refs[amount : amount + 4]
        grad_ref, low_ref, sums_ref = refs[amount + 4 :]
        grad = whole_ref[...]
        for ref in refs[:amount]:
            grad = grad + ref[...].astype(F32)
        normed = hat_ref[...]
        cot_float = cot_ref[...].astype(F32)
        grad_mid = cot_float + norm_backward(grad, normed, inv_ref[:, 0:1], gain_ref[...])
        grad_ref[...] = grad_mid
        low_ref[...] = grad_mid.astype(BF16)
        total = lambda v: jnp.sum(v, axis=0, keepdims=True)
        sums_ref[0:1] = total(grad_mid)
        sums_ref[1:2] = total(cot_float)
        sums_ref[2:3] = total(grad * normed)
        sums_ref[3:4] = total(grad)
        sums_ref[4:8] = jnp.zeros((4, model), F32)

    flat = lambda rows, width: pl.BlockSpec((rows, width), lambda b: (0, 0))
    return call(
        kernel,
        [
            jax.ShapeDtypeStruct((length, model), F32),
            jax.ShapeDtypeStruct((length, model), BF16),
            jax.ShapeDtypeStruct((8, model), F32),
        ],
        [flat(length, model), flat(length, model), flat(8, model)],
        [flat(length, model)] * (amount + 2)
        + [flat(length, LANES), flat(length, model), flat(1, model)],
        grid=(1,),
    )(whole, *pieces, hat, inv_std, cot, gain[None])


def place_grads(out_part, pieces, slots, wide):
    amount = len(pieces)
    rows, model = out_part.shape

    def kernel(slot_ref, *refs):
        out_ref = refs[amount + 1]
        out_ref[0] = refs[0][...]
        for m in range(3):
            extra = slice(3 * wide + m * HD, 3 * wide + (m + 1) * HD)
            shared = refs[1][:, extra].astype(F32)
            for k in range(amount):
                start = pl.multiple_of(slot_ref[k] * wide, LANES)
                out_ref[1 + m, :, pl.ds(start, wide)] = refs[1 + k][:, m * wide : (m + 1) * wide]
                if k > 0:
                    shared = shared + refs[1 + k][:, extra].astype(F32)
            out_ref[1 + m, :, amount * wide :] = shared.astype(BF16)

    return call(
        kernel,
        jax.ShapeDtypeStruct((4, rows, model), BF16),
        pl.BlockSpec(memory_space=pltpu.VMEM),
        [pl.BlockSpec(memory_space=pltpu.SMEM)]
        + [pl.BlockSpec(memory_space=pltpu.VMEM)] * (amount + 1),
    )(jnp.stack(slots).astype(jnp.int32), out_part, *pieces)


def split_forward(qkv, rows_info, cols_info, heads, length):
    tokens = qkv.shape[0]
    wide = heads * HD
    block = min(256, tokens)
    full = qkv.shape[1]

    count = tokens // length
    piece = jax.ShapeDtypeStruct((length, wide), BF16)

    def kernel(q_ref, kv_ref, rows_ref, cols_ref, out_ref, last_ref, log_ref, *piece_refs):
        bias = mask_bias(
            rows_ref[:, 0:1], rows_ref[:, 1:2], cols_ref[0:1, :], cols_ref[1:2, :]
        )
        lane = lax.broadcasted_iota(jnp.int32, (block, LANES), 1)

        def head(query, keys, vals, seen):
            scores = contract_last(query, keys) * SCORE_SCALE + seen
            largest = jnp.max(scores, axis=1, keepdims=True)
            grown = jnp.exp(scores - largest)
            total = jnp.sum(grown, axis=1, keepdims=True)
            probs = (grown * (1.0 / total)).astype(BF16)
            return matmul(probs, vals).astype(BF16), largest + jnp.log(total)

        logs = jnp.zeros((block, LANES), F32)
        for h in range(heads):
            own = slice(h * HD, (h + 1) * HD)
            got, log = head(
                q_ref[:, own],
                kv_ref[:, wide + h * HD : wide + (h + 1) * HD],
                kv_ref[:, 2 * wide + h * HD : 2 * wide + (h + 1) * HD],
                bias,
            )
            out_ref[:, own] = got
            logs = jnp.where(lane == h, log, logs)
        log_ref[...] = logs

        @pl.when(pl.program_id(0) == 0)
        def _():
            base = 3 * wide
            got, log = head(
                q_ref[0:length, base : base + HD],
                kv_ref[:, base + HD : base + 2 * HD],
                kv_ref[:, base + 2 * HD : base + 3 * HD],
                bias[0:length],
            )
            last_ref[...] = got
            log_ref[0:length, :] = jnp.where(lane[0:length] == heads, log, logs[0:length])

        for k in range(1, count):
            at = k * length

            @pl.when(pl.program_id(0) == at // block)
            def _():
                piece_refs[k - 1][...] = out_ref[at % block : at % block + length, :]

    return call(
        kernel,
        [
            jax.ShapeDtypeStruct((tokens, wide), BF16),
            jax.ShapeDtypeStruct((length, HD), BF16),
            jax.ShapeDtypeStruct((tokens, LANES), F32),
        ]
        + [piece] * (count - 1),
        [
            pl.BlockSpec((block, wide), lambda b: (b, 0)),
            pl.BlockSpec((length, HD), lambda b: (0, 0)),
            pl.BlockSpec((block, LANES), lambda b: (b, 0)),
        ]
        + [pl.BlockSpec((length, wide), lambda b: (0, 0))] * (count - 1),
        [
            pl.BlockSpec((block, full), lambda b: (b, 0)),
            pl.BlockSpec((tokens, full), lambda b: (0, 0)),
            pl.BlockSpec((block, 2), lambda b: (b, 0)),
            pl.BlockSpec((2, tokens), lambda b: (0, 0)),
        ],
        grid=(tokens // block,),
    )(qkv, qkv, rows_info, cols_info)


def att_grads(pieces, head_out, last_out):
    amount = len(pieces)
    length, model = pieces[0].shape
    wide = head_out.shape[0]

    def kernel(*refs):
        head_ref, last_ref = refs[amount : amount + 2]
        all_ref, grad_ref, glast_ref = refs[amount + 2 :]
        for k in range(amount):
            rows = slice(k * length, (k + 1) * length)
            all_ref[rows, :] = refs[k][...]
        grad_ref[...] = contract_last(all_ref[...], head_ref[...]).astype(BF16)
        glast_ref[...] = contract_last(refs[0][...], last_ref[...]).astype(BF16)

    return call(
        kernel,
        [
            jax.ShapeDtypeStruct((amount * length, model), BF16),
            jax.ShapeDtypeStruct((amount * length, wide), BF16),
            jax.ShapeDtypeStruct((length, HD), BF16),
        ],
        [pl.BlockSpec(memory_space=pltpu.VMEM)] * 3,
        [pl.BlockSpec(memory_space=pltpu.VMEM)] * (amount + 2),
    )(*pieces, head_out, last_out)


def split_backward(qkv, grad_att, grad_last, attended, last, logs, rows_info, cols_info, heads):
    tokens, full = qkv.shape
    length = last.shape[0]
    wide = heads * HD
    block = min(256, tokens)
    steps = tokens // block
    base = 3 * wide

    def kernel(
        q_ref, kv_ref, grad_ref, glast_ref, att_ref, last_ref, log_ref, rows_ref, cols_ref,
        out_ref, sums_ref, acc_ref, bias_ref,
    ):
        step = pl.program_id(0)
        start = pl.multiple_of(step * block, block)

        @pl.when(step == 0)
        def _():
            acc_ref[...] = jnp.zeros_like(acc_ref)
            bias_ref[...] = jnp.zeros_like(bias_ref)
            out_ref[:, base : base + HD] = jnp.zeros((tokens, HD), BF16)

        seen = mask_bias(
            rows_ref[:, 0:1], rows_ref[:, 1:2], cols_ref[0:1, :], cols_ref[1:2, :]
        )

        def head(query, keys, vals, grad, got, log, bias):
            delta = jnp.sum(grad.astype(F32) * got.astype(F32), axis=1, keepdims=True)
            scores = contract_last(query, keys) * SCORE_SCALE + bias
            exact = jnp.exp(scores - log)
            grad_probs = contract_last(grad, vals)
            grad_scores = (exact * (grad_probs - delta) * SCORE_SCALE).astype(BF16)
            return (
                matmul(grad_scores, keys),
                contract_rows(grad_scores, query),
                contract_rows(exact.astype(BF16), grad),
            )

        for h in range(heads):
            own = slice(h * HD, (h + 1) * HD)
            keys_at = slice(wide + h * HD, wide + (h + 1) * HD)
            vals_at = slice(2 * wide + h * HD, 2 * wide + (h + 1) * HD)
            grad_query, grad_key, grad_value = head(
                q_ref[:, own], kv_ref[:, keys_at], kv_ref[:, vals_at],
                grad_ref[:, own], att_ref[:, own], log_ref[:, h : h + 1], seen,
            )
            out_ref[pl.ds(start, block), own] = grad_query.astype(BF16)
            bias_ref[0:1, own] += jnp.sum(grad_query, axis=0, keepdims=True)
            acc_ref[:, own] += grad_key
            acc_ref[:, keys_at] += grad_value

        @pl.when(step == 0)
        def _():
            grad_query, grad_key, grad_value = head(
                q_ref[0:length, base : base + HD],
                kv_ref[:, base + HD : base + 2 * HD],
                kv_ref[:, base + 2 * HD : base + 3 * HD],
                glast_ref[...], last_ref[...], log_ref[0:length, heads : heads + 1],
                seen[0:length],
            )
            out_ref[0:length, base : base + HD] = grad_query.astype(BF16)
            out_ref[:, base + HD : base + 2 * HD] = grad_key.astype(BF16)
            out_ref[:, base + 2 * HD : base + 3 * HD] = grad_value.astype(BF16)
            bias_ref[0:1, wide : wide + HD] = jnp.sum(grad_query, axis=0, keepdims=True)
            bias_ref[1:2, wide : wide + HD] = jnp.sum(grad_value, axis=0, keepdims=True)

        @pl.when(step == steps - 1)
        def _():
            out_ref[:, wide:base] = acc_ref[...].astype(BF16)
            bias_ref[1:2, 0:wide] = jnp.sum(acc_ref[:, wide:], axis=0, keepdims=True)
            sums_ref[...] = bias_ref[...]

    return call(
        kernel,
        [
            jax.ShapeDtypeStruct((tokens, full), BF16),
            jax.ShapeDtypeStruct((8, wide + HD), F32),
        ],
        [
            pl.BlockSpec((tokens, full), lambda b: (0, 0)),
            pl.BlockSpec((8, wide + HD), lambda b: (0, 0)),
        ],
        [
            pl.BlockSpec((block, full), lambda b: (b, 0)),
            pl.BlockSpec((tokens, full), lambda b: (0, 0)),
            pl.BlockSpec((block, wide), lambda b: (b, 0)),
            pl.BlockSpec((length, HD), lambda b: (0, 0)),
            pl.BlockSpec((block, wide), lambda b: (b, 0)),
            pl.BlockSpec((length, HD), lambda b: (0, 0)),
            pl.BlockSpec((block, LANES), lambda b: (b, 0)),
            pl.BlockSpec((block, 2), lambda b: (b, 0)),
            pl.BlockSpec((2, tokens), lambda b: (0, 0)),
        ],
        [pltpu.VMEM((tokens, 2 * wide), F32), pltpu.VMEM((8, wide + HD), F32)],
        grid=(steps,),
    )(qkv, qkv, grad_att, grad_last, attended, last, logs, rows_info, cols_info)


def on_device_paired(
    count,
    inputs,
    segment,
    cotangent,
    query_weight,
    key_weight,
    value_weight,
    out_weight,
    up_weight,
    down_weight,
    query_bias,
    value_bias,
    out_bias,
    up_bias,
    down_bias,
    first_gain,
    first_shift,
    second_gain,
    second_shift,
):
    me = lax.axis_index("shard")
    copy_index = lax.axis_index("dp")
    core = copy_index & 1
    near = (copy_index >> 1) & 1
    far = (copy_index >> 2) & 1
    others = range(1, count)
    order = me ^ jnp.arange(count, dtype=jnp.int32)
    slots = [me ^ k for k in range(count)]
    length = inputs.shape[1]
    model = inputs.shape[2]
    own = query_weight.shape[0]
    half = own // 2
    hidden = down_weight.shape[0]
    heads = HEADS // count
    wide = heads * HD
    full = 3 * (wide + HD)

    def send(value, k):
        return lax.ppermute(value, "shard", [(j, j ^ k) for j in range(count)])

    def cross(value, k):
        return lax.ppermute(value, "dp", [(j, j ^ k) for j in range(8)])

    def gather(value):
        return [value] + [send(value, k) for k in others]

    def pick(value, index):
        return lax.dynamic_index_in_dim(value, index, 0, False)

    def added(left, right):
        return (left.astype(F32) + right.astype(F32)).astype(BF16)

    def scatter_sum(partial_rows):
        total = partial_rows[0:length]
        for k in others:
            piece = partial_rows[k * length : (k + 1) * length].astype(BF16)
            total = total + send(piece, k).astype(F32)
        return total

    def rows_of_core(value, which):
        return lax.dynamic_slice_in_dim(value, which * half, half, axis=value.ndim - 2)

    def fetch(cuts, hold=None):
        got = [send(cuts[k], k) for k in others]
        if hold is not None:
            got = list(lax.optimization_barrier((*got, hold)))[:-1]
        swapped = [cross(g, 1) for g in got]
        pieces, places = [], []
        for k in others:
            pieces += [got[k - 1], swapped[k - 1]]
            places += [2 * slots[k] + core, 2 * slots[k] + 1 - core]
        pieces.append(cuts[0].reshape(2, half, -1))
        places += [2 * me, 2 * me + 1]
        return assemble(pieces, places, 2 * count)

    vectors = jnp.stack(
        [
            query_bias, value_bias, out_bias, down_bias,
            first_gain, first_shift, second_gain, second_shift,
        ]
    )
    input_pieces = gather(inputs[0])
    vector_pieces = gather(vectors)
    all_inputs = jnp.concatenate(input_pieces, axis=0)
    vectors = jnp.stack(vector_pieces)[order].transpose(1, 0, 2).reshape(8, model).astype(F32)

    squares = (query_weight, key_weight, value_weight)
    qkv_cols = fetch(cut_columns(squares, me, core, count, wide)).reshape(model, full)
    cot_pieces = gather(cotangent[0])
    all_cot = jnp.concatenate(cot_pieces, axis=0)

    pos = (order[:, None] * length + jnp.arange(length, dtype=jnp.int32)[None, :]).reshape(-1)
    seg = segment[0].reshape(count, length)[order].reshape(-1)
    rows_info = jnp.stack([seg, pos], axis=1)
    cols_info = jnp.stack([seg, pos], axis=0)

    head_slice = lambda v: lax.dynamic_slice_in_dim(v, me * wide, wide)
    tail = lambda v: v[count * wide :]
    qkv_bias = jnp.concatenate(
        [
            head_slice(vectors[0]), jnp.zeros((wide,), F32), head_slice(vectors[1]),
            tail(vectors[0]), jnp.zeros((HD,), F32), tail(vectors[1]),
        ]
    )

    first_gain_full, first_shift_full = vectors[4], vectors[5]
    second_gain_full, second_shift_full = vectors[6], vectors[7]
    all_hat, _ = normalise(all_inputs.astype(F32))
    first_in = (all_hat * first_gain_full + first_shift_full).astype(BF16)
    qkv = (matmul(first_in, qkv_cols) + qkv_bias).astype(BF16)
    out_half = rows_of_core(out_weight, core)
    full_out = fetch([out_weight] + [out_half] * 3, qkv).reshape(model, model)
    head_out = lax.dynamic_slice_in_dim(full_out, me * wide, wide, axis=0)
    last_out = full_out[count * wide :]
    attended, last, logs, *others_rows = split_forward(qkv, rows_info, cols_info, heads, length)
    att_pieces = [attended[0:length]] + [send(others_rows[k - 1], k) for k in others]
    stacked_up = jnp.stack([up_weight[:, j * hidden : (j + 1) * hidden] for j in range(count)])
    up_halves = rows_of_core(stacked_up, core)
    up_cuts = [pick(stacked_up, me)] + [pick(up_halves, slots[k]) for k in others]
    up_cols = fetch(up_cuts, attended).reshape(model, hidden)
    own_attended, middle, second_hat, second_inv, own_second_in = mid_forward(
        att_pieces, last, slots, wide, full_out, inputs[0],
        jnp.stack([vectors[2], second_gain_full, second_shift_full]),
    )
    residual_in = inputs[0].astype(F32)
    second_in = jnp.concatenate(gather(own_second_in), axis=0)
    pre_act = matmul(second_in, up_cols) + up_bias.astype(F32)
    below = 0.5 * (1.0 + lax.erf(pre_act * (0.5**0.5)))
    activated = (pre_act * below).astype(BF16)
    slope = below + pre_act * (jnp.exp(-0.5 * pre_act * pre_act) * 0.3989422804014327)
    grad_pre = contract_last(all_cot, down_weight) * slope
    grad_pre_low = grad_pre.astype(BF16)
    up_bias_part = jnp.sum(grad_pre, axis=0)
    second_rows = contract_last(grad_pre_low, up_cols)
    second_pieces = [
        send(second_rows[k * length : (k + 1) * length].astype(BF16), k) for k in others
    ]

    def reduce_far(part, mode):
        keep = lax.dynamic_slice_in_dim(part, 2 * near, 2, axis=0)
        give = lax.dynamic_slice_in_dim(part, 2 - 2 * near, 2, axis=0)
        pair = added(keep, cross(give, 2))
        one = added(pick(pair, far), cross(pick(pair, 1 - far), 4))
        back = cross(one, 4)
        mine = [one, back, cross(one, 2), cross(back, 2)]
        theirs = [cross(v, 1) for v in mine]
        return unfold(mine, theirs, core, near, far, mode), one

    down_part = contract_rows(activated, all_cot).astype(BF16)
    down_part = down_part.reshape(2, 4, hidden // 8, model)
    down_given = cross(pick(down_part, 1 - core), 1)
    down_half = added(pick(down_part, core), down_given)
    (down_sum,), _ = reduce_far(down_half, "rows")
    down_weight_grad = down_sum.reshape(hidden, model)

    up_part = contract_rows(second_in, grad_pre_low).astype(BF16)
    up_part = up_part.reshape(count, own, hidden)
    up_given = cross(rows_of_core(up_part, 1 - core), 1)
    up_part = added(rows_of_core(up_part, core), up_given)
    up_pieces = [pick(up_part, me)] + [send(pick(up_part, slots[k]), k) for k in others]
    grad_middle, grad_middle_low, mid_sums = mid_backward(
        second_rows, second_pieces, second_hat, second_inv, cotangent[0], second_gain_full
    )
    all_grad_middle, grad_attended, grad_last = att_grads(
        gather(grad_middle_low), head_out, last_out
    )
    grad_qkv, head_sums = split_backward(
        qkv, grad_attended, grad_last, attended, last, logs, rows_info, cols_info, heads
    )
    up_pieces = list(lax.optimization_barrier((*up_pieces, head_sums)))[:-1]
    (up_weight_grad,), _ = reduce_far(assemble(up_pieces, slots, count), "columns")
    qkv_keep, qkv_give = grad_columns(first_in, grad_qkv, core, count)
    qkv_part = added(qkv_keep, cross(qkv_give, 1))
    late_qkv, _ = lax.optimization_barrier((grad_qkv, qkv_part))
    first_rows = contract_last(late_qkv, qkv_cols)
    first_pieces = [send(first_rows[k * length : (k + 1) * length].astype(BF16), k) for k in others]
    features = jnp.stack([own_attended[:, j * own : (j + 1) * own] for j in range(count)])
    feature_pieces = [send(pick(features, slots[k]), k) for k in others]
    *feature_pieces, _ = lax.optimization_barrier((*feature_pieces, qkv_give))
    own_features = jnp.concatenate([pick(features, me)] + feature_pieces, axis=0)
    out_part = contract_rows(own_features, all_grad_middle).astype(BF16)
    out_part = added(rows_of_core(out_part, core), cross(rows_of_core(out_part, 1 - core), 1))
    qkv_pieces = [pick(qkv_part, me)] + [send(pick(qkv_part, slots[k]), k) for k in others]
    placed = place_grads(out_part, qkv_pieces, slots, wide)
    *first_pieces, _ = lax.optimization_barrier((*first_pieces, placed))
    grad_first = sum((v.astype(F32) for v in first_pieces), first_rows[0:length])
    first_hat, first_inv = normalise(residual_in)
    input_grad = grad_middle + norm_backward(grad_first, first_hat, first_inv, first_gain_full)
    square, _ = reduce_far(placed, "arrays")

    def to_full(row):
        main = lax.dynamic_update_slice(
            jnp.zeros((count * wide,), F32), row[:wide], (me * wide,)
        )
        return jnp.concatenate([main, row[wide:]])

    partials = jnp.stack(
        [
            to_full(head_sums[0]),
            to_full(head_sums[1]),
            mid_sums[0],
            mid_sums[1],
            jnp.sum(grad_first * first_hat, axis=0),
            jnp.sum(grad_first, axis=0),
            mid_sums[2],
            mid_sums[3],
        ]
    )
    rows = partials.reshape(8, count, own).transpose(1, 0, 2)
    mine = pick(rows, me)
    for k in others:
        mine = mine + send(pick(rows, slots[k]), k)
    summed = jnp.concatenate([mine, up_bias_part.reshape(count, own)], axis=0)
    for k in (1, 2, 4):
        given = cross(summed, k)
        summed = summed + given
        if k == 2:
            third = given
    late_activated, _ = lax.optimization_barrier((activated, third))
    output_rows = matmul(late_activated, down_weight)
    outputs = (middle + scatter_sum(output_rows) + vectors[3]).astype(BF16)
    return (
        outputs[None],
        input_grad[None],
        square[1],
        square[2],
        square[3],
        square[0],
        up_weight_grad,
        down_weight_grad,
        summed[0],
        summed[1],
        summed[2],
        summed[8:].reshape(hidden),
        summed[3],
        summed[4],
        summed[5],
        summed[6],
        summed[7],
    )


def on_device(count, copies, *args):
    model = args[0].shape[2]
    heads = HEADS // count
    paired = (
        count == 4
        and copies == 8
        and HEADS == count * heads + 1
        and (heads * HD) % LANES == 0
        and model % (count * 16) == 0
        and args[0].shape[1] <= 256
        and args[8].shape[0] == model
    )
    if paired:
        return on_device_paired(count, *args)
    return on_device_general(count, *args)


def solution(mesh):
    tokens = P("dp", "shard", None)
    matrix = P("shard", None)
    vector = P("shard")
    return jax.shard_map(
        partial(on_device, mesh.shape["shard"], mesh.shape["dp"]),
        mesh=mesh,
        in_specs=(tokens, P("dp", None), tokens) + (matrix,) * 6 + (vector,) * 9,
        out_specs=(tokens, tokens) + (matrix,) * 6 + (vector,) * 9,
        check_vma=False,
    )
```
